32 devices in a mesh: rep: 4 (over y, core), fsdp: 8 (over z, x).
Axes of the slice: x: 2, y: 2, z: 4, core: 2. Of those that a mesh axis runs over, the one named last changes fastest.
Arguments:
- block_input: float32 [4096, 1024], P(('rep', 'fsdp')), may hold values from -6 to 6
- cotangent: float32 [4096, 1024], P(('rep', 'fsdp')), may hold values from -6 to 6
- doc_lengths: int32 [32, 3], P(('rep', 'fsdp')), may hold values from 1 to 64, 128 in all within a row
- gain_mix: float32 [1024], replicated, may hold values from 0.5 to 1.5
- w_query: bfloat16 [1024, 1024], P('fsdp'), may hold values from -0.1875 to 0.1875
- w_key: bfloat16 [1024, 1024], P('fsdp'), may hold values from -0.1875 to 0.1875
- w_value: bfloat16 [1024, 2048], P('fsdp'), may hold values from -0.1875 to 0.1875
- w_gate: bfloat16 [1024, 2048], P('fsdp'), may hold values from -0.1875 to 0.1875
- w_decay: bfloat16 [1024, 8], P('fsdp'), may hold values from -0.1875 to 0.1875
- w_write: bfloat16 [1024, 8], P('fsdp'), may hold values from -0.1875 to 0.1875
- conv_query: float32 [4, 1024], replicated, may hold values from -3 to 3
- conv_key: float32 [4, 1024], replicated, may hold values from -3 to 3
- conv_value: float32 [4, 2048], replicated, may hold values from -3 to 3
- decay_log: float32 [8], replicated, may hold values from -2.5 to -0.5
- decay_bias: float32 [8], replicated, may hold values from -1 to 1
- out_gain: float32 [256], replicated, may hold values from 0.5 to 1.5
- w_out: bfloat16 [2048, 1024], P('fsdp'), may hold values from -0.125 to 0.125
- gain_ffn: float32 [1024], replicated, may hold values from 0.5 to 1.5
- w_hidden: bfloat16 [1024, 2816], P('fsdp'), may hold values from -0.1875 to 0.1875
- w_up: bfloat16 [1024, 2816], P('fsdp'), may hold values from -0.1875 to 0.1875
- w_down: bfloat16 [2816, 1024], P('fsdp'), may hold values from -0.109375 to 0.109375
Outputs:
- block_out: float32 [4096, 1024], P(('rep', 'fsdp'))
- input_grad: float32 [4096, 1024], P(('rep', 'fsdp'))
- grad_gain_mix: float32 [1024], replicated
- grad_w_query: float32 [1024, 1024], P('fsdp')
- grad_w_key: float32 [1024, 1024], P('fsdp')
- grad_w_value: float32 [1024, 2048], P('fsdp')
- grad_w_gate: float32 [1024, 2048], P('fsdp')
- grad_w_decay: float32 [1024, 8], P('fsdp')
- grad_w_write: float32 [1024, 8], P('fsdp')
- grad_conv_query: float32 [4, 1024], replicated
- grad_conv_key: float32 [4, 1024], replicated
- grad_conv_value: float32 [4, 2048], replicated
- grad_decay_log: float32 [8], replicated
- grad_decay_bias: float32 [8], replicated
- grad_out_gain: float32 [256], replicated
- grad_w_out: float32 [2048, 1024], P('fsdp')
- grad_gain_ffn: float32 [1024], replicated
- grad_w_hidden: float32 [1024, 2816], P('fsdp')
- grad_w_up: float32 [1024, 2816], P('fsdp')
- grad_w_down: float32 [2816, 1024], P('fsdp')
The draws below stay inside these ranges and needn't reach their ends.
Inputs may be any that keep to these rules, and one draw needn't show every extreme that they name: `doc_lengths`: each row holds the lengths of the 3 documents packed in order into one device's 128 tokens and sums to 128; the longest in each row has 64 tokens.
All inputs are finite; a program needn't handle non-finite values.
Results may differ from the reference program's by a relative error of at most 0.013.
Values may be sent and summed in bfloat16 or wider, within the bound.
A program may use at most 192 MiB of HBM per device.

```python
import math
from functools import partial
import jax
import jax.numpy as jnp
import numpy as np
from jax import lax

D = 1024
HEADS = 8
DV = 256
FF = 2816
CONV = 4
BLOCK = 64
TOK_DEV = 128
DOCS_DEV = 3
DOC_MOST = 64
KEYS = 1024
VALS = 2048
TOKENS = 4096
N_REP = 4
N_FSDP = 8


def levels(rng, extent, split, smallest, top_value):
    def one(position, parts):
        steps = jax.random.uniform(jax.random.fold_in(jax.random.fold_in(rng, 6), position), (parts,), jnp.float32, smallest / len(split), top_value / len(split))
        return jnp.repeat(jnp.exp(steps), extent[position] // parts).reshape((-1,) + (1,) * (len(extent) - position - 1))

    loudness = one(*split[0])
    for cut in split[1:]:
        loudness = loudness * one(*cut)
    return loudness


def length_profile(number_of, total, limit, skew):
    loads = [(1 << 20) // math.isqrt(standing ** skew) + 1 for standing in range(2, number_of + 1)]
    surplus, holding = total - limit - (number_of - 1), [1] * (number_of - 1)
    while surplus > 0:
        candidates = [i for i in range(number_of - 1) if holding[i] < limit]
        mass, left = sum([loads[i] for i in candidates]), surplus
        for i in candidates:
            more = min(limit - holding[i], max(1, left * loads[i] // mass), surplus)
            holding[i] = holding[i] + more
            surplus = surplus - more
    return np.array([limit] + holding)


def uneven(own_key, amount, total, bound, skew):
    if amount == 2:
        one = jax.random.randint(own_key, (), max(1, total - bound), min(bound, total - 1) + 1)
        return jnp.stack([one, total - one])
    sizes = jnp.asarray(length_profile(amount, total, bound, skew), jnp.int32)
    twos = (amount - 1) // 2
    donor, taker = sizes[1:1 + 2 * twos:2], sizes[2:2 + 2 * twos:2]
    margin = jnp.minimum(donor - 1, bound - taker)
    moved = jax.random.randint(jax.random.fold_in(own_key, 1), (twos,), 0, 1 << 20) % (margin + 1)
    sizes = sizes.at[1:1 + 2 * twos:2].set(donor - moved).at[2:2 + 2 * twos:2].set(taker + moved)
    return sizes[jax.random.permutation(jax.random.fold_in(own_key, 2), amount)]


def normal_values(key, extent, scale, limit, pieces=(), held_as=jnp.bfloat16):
    values = jax.random.normal(key, extent, jnp.float32) * scale
    if len(pieces) > 0:
        values = levels(key, extent, pieces, -0.22, 0.18) * values
    return jnp.clip(values, min=-limit, max=limit).astype(held_as)


def setup_inputs(seed: int = 0) -> dict:
    arg_keys = jax.random.split(jax.random.key(seed), 22)
    block_input = normal_values(arg_keys[0], (TOKENS, D), 1.0, 6.0, ((0, 32),), jnp.float32)
    cotangent = normal_values(arg_keys[1], (TOKENS, D), 1.0, 6.0, ((0, 32),), jnp.float32)
    doc_lengths = jax.vmap(lambda own: uneven(own, DOCS_DEV, TOK_DEV, DOC_MOST, 1))(jax.random.split(arg_keys[2], (N_REP * N_FSDP))).reshape((N_REP * N_FSDP, DOCS_DEV)).astype(jnp.int32)
    gain_mix = jnp.clip(1.0 + 0.1 * jax.random.normal(arg_keys[3], (D,), jnp.float32), 0.5, 1.5)
    w_query = normal_values(arg_keys[4], (D, KEYS), D ** -0.5, 0.1875, ((0, 8),))
    w_key = normal_values(arg_keys[5], (D, KEYS), D ** -0.5, 0.1875, ((0, 8),))
    w_value = normal_values(arg_keys[6], (D, VALS), D ** -0.5, 0.1875, ((0, 8),))
    w_gate = normal_values(arg_keys[7], (D, VALS), D ** -0.5, 0.1875, ((0, 8),))
    w_decay = normal_values(arg_keys[8], (D, HEADS), D ** -0.5, 0.1875, ((0, 8),))
    w_write = normal_values(arg_keys[9], (D, HEADS), D ** -0.5, 0.1875, ((0, 8),))
    conv_query = normal_values(arg_keys[10], (CONV, KEYS), 0.5, 3.0, (), jnp.float32)
    conv_key = normal_values(arg_keys[11], (CONV, KEYS), 0.5, 3.0, (), jnp.float32)
    conv_value = normal_values(arg_keys[12], (CONV, VALS), 0.5, 3.0, (), jnp.float32)
    decay_log = jnp.clip(jax.random.uniform(arg_keys[13], (HEADS,), jnp.float32, -2.5, -0.5), -2.5, -0.5)
    decay_bias = jnp.clip(jax.random.uniform(arg_keys[14], (HEADS,), jnp.float32, -1.0, 1.0), -1.0, 1.0)
    out_gain = jnp.clip(1.0 + 0.1 * jax.random.normal(arg_keys[15], (DV,), jnp.float32), 0.5, 1.5)
    w_out = normal_values(arg_keys[16], (VALS, D), VALS ** -0.5, 0.125, ((0, 8),))
    gain_ffn = jnp.clip(1.0 + 0.1 * jax.random.normal(arg_keys[17], (D,), jnp.float32), 0.5, 1.5)
    w_hidden = normal_values(arg_keys[18], (D, FF), D ** -0.5, 0.1875, ((0, 8),))
    w_up = normal_values(arg_keys[19], (D, FF), D ** -0.5, 0.1875, ((0, 8),))
    w_down = normal_values(arg_keys[20], (FF, D), FF ** -0.5, 0.109375, ((0, 8),))
    return {"block_input": block_input, "cotangent": cotangent, "doc_lengths": doc_lengths, "gain_mix": gain_mix, "w_query": w_query, "w_key": w_key, "w_value": w_value, "w_gate": w_gate, "w_decay": w_decay, "w_write": w_write, "conv_query": conv_query, "conv_key": conv_key, "conv_value": conv_value, "decay_log": decay_log, "decay_bias": decay_bias, "out_gain": out_gain, "w_out": w_out, "gain_ffn": gain_ffn, "w_hidden": w_hidden, "w_up": w_up, "w_down": w_down}


EPSILON = 1e-06
TOP_PRECISION = lax.Precision.HIGHEST

def product(left, right):
    return jnp.dot(left.astype(jnp.float32), right.astype(jnp.float32), preferred_element_type=jnp.float32)

def product_left(left, right):
    return lax.dot_general(left.astype(jnp.float32), right.astype(jnp.float32), (((0,), (0,)), ((), ())), preferred_element_type=jnp.float32)

def product_right(left, right):
    return lax.dot_general(left.astype(jnp.float32), right.astype(jnp.float32), (((1,), (1,)), ((), ())), preferred_element_type=jnp.float32)

def rms_norm(values, gain):
    return values * lax.rsqrt(lax.optimization_barrier(jnp.mean(values * values, axis=-1, keepdims=True)) + EPSILON) * gain

def swiglu(hidden_pre, up_pre):
    return jax.nn.silu(hidden_pre) * up_pre

def doc_segments(lengths, tokens):
    doc_ends = jnp.cumsum(lengths).astype(jnp.int32)
    positions = jnp.arange(tokens, dtype=jnp.int32)
    return lax.optimization_barrier(jnp.sum((positions[:, None] >= doc_ends[None, :]).astype(jnp.int32), axis=1)).astype(jnp.int32)

def shifted(values, offset, fill):
    filler = jnp.full((offset,) + values.shape[1:], fill, values.dtype)
    return jnp.concatenate([filler, values[:-offset]], axis=0)

def short_conv(values, kernel, segment):
    summed = values * kernel[0]
    for offset in range(1, kernel.shape[0]):
        same_doc = (shifted(segment, offset, -1) == segment).astype(values.dtype)
        summed = summed + shifted(values, offset, 0.0) * kernel[offset] * same_doc[:, None]
    return summed

def delta_block(memory_state, inputs):
    query_rows, key_matrix, value_rows, decays, strength, segment, before = inputs
    width = segment.shape[0]
    positions = jnp.arange(width, dtype=jnp.int32)
    same_doc = segment[:, None] == segment[None, :]
    lower_mask = same_doc & (positions[:, None] >= positions[None, :])
    strict_mask = same_doc & (positions[:, None] > positions[None, :])
    cumulative = jnp.cumsum(decays, axis=1)
    spread = jnp.minimum(cumulative[:, :, None] - cumulative[:, None, :], 0.0)
    ratios = jnp.where(lower_mask[None], jnp.exp(spread), 0.0)
    carried = (segment == before).astype(decays.dtype)
    reaching_terms = jnp.exp(cumulative) * carried[None, :]
    key_inner = jnp.einsum('hid,hjd->hij', key_matrix, key_matrix, precision=TOP_PRECISION)
    lower_part = jnp.where(strict_mask[None], strength[:, :, None] * ratios * key_inner, 0.0)
    sources = jnp.concatenate([strength[:, :, None] * value_rows, (strength * reaching_terms)[:, :, None] * key_matrix], axis=2)
    solved = jax.scipy.linalg.solve_triangular(lower_part, sources, lower=True, unit_diagonal=True)
    value_dim = value_rows.shape[2]
    update_rows = solved[:, :, :value_dim]
    removal_terms = solved[:, :, value_dim:]
    delta_rows = update_rows - jnp.einsum('uws,usb->uwb', removal_terms, memory_state, precision=TOP_PRECISION)
    scores = jnp.einsum('hid,hjd->hij', query_rows, key_matrix, precision=TOP_PRECISION) * ratios
    readout_rows = reaching_terms[:, :, None] * jnp.einsum('uws,usb->uwb', query_rows, memory_state, precision=TOP_PRECISION)
    readout_rows = readout_rows + jnp.einsum('hij,hjv->hiv', scores, delta_rows, precision=TOP_PRECISION)
    tail_fraction = ratios[:, -1, :]
    memory_state = reaching_terms[:, -1][:, None, None] * memory_state + jnp.einsum('fsz,fsb->fzb', key_matrix * tail_fraction[:, :, None], delta_rows, precision=TOP_PRECISION)
    return (memory_state, readout_rows)

def delta_mixer(query_proj, key_proj, value_proj, gate_proj, decay_proj, write_proj, conv_query, conv_key, conv_value, decay_log, decay_bias, out_gain, segment):
    tokens = query_proj.shape[0]
    head_count = decay_log.shape[0]
    key_dim = query_proj.shape[1] // head_count
    value_dim = value_proj.shape[1] // head_count
    block_count = tokens // BLOCK
    query_rows = jax.nn.silu(short_conv(query_proj, conv_query, segment)).reshape(tokens, head_count, key_dim)
    key_matrix = jax.nn.silu(short_conv(key_proj, conv_key, segment)).reshape(tokens, head_count, key_dim)
    value_rows = jax.nn.silu(short_conv(value_proj, conv_value, segment)).reshape(tokens, head_count, value_dim)
    query_rows = query_rows * lax.rsqrt(lax.optimization_barrier(jnp.sum(query_rows * query_rows, axis=2, keepdims=True)) + EPSILON) * key_dim ** (-0.5)
    key_matrix = key_matrix * lax.rsqrt(lax.optimization_barrier(jnp.sum(key_matrix * key_matrix, axis=2, keepdims=True)) + EPSILON)
    decays = -jnp.exp(decay_log) * jax.nn.softplus(decay_proj + decay_bias)
    strength = jax.nn.sigmoid(write_proj)

    def heads_first(array):
        return jnp.swapaxes(array.reshape((block_count, BLOCK) + array.shape[1:]), 1, 2)
    seg_blocks = segment.reshape(block_count, BLOCK)
    before = jnp.concatenate([jnp.full((1,), -1, jnp.int32), seg_blocks[:-1, -1].astype(jnp.int32)], axis=0)
    initial = jnp.zeros((head_count, key_dim, value_dim), query_proj.dtype)
    final_memory, outputs = lax.scan(delta_block, initial, (heads_first(query_rows), heads_first(key_matrix), heads_first(value_rows), heads_first(decays), heads_first(strength), seg_blocks, before))
    readout_rows = jnp.swapaxes(outputs, 1, 2).reshape(tokens, head_count, value_dim)
    readout_rows = readout_rows * lax.rsqrt(lax.optimization_barrier(jnp.mean(readout_rows * readout_rows, axis=2, keepdims=True)) + EPSILON) * out_gain
    readout_rows = readout_rows * jax.nn.silu(gate_proj.reshape(tokens, head_count, value_dim))
    return readout_rows.reshape(tokens, head_count * value_dim)

def reference(block_input, cotangent, doc_lengths, gain_mix, w_query, w_key, w_value, w_gate, w_decay, w_write, conv_query, conv_key, conv_value, decay_log, decay_bias, out_gain, w_out, gain_ffn, w_hidden, w_up, w_down):
    devices = N_REP * N_FSDP
    per_round = math.gcd(32, devices)
    rounds = devices // per_round
    round_rows = per_round * TOK_DEV
    mixing = (w_query, w_key, w_value, w_gate, w_decay, w_write)
    small_params = (conv_query, conv_key, conv_value, decay_log, decay_bias, out_gain)
    params = (gain_mix, w_query, w_key, w_value, w_gate, w_decay, w_write, conv_query, conv_key, conv_value, decay_log, decay_bias, out_gain, w_out, gain_ffn, w_hidden, w_up, w_down)
    batched_mixer = jax.vmap(delta_mixer, in_axes=(0, 0, 0, 0, 0, 0, None, None, None, None, None, None, 0))

    def one_round(totals, inputs):
        rows_in, rows_cot, rows_len = inputs
        segments = jax.vmap(partial(doc_segments, tokens=TOK_DEV))(rows_len)
        normed, norm_back = jax.vjp(rms_norm, rows_in, gain_mix)
        first_input = normed.astype(jnp.bfloat16)
        projections = tuple((product(first_input, weight) for weight in mixing))

        def mix_all(*operands):
            per_device = [item.reshape(per_round, TOK_DEV, item.shape[1]) for item in operands[:6]]
            mixed_rows = batched_mixer(*per_device, *operands[6:], segments)
            return mixed_rows.reshape(round_rows, mixed_rows.shape[2])
        mixed_out, mix_back = jax.vjp(mix_all, *projections, *small_params)
        gated_out = mixed_out.astype(jnp.bfloat16)
        residual = rows_in + product(gated_out, w_out)
        normed_ffn, norm_ffn_back = jax.vjp(rms_norm, residual, gain_ffn)
        second = normed_ffn.astype(jnp.bfloat16)
        swiglu_out, swiglu_back = jax.vjp(swiglu, product(second, w_hidden), product(second, w_up))
        activation = swiglu_out.astype(jnp.bfloat16)
        block_rows = residual + product(activation, w_down)
        upstream = rows_cot.astype(jnp.bfloat16)
        grad_down = product_left(activation, upstream)
        d_hidden, d_up = swiglu_back(product_right(upstream, w_down))
        d_hidden = d_hidden.astype(jnp.bfloat16)
        d_up = d_up.astype(jnp.bfloat16)
        grad_hidden = product_left(second, d_hidden)
        grad_up = product_left(second, d_up)
        d_second = product_right(d_hidden, w_hidden) + product_right(d_up, w_up)
        d_norm_ffn, grad_gain_ffn = norm_ffn_back(d_second)
        d_residual = rows_cot + d_norm_ffn
        upstream_mix = d_residual.astype(jnp.bfloat16)
        grad_out = product_left(gated_out, upstream_mix)
        mix_grads = mix_back(product_right(upstream_mix, w_out))
        d_first = jnp.zeros(rows_in.shape, jnp.float32)
        grads_in = []
        for index in range(6):
            d_proj = mix_grads[index].astype(jnp.bfloat16)
            grads_in.append(product_left(first_input, d_proj))
            d_first = d_first + product_right(d_proj, mixing[index])
        d_norm, grad_gain_mix = norm_back(d_first)
        input_rows = d_residual + d_norm
        new_grads = (grad_gain_mix, *grads_in, *mix_grads[6:], grad_out, grad_gain_ffn, grad_hidden, grad_up, grad_down)
        totals = tuple((old + new for old, new in zip(totals, new_grads)))
        return (totals, (block_rows, input_rows))
    initial = tuple((jnp.zeros(param.shape, jnp.float32) for param in params))
    inputs = (block_input.reshape(rounds, round_rows, D), cotangent.reshape(rounds, round_rows, D), doc_lengths.reshape(rounds, per_round, DOCS_DEV))
    totals, results = lax.scan(one_round, initial, inputs)
    block_out = results[0].reshape(rounds * round_rows, D)
    input_grad = results[1].reshape(rounds * round_rows, D)
    return (block_out, input_grad, totals[0], totals[1], totals[2], totals[3], totals[4], totals[5], totals[6], totals[7], totals[8], totals[9], totals[10], totals[11], totals[12], totals[13], totals[14], totals[15], totals[16], totals[17])
```

```python
import jax
import jax.numpy as jnp
from jax import lax
from jax.sharding import PartitionSpec as P

EPSILON = 1e-06
TOP_PRECISION = lax.Precision.HIGHEST
MIX_PRECISION = lax.Precision.HIGH


def product(left, right):
    return jnp.dot(left, right, preferred_element_type=jnp.float32)


def product_left(left, right):
    return lax.dot_general(
        left, right, (((0,), (0,)), ((), ())), preferred_element_type=jnp.float32
    )


def product_right(left, right):
    return lax.dot_general(
        left, right, (((1,), (1,)), ((), ())), preferred_element_type=jnp.float32
    )


def rms_norm(values, gain):
    return values * lax.rsqrt(jnp.mean(values * values, axis=-1, keepdims=True) + EPSILON) * gain


def swiglu(hidden_pre, up_pre):
    return jax.nn.silu(hidden_pre) * up_pre


def doc_segments(lengths, tokens):
    order = jnp.arange(lengths.shape[0], dtype=jnp.int32)
    upto = order[None, :] <= order[:, None]
    doc_ends = jnp.sum(jnp.where(upto, lengths[None, :], 0), axis=1)
    positions = jnp.arange(tokens, dtype=jnp.int32)
    return jnp.sum((positions[:, None] >= doc_ends[None, :]).astype(jnp.int32), axis=1)


def shifted(values, offset, fill):
    filler = jnp.full((offset,) + values.shape[1:], fill, values.dtype)
    return jnp.concatenate([filler, values[:-offset]], axis=0)


def short_conv(values, kernel, segment):
    summed = values * kernel[0]
    for offset in range(1, kernel.shape[0]):
        same_doc = (shifted(segment, offset, -1) == segment).astype(values.dtype)
        summed = summed + shifted(values, offset, 0.0) * kernel[offset] * same_doc[:, None]
    return summed


def unit_inverse(lower_part):
    width = lower_part.shape[-1]
    index = jnp.arange(width, dtype=jnp.int32)
    inverse = None
    size = 1
    while size < width:
        rows, columns = index[:, None] // size, index[None, :] // size
        pairs = (rows % 2 == 1) & (columns == rows - 1)
        level = jnp.where(pairs[None], lower_part, 0.0)
        if inverse is None:
            inverse = jnp.eye(width, dtype=lower_part.dtype)[None] - level
        else:
            step = jnp.einsum("hij,hjk->hik", level, inverse, precision=MIX_PRECISION)
            inverse = inverse - jnp.einsum("hij,hjk->hik", inverse, step, precision=MIX_PRECISION)
        size = 2 * size
    return inverse


@jax.custom_vjp
def unit_solve(lower_part, sources):
    return jnp.einsum("hij,hjv->hiv", unit_inverse(lower_part), sources, precision=MIX_PRECISION)


def unit_solve_fwd(lower_part, sources):
    inverse = unit_inverse(lower_part)
    solved = jnp.einsum("hij,hjv->hiv", inverse, sources, precision=MIX_PRECISION)
    return solved, (inverse, solved)


def unit_solve_bwd(saved, d_solved):
    inverse, solved = saved
    d_sources = jnp.einsum("hji,hjv->hiv", inverse, d_solved, precision=MIX_PRECISION)
    d_lower = -jnp.einsum("hiv,hjv->hij", d_sources, solved, precision=MIX_PRECISION)
    return d_lower, d_sources


unit_solve.defvjp(unit_solve_fwd, unit_solve_bwd)


def delta_rule(query_rows, key_matrix, value_rows, decays, strength, segment):
    width = segment.shape[0]
    positions = jnp.arange(width, dtype=jnp.int32)
    same_doc = segment[:, None] == segment[None, :]
    lower_mask = same_doc & (positions[:, None] >= positions[None, :])
    strict_mask = same_doc & (positions[:, None] > positions[None, :])
    cumulative = jnp.einsum(
        "ij,hj->hi", lower_mask.astype(decays.dtype), decays, precision=TOP_PRECISION
    )
    spread = jnp.minimum(cumulative[:, :, None] - cumulative[:, None, :], 0.0)
    ratios = jnp.where(lower_mask[None], jnp.exp(spread), 0.0)
    key_inner = jnp.einsum("hid,hjd->hij", key_matrix, key_matrix, precision=MIX_PRECISION)
    lower_part = jnp.where(strict_mask[None], strength[:, :, None] * ratios * key_inner, 0.0)
    delta_rows = unit_solve(lower_part, strength[:, :, None] * value_rows)
    scores = jnp.einsum("hid,hjd->hij", query_rows, key_matrix, precision=MIX_PRECISION) * ratios
    return jnp.einsum("hij,hjv->hiv", scores, delta_rows, precision=MIX_PRECISION)


def delta_mixer(
    query_proj,
    key_proj,
    value_proj,
    gate_proj,
    decay_proj,
    write_proj,
    conv_query,
    conv_key,
    conv_value,
    decay_log,
    decay_bias,
    out_gain,
    segment,
):
    tokens = query_proj.shape[0]
    head_count = decay_log.shape[0]
    key_dim = query_proj.shape[1] // head_count
    value_dim = value_proj.shape[1] // head_count
    query_rows = jax.nn.silu(short_conv(query_proj, conv_query, segment)).reshape(
        tokens, head_count, key_dim
    )
    key_matrix = jax.nn.silu(short_conv(key_proj, conv_key, segment)).reshape(
        tokens, head_count, key_dim
    )
    value_rows = jax.nn.silu(short_conv(value_proj, conv_value, segment)).reshape(
        tokens, head_count, value_dim
    )
    query_rows = (
        query_rows
        * lax.rsqrt(jnp.sum(query_rows * query_rows, axis=2, keepdims=True) + EPSILON)
        * key_dim ** (-0.5)
    )
    key_matrix = key_matrix * lax.rsqrt(
        jnp.sum(key_matrix * key_matrix, axis=2, keepdims=True) + EPSILON
    )
    decays = -jnp.exp(decay_log) * jax.nn.softplus(decay_proj + decay_bias)
    strength = jax.nn.sigmoid(write_proj)

    readout_rows = delta_rule(
        jnp.swapaxes(query_rows, 0, 1),
        jnp.swapaxes(key_matrix, 0, 1),
        jnp.swapaxes(value_rows, 0, 1),
        decays.T,
        strength.T,
        segment,
    )
    readout_rows = jnp.swapaxes(readout_rows, 0, 1)
    readout_rows = (
        readout_rows
        * lax.rsqrt(jnp.mean(readout_rows * readout_rows, axis=2, keepdims=True) + EPSILON)
        * out_gain
    )
    readout_rows = readout_rows * jax.nn.silu(gate_proj.reshape(tokens, head_count, value_dim))
    return readout_rows.reshape(tokens, head_count * value_dim)


def swapped(array, axis_size, bit):
    return lax.ppermute(array, "rep", [(rank, rank ^ bit) for rank in range(axis_size)])


def paired(axis_size):
    return axis_size > 1 and axis_size & (axis_size - 1) == 0


def gathered_halves(weight):
    reps = lax.axis_size("rep")
    if not paired(reps):
        return (lax.all_gather(weight, "fsdp", axis=0, tiled=True),)
    half = weight.shape[0] // 2
    parity = lax.axis_index("rep") % 2
    own = lax.dynamic_slice_in_dim(weight, parity * half, half, axis=0)
    own = lax.all_gather(own, "fsdp", axis=0, tiled=True)
    return (own, swapped(own, reps, 1))


def feature_halves(rows):
    if not paired(lax.axis_size("rep")):
        return (rows,)
    group = lax.axis_size("fsdp")
    tokens, features = rows.shape
    split = rows.reshape(tokens, group, 2, features // (2 * group))
    first = split[:, :, 0].reshape(tokens, features // 2)
    second = split[:, :, 1].reshape(tokens, features // 2)
    even = lax.axis_index("rep") % 2 == 0
    return (jnp.where(even, first, second), jnp.where(even, second, first))


def joined_halves(parts):
    if len(parts) == 1:
        return parts[0]
    group = lax.axis_size("fsdp")
    own, other = parts
    tokens, features = own.shape
    even = lax.axis_index("rep") % 2 == 0
    pair = (jnp.where(even, own, other), jnp.where(even, other, own))
    split = [part.reshape(tokens, group, features // group) for part in pair]
    return jnp.stack(split, axis=2).reshape(tokens, 2 * features)


def times(rows, halves):
    parts = [product(left, right) for left, right in zip(feature_halves(rows), halves)]
    return parts[0] if len(parts) == 1 else parts[0] + parts[1]


def times_back(rows, halves):
    return joined_halves([product_right(rows, half) for half in halves])


def rounded(values):
    return lax.reduce_precision(values, 8, 7).astype(jnp.bfloat16)


def rep_sum(total):
    reps = lax.axis_size("rep")
    if not paired(reps):
        return lax.psum(total.astype(jnp.bfloat16), "rep").astype(jnp.float32)
    half = total.shape[0] // 2
    parity = lax.axis_index("rep") % 2
    sent = lax.dynamic_slice_in_dim(total, (1 - parity) * half, half, axis=0)
    kept = lax.dynamic_slice_in_dim(total, parity * half, half, axis=0)
    own = rounded(kept + swapped(rounded(sent), reps, 1).astype(jnp.float32))
    bit = 2
    while bit < reps:
        own = rounded(own.astype(jnp.float32) + swapped(own, reps, bit).astype(jnp.float32))
        bit = 2 * bit
    other = swapped(own, reps, 1)
    first = jnp.where(parity == 0, own, other)
    second = jnp.where(parity == 0, other, own)
    return jnp.concatenate([first, second], axis=0).astype(jnp.float32)


def total_sum(values):
    for name in ("rep", "fsdp"):
        size = lax.axis_size(name)
        if size & (size - 1):
            values = lax.psum(values, name)
            continue
        bit = 1
        while bit < size:
            pairs = [(rank, rank ^ bit) for rank in range(size)]
            values = values + lax.ppermute(values, name, pairs)
            bit = 2 * bit
    return values


def group_tokens(rows):
    return lax.all_gather(rows, "fsdp", axis=0, tiled=True)


def owned_features(rows):
    return lax.all_to_all(rows, "fsdp", split_axis=1, concat_axis=0, tiled=True)


def column_parts(array, widths):
    parts, start = [], 0
    for width in widths:
        parts.append(array[:, start : start + width])
        start = start + width
    return parts


def local(
    block_input,
    cotangent,
    doc_lengths,
    gain_mix,
    w_query,
    w_key,
    w_value,
    w_gate,
    w_decay,
    w_write,
    conv_query,
    conv_key,
    conv_value,
    decay_log,
    decay_bias,
    out_gain,
    w_out,
    gain_ffn,
    w_hidden,
    w_up,
    w_down,
):
    tokens = block_input.shape[0]
    segment = doc_segments(doc_lengths[0], tokens)
    mix_weights = (w_query, w_key, w_value, w_gate, w_decay, w_write)
    mix_widths = [weight.shape[1] for weight in mix_weights]
    ffn_widths = [w_hidden.shape[1], w_up.shape[1]]
    mixing = gathered_halves(jnp.concatenate(mix_weights, axis=1))
    outward = gathered_halves(w_out)
    feeding = gathered_halves(jnp.concatenate([w_hidden, w_up], axis=1))
    downward = gathered_halves(w_down)
    upstream = cotangent.astype(jnp.bfloat16)

    normed, norm_back = jax.vjp(rms_norm, block_input, gain_mix)
    first_input = normed.astype(jnp.bfloat16)
    projections = column_parts(times(first_input, mixing), mix_widths)

    def mix_local(*operands):
        return delta_mixer(*operands, segment)

    mixed_out, mix_back = jax.vjp(
        mix_local, *projections, conv_query, conv_key, conv_value, decay_log, decay_bias, out_gain
    )
    gated_out = mixed_out.astype(jnp.bfloat16)
    residual = block_input + times(gated_out, outward)
    normed_ffn, norm_ffn_back = jax.vjp(rms_norm, residual, gain_ffn)
    second = normed_ffn.astype(jnp.bfloat16)
    swiglu_out, swiglu_back = jax.vjp(swiglu, *column_parts(times(second, feeding), ffn_widths))
    activation = swiglu_out.astype(jnp.bfloat16)
    block_out = residual + times(activation, downward)
    d_hidden, d_up = swiglu_back(times_back(upstream, downward))
    d_ffn = jnp.concatenate([d_hidden.astype(jnp.bfloat16), d_up.astype(jnp.bfloat16)], axis=1)
    d_second = times_back(d_ffn, feeding)
    ffn_group = group_tokens(jnp.concatenate([d_ffn, upstream], axis=1))
    width = d_ffn.shape[1]
    grad_down = rep_sum(product_left(owned_features(activation), ffn_group[:, width:]))
    grad_ffn = rep_sum(product_left(owned_features(second), ffn_group[:, :width]))
    d_norm_ffn, grad_gain_ffn = norm_ffn_back(d_second)
    d_residual = cotangent + d_norm_ffn
    upstream_mix = d_residual.astype(jnp.bfloat16)
    mix_grads = mix_back(times_back(upstream_mix, outward))
    d_mix = jnp.concatenate([grad.astype(jnp.bfloat16) for grad in mix_grads[:6]], axis=1)
    model = upstream_mix.shape[1]
    mix_group = group_tokens(jnp.concatenate([upstream_mix, d_mix], axis=1))
    grad_out = rep_sum(product_left(owned_features(gated_out), mix_group[:, :model]))
    grad_mix = rep_sum(product_left(owned_features(first_input), mix_group[:, model:]))
    d_first = times_back(d_mix, mixing)
    d_norm, grad_gain_mix = norm_back(d_first)
    input_grad = d_residual + d_norm
    small = (grad_gain_mix, *mix_grads[6:12], grad_gain_ffn)
    flat = jnp.concatenate([grad.reshape(-1) for grad in small])
    flat = total_sum(flat)
    small_totals, start = [], 0
    for grad in small:
        small_totals.append(flat[start : start + grad.size].reshape(grad.shape))
        start = start + grad.size
    mixer_totals = column_parts(grad_mix, mix_widths)
    ffn_totals = column_parts(grad_ffn, ffn_widths)
    return (
        block_out,
        input_grad,
        small_totals[0],
        mixer_totals[0],
        mixer_totals[1],
        mixer_totals[2],
        mixer_totals[3],
        mixer_totals[4],
        mixer_totals[5],
        small_totals[1],
        small_totals[2],
        small_totals[3],
        small_totals[4],
        small_totals[5],
        small_totals[6],
        grad_out,
        small_totals[7],
        ffn_totals[0],
        ffn_totals[1],
        grad_down,
    )


def solution(mesh):
    placed = (
        P(("rep", "fsdp"), None),
        P(("rep", "fsdp"), None),
        P(("rep", "fsdp"), None),
        P(),
        P("fsdp", None),
        P("fsdp", None),
        P("fsdp", None),
        P("fsdp", None),
        P("fsdp", None),
        P("fsdp", None),
        P(),
        P(),
        P(),
        P(),
        P(),
        P(),
        P("fsdp", None),
        P(),
        P("fsdp", None),
        P("fsdp", None),
        P("fsdp", None),
    )
    return jax.shard_map(
        local,
        mesh=mesh,
        in_specs=placed,
        out_specs=(
            P(("rep", "fsdp"), None),
            P(("rep", "fsdp"), None),
            P(),
            P("fsdp", None),
            P("fsdp", None),
            P("fsdp", None),
            P("fsdp", None),
            P("fsdp", None),
            P("fsdp", None),
            P(),
            P(),
            P(),
            P(),
            P(),
            P(),
            P("fsdp", None),
            P(),
            P("fsdp", None),
            P("fsdp", None),
            P("fsdp", None),
        ),
        check_vma=False,
    )
```

```python
import functools

import jax
import jax.numpy as jnp
from jax import lax
from jax.experimental import pallas as pl
from jax.experimental.pallas import tpu as pltpu
from jax.sharding import PartitionSpec as P

EPSILON = 1e-06
TOP_PRECISION = lax.Precision.HIGHEST
MIX_PRECISION = lax.Precision.HIGH
LANES = 128
SUBLANES = 16
MESH = pl.DeviceIdType.MESH


def product(left, right):
    return jnp.dot(left, right, preferred_element_type=jnp.float32)


def product_left(left, right):
    return lax.dot_general(
        left, right, (((0,), (0,)), ((), ())), preferred_element_type=jnp.float32
    )


def product_right(left, right):
    return lax.dot_general(
        left, right, (((1,), (1,)), ((), ())), preferred_element_type=jnp.float32
    )


def rms_norm(values, gain):
    return values * lax.rsqrt(jnp.mean(values * values, axis=-1, keepdims=True) + EPSILON) * gain


def swiglu(hidden_pre, up_pre):
    return jax.nn.silu(hidden_pre) * up_pre


def doc_segments(lengths, tokens):
    order = jnp.arange(lengths.shape[0], dtype=jnp.int32)
    upto = order[None, :] <= order[:, None]
    doc_ends = jnp.sum(jnp.where(upto, lengths[None, :], 0), axis=1)
    positions = jnp.arange(tokens, dtype=jnp.int32)
    return jnp.sum((positions[:, None] >= doc_ends[None, :]).astype(jnp.int32), axis=1)


def shifted(values, offset, fill):
    filler = jnp.full((offset,) + values.shape[1:], fill, values.dtype)
    return jnp.concatenate([filler, values[:-offset]], axis=0)


def short_conv(values, kernel, segment):
    summed = values * kernel[0]
    for offset in range(1, kernel.shape[0]):
        same_doc = (shifted(segment, offset, -1) == segment).astype(values.dtype)
        summed = summed + shifted(values, offset, 0.0) * kernel[offset] * same_doc[:, None]
    return summed


def unit_inverse(lower_part):
    width = lower_part.shape[-1]
    index = jnp.arange(width, dtype=jnp.int32)
    inverse = None
    size = 1
    while size < width:
        rows, columns = index[:, None] // size, index[None, :] // size
        pairs = (rows % 2 == 1) & (columns == rows - 1)
        level = jnp.where(pairs[None], lower_part, 0.0)
        if inverse is None:
            inverse = jnp.eye(width, dtype=lower_part.dtype)[None] - level
        else:
            step = jnp.einsum("hij,hjk->hik", level, inverse, precision=MIX_PRECISION)
            inverse = inverse - jnp.einsum("hij,hjk->hik", inverse, step, precision=MIX_PRECISION)
        size = 2 * size
    return inverse


@jax.custom_vjp
def unit_solve(lower_part, sources):
    return jnp.einsum("hij,hjv->hiv", unit_inverse(lower_part), sources, precision=MIX_PRECISION)


def unit_solve_fwd(lower_part, sources):
    inverse = unit_inverse(lower_part)
    solved = jnp.einsum("hij,hjv->hiv", inverse, sources, precision=MIX_PRECISION)
    return solved, (inverse, solved)


def unit_solve_bwd(saved, d_solved):
    inverse, solved = saved
    d_sources = jnp.einsum("hji,hjv->hiv", inverse, d_solved, precision=MIX_PRECISION)
    d_lower = -jnp.einsum("hiv,hjv->hij", d_sources, solved, precision=MIX_PRECISION)
    return d_lower, d_sources


unit_solve.defvjp(unit_solve_fwd, unit_solve_bwd)


def delta_rule(query_rows, key_matrix, value_rows, decays, strength, segment):
    width = segment.shape[0]
    positions = jnp.arange(width, dtype=jnp.int32)
    same_doc = segment[:, None] == segment[None, :]
    lower_mask = same_doc & (positions[:, None] >= positions[None, :])
    strict_mask = same_doc & (positions[:, None] > positions[None, :])
    cumulative = jnp.einsum(
        "ij,hj->hi", lower_mask.astype(decays.dtype), decays, precision=TOP_PRECISION
    )
    spread = jnp.minimum(cumulative[:, :, None] - cumulative[:, None, :], 0.0)
    ratios = jnp.where(lower_mask[None], jnp.exp(spread), 0.0)
    key_inner = jnp.einsum("hid,hjd->hij", key_matrix, key_matrix, precision=MIX_PRECISION)
    lower_part = jnp.where(strict_mask[None], strength[:, :, None] * ratios * key_inner, 0.0)
    delta_rows = unit_solve(lower_part, strength[:, :, None] * value_rows)
    scores = jnp.einsum("hid,hjd->hij", query_rows, key_matrix, precision=MIX_PRECISION) * ratios
    return jnp.einsum("hij,hjv->hiv", scores, delta_rows, precision=MIX_PRECISION)


def delta_mixer(
    query_proj,
    key_proj,
    value_proj,
    gate_proj,
    decay_proj,
    write_proj,
    conv_query,
    conv_key,
    conv_value,
    decay_log,
    decay_bias,
    out_gain,
    segment,
):
    tokens = query_proj.shape[0]
    head_count = decay_log.shape[0]
    key_dim = query_proj.shape[1] // head_count
    value_dim = value_proj.shape[1] // head_count
    query_rows = jax.nn.silu(short_conv(query_proj, conv_query, segment)).reshape(
        tokens, head_count, key_dim
    )
    key_matrix = jax.nn.silu(short_conv(key_proj, conv_key, segment)).reshape(
        tokens, head_count, key_dim
    )
    value_rows = jax.nn.silu(short_conv(value_proj, conv_value, segment)).reshape(
        tokens, head_count, value_dim
    )
    query_rows = (
        query_rows
        * lax.rsqrt(jnp.sum(query_rows * query_rows, axis=2, keepdims=True) + EPSILON)
        * key_dim ** (-0.5)
    )
    key_matrix = key_matrix * lax.rsqrt(
        jnp.sum(key_matrix * key_matrix, axis=2, keepdims=True) + EPSILON
    )
    decays = -jnp.exp(decay_log) * jax.nn.softplus(decay_proj + decay_bias)
    strength = jax.nn.sigmoid(write_proj)

    readout_rows = delta_rule(
        jnp.swapaxes(query_rows, 0, 1),
        jnp.swapaxes(key_matrix, 0, 1),
        jnp.swapaxes(value_rows, 0, 1),
        decays.T,
        strength.T,
        segment,
    )
    readout_rows = jnp.swapaxes(readout_rows, 0, 1)
    readout_rows = (
        readout_rows
        * lax.rsqrt(jnp.mean(readout_rows * readout_rows, axis=2, keepdims=True) + EPSILON)
        * out_gain
    )
    readout_rows = readout_rows * jax.nn.silu(gate_proj.reshape(tokens, head_count, value_dim))
    return readout_rows.reshape(tokens, head_count * value_dim)


def ring_index(place, size):
    half = (size + 1) // 2
    back = place // half
    return (1 - back) * (2 * place) + back * (2 * (size - 1 - place) + 1)


def ring_place(index, size):
    odd = index % 2
    return (1 - odd) * (index // 2) + odd * (size - 1 - index // 2)


def ring_neighbours(size):
    place = ring_place(lax.axis_index("fsdp"), size)
    return (
        place,
        ring_index((place + 1) % size, size),
        ring_index((place + size - 1) % size, size),
    )


def greet(partners):
    barrier = pltpu.get_barrier_semaphore()
    for partner in partners:
        pl.semaphore_signal(barrier, inc=1, device_id=partner, device_id_type=MESH)
    pl.semaphore_wait(barrier, len(partners))


def share(shape, core, way):
    rows, columns = shape
    by_rows = (rows // 2) % SUBLANES == 0
    height = rows // 2 if by_rows else rows
    width = columns if by_rows else columns // 2
    cut = (width // (2 * LANES)) * LANES
    first, part = ((0, cut), (cut, width - cut))[way]
    if by_rows:
        return core * height, height, first, part
    return 0, height, pl.multiple_of(core * width + first, LANES), part


def gather_kernel(size, count, *refs):
    shards, wholes = refs[:count], refs[count : 2 * count]
    ring_out, ring_in, core_out, core_in, local_sem = refs[2 * count :]
    place, right, left = ring_neighbours(size)
    me, rep = lax.axis_index("fsdp"), lax.axis_index("rep")
    core = rep % 2
    sibling = rep + 1 - 2 * core
    greet(((rep, right), (rep, left), (sibling, me)))

    def piece(ref, array, way, base):
        top, height, first, width = share(shards[array].shape, core, way)
        start = pl.multiple_of(base + top, SUBLANES)
        return ref.at[pl.ds(start, height), pl.ds(first, width)]

    def placed(array, way, step):
        shift = (size - step) if way == 0 else step
        owner = ring_index((place + shift) % size, size)
        return piece(wholes[array], array, way, owner * shards[array].shape[0])

    def ring_copy(array, way, step):
        block = placed(array, way, step)
        return pltpu.make_async_remote_copy(
            src_ref=block if step else piece(shards[array], array, way, 0),
            dst_ref=block,
            send_sem=ring_out.at[array, way, step],
            recv_sem=ring_in.at[array, way, step],
            device_id=(rep, right if way == 0 else left),
            device_id_type=MESH,
        )

    def core_copy(array, way, step):
        block = placed(array, way, step + 1)
        return pltpu.make_async_remote_copy(
            src_ref=block,
            dst_ref=block,
            send_sem=core_out.at[array, way, step],
            recv_sem=core_in.at[array, way, step],
            device_id=(sibling, me),
            device_id_type=MESH,
        )

    def own_copy(array):
        rows = shards[array].shape[0]
        start = pl.multiple_of(me * rows, SUBLANES)
        return pltpu.make_async_copy(
            shards[array], wholes[array].at[pl.ds(start, rows)], local_sem.at[array]
        )

    pairs = [(array, way) for array in range(count) for way in range(2)]
    for array, way in pairs:
        ring_copy(array, way, 0).start()
    for array in range(count):
        own_copy(array).start()
    for step in range(size - 1):
        for array, way in pairs:
            ring_copy(array, way, step).wait_recv()
            if step < size - 2:
                ring_copy(array, way, step + 1).start()
            core_copy(array, way, step).start()
    for array in range(count):
        own_copy(array).wait()
    for step in range(size - 1):
        for array, way in pairs:
            ring_copy(array, way, step).wait_send()
            core_copy(array, way, step).wait()


def gathered(weights, kernel_id):
    size, reps = lax.axis_size("fsdp"), lax.axis_size("rep")
    if size < 3 or reps % 2:
        return [lax.all_gather(weight, "fsdp", axis=0, tiled=True) for weight in weights]
    count = len(weights)
    anywhere = pl.BlockSpec(memory_space=pl.ANY)
    semaphores = pltpu.SemaphoreType.DMA((count, 2, size - 1))
    return pl.pallas_call(
        functools.partial(gather_kernel, size, count),
        out_shape=[
            jax.ShapeDtypeStruct((size * weight.shape[0], weight.shape[1]), weight.dtype)
            for weight in weights
        ],
        in_specs=[anywhere] * count,
        out_specs=[anywhere] * count,
        scratch_shapes=[semaphores] * 4 + [pltpu.SemaphoreType.DMA((count,))],
        compiler_params=pltpu.CompilerParams(collective_id=kernel_id, has_side_effects=True),
        name="gather_rows",
    )(*weights)


def swapped(array, axis_size, bit):
    return lax.ppermute(array, "rep", [(rank, rank ^ bit) for rank in range(axis_size)])


def paired(axis_size):
    return axis_size > 1 and axis_size & (axis_size - 1) == 0


def rounded(values):
    return lax.reduce_precision(values, 8, 7).astype(jnp.bfloat16)


def rep_sum(total):
    reps = lax.axis_size("rep")
    if not paired(reps):
        return lax.psum(total.astype(jnp.bfloat16), "rep").astype(jnp.float32)
    half = total.shape[0] // 2
    parity = lax.axis_index("rep") % 2
    sent = lax.dynamic_slice_in_dim(total, (1 - parity) * half, half, axis=0)
    kept = lax.dynamic_slice_in_dim(total, parity * half, half, axis=0)
    own = rounded(kept + swapped(rounded(sent), reps, 1).astype(jnp.float32))
    bit = 2
    while bit < reps:
        own = rounded(own.astype(jnp.float32) + swapped(own, reps, bit).astype(jnp.float32))
        bit = 2 * bit
    other = swapped(own, reps, 1)
    first = jnp.where(parity == 0, own, other)
    second = jnp.where(parity == 0, other, own)
    return jnp.concatenate([first, second], axis=0).astype(jnp.float32)


def total_sum(values):
    for name in ("rep", "fsdp"):
        size = lax.axis_size(name)
        if size & (size - 1):
            values = lax.psum(values, name)
            continue
        bit = 1
        while bit < size:
            pairs = [(rank, rank ^ bit) for rank in range(size)]
            values = values + lax.ppermute(values, name, pairs)
            bit = 2 * bit
    return values


def group_tokens(rows):
    return lax.all_gather(rows, "fsdp", axis=0, tiled=True)


def owned_features(rows):
    return lax.all_to_all(rows, "fsdp", split_axis=1, concat_axis=0, tiled=True)


def column_parts(array, widths):
    parts, start = [], 0
    for width in widths:
        parts.append(array[:, start : start + width])
        start = start + width
    return parts


def local(
    block_input,
    cotangent,
    doc_lengths,
    gain_mix,
    w_query,
    w_key,
    w_value,
    w_gate,
    w_decay,
    w_write,
    conv_query,
    conv_key,
    conv_value,
    decay_log,
    decay_bias,
    out_gain,
    w_out,
    gain_ffn,
    w_hidden,
    w_up,
    w_down,
):
    tokens = block_input.shape[0]
    segment = doc_segments(doc_lengths[0], tokens)
    mix_weights = (w_query, w_key, w_value, w_gate, w_decay, w_write)
    mix_widths = [weight.shape[1] for weight in mix_weights]
    ffn_widths = [w_hidden.shape[1], w_up.shape[1]]
    mix_width = sum(mix_widths)
    spare = -mix_width % LANES
    filler = jnp.zeros((w_query.shape[0], spare), w_query.dtype)
    (mixing,) = gathered([jnp.concatenate([*mix_weights, filler], axis=1)], 0)
    outward, feeding, downward = gathered(
        [w_out, jnp.concatenate([w_hidden, w_up], axis=1), w_down], 1
    )
    upstream = cotangent.astype(jnp.bfloat16)

    normed, norm_back = jax.vjp(rms_norm, block_input, gain_mix)
    first_input = normed.astype(jnp.bfloat16)
    projections = column_parts(product(first_input, mixing), mix_widths)

    def mix_local(*operands):
        return delta_mixer(*operands, segment)

    mixed_out, mix_back = jax.vjp(
        mix_local, *projections, conv_query, conv_key, conv_value, decay_log, decay_bias, out_gain
    )
    gated_out = mixed_out.astype(jnp.bfloat16)
    residual = block_input + product(gated_out, outward)
    normed_ffn, norm_ffn_back = jax.vjp(rms_norm, residual, gain_ffn)
    second = normed_ffn.astype(jnp.bfloat16)
    swiglu_out, swiglu_back = jax.vjp(swiglu, *column_parts(product(second, feeding), ffn_widths))
    activation = swiglu_out.astype(jnp.bfloat16)
    block_out = residual + product(activation, downward)
    d_hidden, d_up = swiglu_back(product_right(upstream, downward))
    d_ffn = jnp.concatenate([d_hidden.astype(jnp.bfloat16), d_up.astype(jnp.bfloat16)], axis=1)
    d_second = product_right(d_ffn, feeding)
    ffn_group = group_tokens(jnp.concatenate([d_ffn, upstream], axis=1))
    width = d_ffn.shape[1]
    grad_down = rep_sum(product_left(owned_features(activation), ffn_group[:, width:]))
    grad_ffn = rep_sum(product_left(owned_features(second), ffn_group[:, :width]))
    d_norm_ffn, grad_gain_ffn = norm_ffn_back(d_second)
    d_residual = cotangent + d_norm_ffn
    upstream_mix = d_residual.astype(jnp.bfloat16)
    mix_grads = mix_back(product_right(upstream_mix, outward))
    d_mix = jnp.concatenate([grad.astype(jnp.bfloat16) for grad in mix_grads[:6]], axis=1)
    model = upstream_mix.shape[1]
    mix_group = group_tokens(jnp.concatenate([upstream_mix, d_mix], axis=1))
    grad_out = rep_sum(product_left(owned_features(gated_out), mix_group[:, :model]))
    grad_mix = rep_sum(product_left(owned_features(first_input), mix_group[:, model:]))
    d_first = product_right(d_mix, mixing[:, :mix_width])
    d_norm, grad_gain_mix = norm_back(d_first)
    input_grad = d_residual + d_norm
    small = (grad_gain_mix, *mix_grads[6:12], grad_gain_ffn)
    flat = jnp.concatenate([grad.reshape(-1) for grad in small])
    flat = total_sum(flat)
    small_totals, start = [], 0
    for grad in small:
        small_totals.append(flat[start : start + grad.size].reshape(grad.shape))
        start = start + grad.size
    mixer_totals = column_parts(grad_mix, mix_widths)
    ffn_totals = column_parts(grad_ffn, ffn_widths)
    return (
        block_out,
        input_grad,
        small_totals[0],
        mixer_totals[0],
        mixer_totals[1],
        mixer_totals[2],
        mixer_totals[3],
        mixer_totals[4],
        mixer_totals[5],
        small_totals[1],
        small_totals[2],
        small_totals[3],
        small_totals[4],
        small_totals[5],
        small_totals[6],
        grad_out,
        small_totals[7],
        ffn_totals[0],
        ffn_totals[1],
        grad_down,
    )


def solution(mesh):
    placed = (
        P(("rep", "fsdp"), None),
        P(("rep", "fsdp"), None),
        P(("rep", "fsdp"), None),
        P(),
        P("fsdp", None),
        P("fsdp", None),
        P("fsdp", None),
        P("fsdp", None),
        P("fsdp", None),
        P("fsdp", None),
        P(),
        P(),
        P(),
        P(),
        P(),
        P(),
        P("fsdp", None),
        P(),
        P("fsdp", None),
        P("fsdp", None),
        P("fsdp", None),
    )
    return jax.shard_map(
        local,
        mesh=mesh,
        in_specs=placed,
        out_specs=(
            P(("rep", "fsdp"), None),
            P(("rep", "fsdp"), None),
            P(),
            P("fsdp", None),
            P("fsdp", None),
            P("fsdp", None),
            P("fsdp", None),
            P("fsdp", None),
            P("fsdp", None),
            P(),
            P(),
            P(),
            P(),
            P(),
            P(),
            P("fsdp", None),
            P(),
            P("fsdp", None),
            P("fsdp", None),
            P("fsdp", None),
        ),
        check_vma=False,
    )
```

```python
import functools

import jax
import jax.numpy as jnp
from jax import lax
from jax.experimental import pallas as pl
from jax.experimental.pallas import tpu as pltpu
from jax.sharding import PartitionSpec as P

EPSILON = 1e-06
TOP_PRECISION = lax.Precision.HIGHEST
MIX_PRECISION = lax.Precision.HIGH
LANES = 128
SUBLANES = 16
VMEM_BYTES = 48 * 1024 * 1024
MESH = pl.DeviceIdType.MESH


def product(left, right):
    return jnp.dot(left, right, preferred_element_type=jnp.float32)


def product_left(left, right):
    return lax.dot_general(
        left, right, (((0,), (0,)), ((), ())), preferred_element_type=jnp.float32
    )


def product_right(left, right):
    return lax.dot_general(
        left, right, (((1,), (1,)), ((), ())), preferred_element_type=jnp.float32
    )


def rms_norm(values, gain):
    return values * lax.rsqrt(jnp.mean(values * values, axis=-1, keepdims=True) + EPSILON) * gain


def swiglu(hidden_pre, up_pre):
    return jax.nn.silu(hidden_pre) * up_pre


def doc_segments(lengths, tokens):
    order = jnp.arange(lengths.shape[0], dtype=jnp.int32)
    upto = order[None, :] <= order[:, None]
    doc_ends = jnp.sum(jnp.where(upto, lengths[None, :], 0), axis=1)
    positions = jnp.arange(tokens, dtype=jnp.int32)
    return jnp.sum((positions[:, None] >= doc_ends[None, :]).astype(jnp.int32), axis=1)


def shifted(values, offset, fill):
    filler = jnp.full((offset,) + values.shape[1:], fill, values.dtype)
    return jnp.concatenate([filler, values[:-offset]], axis=0)


def short_conv(values, kernel, segment):
    summed = values * kernel[0]
    for offset in range(1, kernel.shape[0]):
        same_doc = (shifted(segment, offset, -1) == segment).astype(values.dtype)
        summed = summed + shifted(values, offset, 0.0) * kernel[offset] * same_doc[:, None]
    return summed


def unit_inverse(lower_part):
    width = lower_part.shape[-1]
    index = jnp.arange(width, dtype=jnp.int32)
    inverse = None
    size = 1
    while size < width:
        rows, columns = index[:, None] // size, index[None, :] // size
        pairs = (rows % 2 == 1) & (columns == rows - 1)
        level = jnp.where(pairs[None], lower_part, 0.0)
        if inverse is None:
            inverse = jnp.eye(width, dtype=lower_part.dtype)[None] - level
        else:
            step = jnp.einsum("hij,hjk->hik", level, inverse, precision=MIX_PRECISION)
            inverse = inverse - jnp.einsum("hij,hjk->hik", inverse, step, precision=MIX_PRECISION)
        size = 2 * size
    return inverse


@jax.custom_vjp
def unit_solve(lower_part, sources):
    return jnp.einsum("hij,hjv->hiv", unit_inverse(lower_part), sources, precision=MIX_PRECISION)


def unit_solve_fwd(lower_part, sources):
    inverse = unit_inverse(lower_part)
    solved = jnp.einsum("hij,hjv->hiv", inverse, sources, precision=MIX_PRECISION)
    return solved, (inverse, solved)


def unit_solve_bwd(saved, d_solved):
    inverse, solved = saved
    d_sources = jnp.einsum("hji,hjv->hiv", inverse, d_solved, precision=MIX_PRECISION)
    d_lower = -jnp.einsum("hiv,hjv->hij", d_sources, solved, precision=MIX_PRECISION)
    return d_lower, d_sources


unit_solve.defvjp(unit_solve_fwd, unit_solve_bwd)


def delta_rule(query_rows, key_matrix, value_rows, decays, strength, segment):
    width = segment.shape[0]
    positions = jnp.arange(width, dtype=jnp.int32)
    same_doc = segment[:, None] == segment[None, :]
    lower_mask = same_doc & (positions[:, None] >= positions[None, :])
    strict_mask = same_doc & (positions[:, None] > positions[None, :])
    cumulative = jnp.einsum(
        "ij,hj->hi", lower_mask.astype(decays.dtype), decays, precision=TOP_PRECISION
    )
    spread = jnp.minimum(cumulative[:, :, None] - cumulative[:, None, :], 0.0)
    ratios = jnp.where(lower_mask[None], jnp.exp(spread), 0.0)
    key_inner = jnp.einsum("hid,hjd->hij", key_matrix, key_matrix, precision=MIX_PRECISION)
    lower_part = jnp.where(strict_mask[None], strength[:, :, None] * ratios * key_inner, 0.0)
    delta_rows = unit_solve(lower_part, strength[:, :, None] * value_rows)
    scores = jnp.einsum("hid,hjd->hij", query_rows, key_matrix, precision=MIX_PRECISION) * ratios
    return jnp.einsum("hij,hjv->hiv", scores, delta_rows, precision=MIX_PRECISION)


def delta_mixer(
    query_proj,
    key_proj,
    value_proj,
    gate_proj,
    decay_proj,
    write_proj,
    conv_query,
    conv_key,
    conv_value,
    decay_log,
    decay_bias,
    out_gain,
    segment,
):
    tokens = query_proj.shape[0]
    head_count = decay_log.shape[0]
    key_dim = query_proj.shape[1] // head_count
    value_dim = value_proj.shape[1] // head_count
    query_rows = jax.nn.silu(short_conv(query_proj, conv_query, segment)).reshape(
        tokens, head_count, key_dim
    )
    key_matrix = jax.nn.silu(short_conv(key_proj, conv_key, segment)).reshape(
        tokens, head_count, key_dim
    )
    value_rows = jax.nn.silu(short_conv(value_proj, conv_value, segment)).reshape(
        tokens, head_count, value_dim
    )
    query_rows = (
        query_rows
        * lax.rsqrt(jnp.sum(query_rows * query_rows, axis=2, keepdims=True) + EPSILON)
        * key_dim ** (-0.5)
    )
    key_matrix = key_matrix * lax.rsqrt(
        jnp.sum(key_matrix * key_matrix, axis=2, keepdims=True) + EPSILON
    )
    decays = -jnp.exp(decay_log) * jax.nn.softplus(decay_proj + decay_bias)
    strength = jax.nn.sigmoid(write_proj)

    readout_rows = delta_rule(
        jnp.swapaxes(query_rows, 0, 1),
        jnp.swapaxes(key_matrix, 0, 1),
        jnp.swapaxes(value_rows, 0, 1),
        decays.T,
        strength.T,
        segment,
    )
    readout_rows = jnp.swapaxes(readout_rows, 0, 1)
    readout_rows = (
        readout_rows
        * lax.rsqrt(jnp.mean(readout_rows * readout_rows, axis=2, keepdims=True) + EPSILON)
        * out_gain
    )
    readout_rows = readout_rows * jax.nn.silu(gate_proj.reshape(tokens, head_count, value_dim))
    return readout_rows.reshape(tokens, head_count * value_dim)


def ring_index(place, size):
    half = (size + 1) // 2
    back = place // half
    return (1 - back) * (2 * place) + back * (2 * (size - 1 - place) + 1)


def ring_place(index, size):
    odd = index % 2
    return (1 - odd) * (index // 2) + odd * (size - 1 - index // 2)


def ring_neighbours(size):
    place = ring_place(lax.axis_index("fsdp"), size)
    return (
        place,
        ring_index((place + 1) % size, size),
        ring_index((place + size - 1) % size, size),
    )


def greet(partners):
    barrier = pltpu.get_barrier_semaphore()
    for partner in partners:
        pl.semaphore_signal(barrier, inc=1, device_id=partner, device_id_type=MESH)
    pl.semaphore_wait(barrier, len(partners))


def column_cuts(columns):
    cut = (columns // (2 * LANES)) * LANES
    return ((0, cut), (cut, columns - cut))


def share(shape, core, way):
    rows, columns = shape
    by_rows = (rows // 2) % SUBLANES == 0
    height = rows // 2 if by_rows else rows
    width = columns if by_rows else columns // 2
    first, part = column_cuts(width)[way]
    if by_rows:
        return core * height, height, first, part
    return 0, height, pl.multiple_of(core * width + first, LANES), part


def gather_kernel(size, count, *refs):
    shards, wholes = refs[:count], refs[count : 2 * count]
    ring_out, ring_in, core_out, core_in, local_sem = refs[2 * count :]
    place, right, left = ring_neighbours(size)
    me, rep = lax.axis_index("fsdp"), lax.axis_index("rep")
    core = rep % 2
    sibling = rep + 1 - 2 * core
    greet(((rep, right), (rep, left), (sibling, me)))

    def piece(ref, array, way, base):
        top, height, first, width = share(shards[array].shape, core, way)
        start = pl.multiple_of(base + top, SUBLANES)
        return ref.at[pl.ds(start, height), pl.ds(first, width)]

    def placed(array, way, step):
        shift = (size - step) if way == 0 else step
        owner = ring_index((place + shift) % size, size)
        return piece(wholes[array], array, way, owner * shards[array].shape[0])

    def ring_copy(array, way, step):
        block = placed(array, way, step)
        return pltpu.make_async_remote_copy(
            src_ref=block if step else piece(shards[array], array, way, 0),
            dst_ref=block,
            send_sem=ring_out.at[array, way, step],
            recv_sem=ring_in.at[array, way, step],
            device_id=(rep, right if way == 0 else left),
            device_id_type=MESH,
        )

    def core_copy(array, way, step):
        block = placed(array, way, step + 1)
        return pltpu.make_async_remote_copy(
            src_ref=block,
            dst_ref=block,
            send_sem=core_out.at[array, way, step],
            recv_sem=core_in.at[array, way, step],
            device_id=(sibling, me),
            device_id_type=MESH,
        )

    def own_copy(array):
        rows = shards[array].shape[0]
        start = pl.multiple_of(me * rows, SUBLANES)
        return pltpu.make_async_copy(
            shards[array], wholes[array].at[pl.ds(start, rows)], local_sem.at[array]
        )

    pairs = [(array, way) for array in range(count) for way in range(2)]
    for array, way in pairs:
        ring_copy(array, way, 0).start()
    for array in range(count):
        own_copy(array).start()
    for step in range(size - 1):
        for array, way in pairs:
            ring_copy(array, way, step).wait_recv()
            if step < size - 2:
                ring_copy(array, way, step + 1).start()
            core_copy(array, way, step).start()
    for array in range(count):
        own_copy(array).wait()
    for step in range(size - 1):
        for array, way in pairs:
            ring_copy(array, way, step).wait_send()
            core_copy(array, way, step).wait()


def gathered(weights, kernel_id):
    size, reps = lax.axis_size("fsdp"), lax.axis_size("rep")
    if size < 3 or reps % 2:
        return [lax.all_gather(weight, "fsdp", axis=0, tiled=True) for weight in weights]
    count = len(weights)
    anywhere = pl.BlockSpec(memory_space=pl.ANY)
    semaphores = pltpu.SemaphoreType.DMA((count, 2, size - 1))
    return pl.pallas_call(
        functools.partial(gather_kernel, size, count),
        out_shape=[
            jax.ShapeDtypeStruct((size * weight.shape[0], weight.shape[1]), weight.dtype)
            for weight in weights
        ],
        in_specs=[anywhere] * count,
        out_specs=[anywhere] * count,
        scratch_shapes=[semaphores] * 4 + [pltpu.SemaphoreType.DMA((count,))],
        compiler_params=pltpu.CompilerParams(collective_id=kernel_id, has_side_effects=True),
        name="gather_rows",
    )(*weights)


def swapped(array, axis_size, bit):
    return lax.ppermute(array, "rep", [(rank, rank ^ bit) for rank in range(axis_size)])


def paired(axis_size):
    return axis_size > 1 and axis_size & (axis_size - 1) == 0


def rounded(values):
    return lax.reduce_precision(values, 8, 7).astype(jnp.bfloat16)


def scatter_kernel(size, count, *refs):
    parts, sums = refs[:count], refs[count : 2 * count]
    slots = refs[2 * count : 4 * count]
    ring_out, ring_in = refs[4 * count :]
    place, right, left = ring_neighbours(size)
    rep = lax.axis_index("rep")
    greet(((rep, right), (rep, left)))

    def part(array, way, step):
        shift = (size - 1 - step) if way == 0 else (1 + step)
        owner = ring_index((place + shift) % size, size)
        first, width = column_cuts(parts[array].shape[2])[way]
        return parts[array].at[owner, :, pl.ds(first, width)]

    def slot(array, way, step):
        return slots[2 * array + way].at[step]

    def ring_copy(array, way, step):
        return pltpu.make_async_remote_copy(
            src_ref=slot(array, way, step - 1) if step else part(array, way, 0),
            dst_ref=slot(array, way, step),
            send_sem=ring_out.at[array, way, step],
            recv_sem=ring_in.at[array, way, step],
            device_id=(rep, right if way == 0 else left),
            device_id_type=MESH,
        )

    pairs = [(array, way) for array in range(count) for way in range(2)]
    for array, way in pairs:
        ring_copy(array, way, 0).start()
    for step in range(size - 1):
        for array, way in pairs:
            ring_copy(array, way, step).wait_recv()
            arrived = slot(array, way, step)
            here = part(array, way, step + 1)
            first, width = column_cuts(parts[array].shape[2])[way]
            total = arrived[...].astype(jnp.float32) + here[...].astype(jnp.float32)
            if step < size - 2:
                arrived[...] = total.astype(arrived.dtype)
                ring_copy(array, way, step + 1).start()
            else:
                sums[array][:, pl.ds(first, width)] = total.astype(sums[array].dtype)
    for step in range(size - 1):
        for array, way in pairs:
            ring_copy(array, way, step).wait_send()


def scattered(parts, kernel_id):
    size = lax.axis_size("fsdp")
    count = len(parts)
    on_chip = pl.BlockSpec(memory_space=pltpu.VMEM)
    slots = [
        pltpu.VMEM((size - 1, part.shape[1], width), part.dtype)
        for part in parts
        for _, width in column_cuts(part.shape[2])
    ]
    semaphores = pltpu.SemaphoreType.DMA((count, 2, size - 1))
    return pl.pallas_call(
        functools.partial(scatter_kernel, size, count),
        out_shape=[jax.ShapeDtypeStruct(part.shape[1:], part.dtype) for part in parts],
        in_specs=[on_chip] * count,
        out_specs=[on_chip] * count,
        scratch_shapes=slots + [semaphores] * 2,
        compiler_params=pltpu.CompilerParams(
            collective_id=kernel_id, has_side_effects=True, vmem_limit_bytes=VMEM_BYTES
        ),
        name="scatter_sums",
    )(*parts)


def core_halves(rows):
    size = lax.axis_size("fsdp")
    tokens, features = rows.shape
    split = rows.reshape(tokens, size, 2, features // (2 * size))
    first = split[:, :, 0].reshape(tokens, features // 2)
    second = split[:, :, 1].reshape(tokens, features // 2)
    even = lax.axis_index("rep") % 2 == 0
    return jnp.where(even, first, second), jnp.where(even, second, first)


def chip_tokens(rows):
    return jnp.concatenate([rows, swapped(rows, lax.axis_size("rep"), 1)], axis=0)


def chip_features(rows):
    own, other = core_halves(rows)
    return jnp.concatenate([own, swapped(other, lax.axis_size("rep"), 1)], axis=0)


def weight_grads(lefts, rights, kernel_id):
    size, reps = lax.axis_size("fsdp"), lax.axis_size("rep")
    if size < 3 or not paired(reps):
        totals = []
        for left, right in zip(lefts, rights):
            part = product_left(left, right).astype(jnp.bfloat16)
            part = lax.psum_scatter(part, "fsdp", scatter_dimension=0, tiled=True)
            totals.append(lax.psum(part, "rep").astype(jnp.float32))
        return totals
    parts = []
    for left, right in zip(lefts, rights):
        spare = -right.shape[1] % LANES
        right = jnp.pad(right, ((0, 0), (0, spare)))
        part = product_left(chip_features(left), chip_tokens(right)).astype(jnp.bfloat16)
        parts.append(part.reshape(size, part.shape[0] // size, part.shape[1]))
    totals = []
    for own, right in zip(scattered(parts, kernel_id), rights):
        own = own[:, : right.shape[1]]
        bit = 2
        while bit < reps:
            own = rounded(own.astype(jnp.float32) + swapped(own, reps, bit).astype(jnp.float32))
            bit = 2 * bit
        other = swapped(own, reps, 1)
        even = lax.axis_index("rep") % 2 == 0
        first, second = jnp.where(even, own, other), jnp.where(even, other, own)
        totals.append(jnp.concatenate([first, second], axis=0).astype(jnp.float32))
    return totals


def total_sum(values):
    for name in ("rep", "fsdp"):
        size = lax.axis_size(name)
        if size & (size - 1):
            values = lax.psum(values, name)
            continue
        bit = 1
        while bit < size:
            pairs = [(rank, rank ^ bit) for rank in range(size)]
            values = values + lax.ppermute(values, name, pairs)
            bit = 2 * bit
    return values


def column_parts(array, widths):
    parts, start = [], 0
    for width in widths:
        parts.append(array[:, start : start + width])
        start = start + width
    return parts


def local(
    block_input,
    cotangent,
    doc_lengths,
    gain_mix,
    w_query,
    w_key,
    w_value,
    w_gate,
    w_decay,
    w_write,
    conv_query,
    conv_key,
    conv_value,
    decay_log,
    decay_bias,
    out_gain,
    w_out,
    gain_ffn,
    w_hidden,
    w_up,
    w_down,
):
    tokens = block_input.shape[0]
    segment = doc_segments(doc_lengths[0], tokens)
    mix_weights = (w_query, w_key, w_value, w_gate, w_decay, w_write)
    mix_widths = [weight.shape[1] for weight in mix_weights]
    ffn_widths = [w_hidden.shape[1], w_up.shape[1]]
    mix_width = sum(mix_widths)
    spare = -mix_width % LANES
    filler = jnp.zeros((w_query.shape[0], spare), w_query.dtype)
    (mixing,) = gathered([jnp.concatenate([*mix_weights, filler], axis=1)], 0)
    outward, feeding, downward = gathered(
        [w_out, jnp.concatenate([w_hidden, w_up], axis=1), w_down], 1
    )
    upstream = cotangent.astype(jnp.bfloat16)

    normed, norm_back = jax.vjp(rms_norm, block_input, gain_mix)
    first_input = normed.astype(jnp.bfloat16)
    projections = column_parts(product(first_input, mixing), mix_widths)

    def mix_local(*operands):
        return delta_mixer(*operands, segment)

    mixed_out, mix_back = jax.vjp(
        mix_local, *projections, conv_query, conv_key, conv_value, decay_log, decay_bias, out_gain
    )
    gated_out = mixed_out.astype(jnp.bfloat16)
    residual = block_input + product(gated_out, outward)
    normed_ffn, norm_ffn_back = jax.vjp(rms_norm, residual, gain_ffn)
    second = normed_ffn.astype(jnp.bfloat16)
    swiglu_out, swiglu_back = jax.vjp(swiglu, *column_parts(product(second, feeding), ffn_widths))
    activation = swiglu_out.astype(jnp.bfloat16)
    block_out = residual + product(activation, downward)
    d_hidden, d_up = swiglu_back(product_right(upstream, downward))
    d_ffn = jnp.concatenate([d_hidden.astype(jnp.bfloat16), d_up.astype(jnp.bfloat16)], axis=1)
    d_second = product_right(d_ffn, feeding)
    grad_down, grad_ffn = weight_grads([activation, second], [upstream, d_ffn], 2)
    d_norm_ffn, grad_gain_ffn = norm_ffn_back(d_second)
    d_residual = cotangent + d_norm_ffn
    upstream_mix = d_residual.astype(jnp.bfloat16)
    mix_grads = mix_back(product_right(upstream_mix, outward))
    d_mix = jnp.concatenate([grad.astype(jnp.bfloat16) for grad in mix_grads[:6]], axis=1)
    grad_out, grad_mix = weight_grads([gated_out, first_input], [upstream_mix, d_mix], 3)
    d_first = product_right(d_mix, mixing[:, :mix_width])
    d_norm, grad_gain_mix = norm_back(d_first)
    input_grad = d_residual + d_norm
    small = (grad_gain_mix, *mix_grads[6:12], grad_gain_ffn)
    flat = jnp.concatenate([grad.reshape(-1) for grad in small])
    flat = total_sum(flat)
    small_totals, start = [], 0
    for grad in small:
        small_totals.append(flat[start : start + grad.size].reshape(grad.shape))
        start = start + grad.size
    mixer_totals = column_parts(grad_mix, mix_widths)
    ffn_totals = column_parts(grad_ffn, ffn_widths)
    return (
        block_out,
        input_grad,
        small_totals[0],
        mixer_totals[0],
        mixer_totals[1],
        mixer_totals[2],
        mixer_totals[3],
        mixer_totals[4],
        mixer_totals[5],
        small_totals[1],
        small_totals[2],
        small_totals[3],
        small_totals[4],
        small_totals[5],
        small_totals[6],
        grad_out,
        small_totals[7],
        ffn_totals[0],
        ffn_totals[1],
        grad_down,
    )


def solution(mesh):
    placed = (
        P(("rep", "fsdp"), None),
        P(("rep", "fsdp"), None),
        P(("rep", "fsdp"), None),
        P(),
        P("fsdp", None),
        P("fsdp", None),
        P("fsdp", None),
        P("fsdp", None),
        P("fsdp", None),
        P("fsdp", None),
        P(),
        P(),
        P(),
        P(),
        P(),
        P(),
        P("fsdp", None),
        P(),
        P("fsdp", None),
        P("fsdp", None),
        P("fsdp", None),
    )
    return jax.shard_map(
        local,
        mesh=mesh,
        in_specs=placed,
        out_specs=(
            P(("rep", "fsdp"), None),
            P(("rep", "fsdp"), None),
            P(),
            P("fsdp", None),
            P("fsdp", None),
            P("fsdp", None),
            P("fsdp", None),
            P("fsdp", None),
            P("fsdp", None),
            P(),
            P(),
            P(),
            P(),
            P(),
            P(),
            P("fsdp", None),
            P(),
            P("fsdp", None),
            P("fsdp", None),
            P("fsdp", None),
        ),
        check_vma=False,
    )
```

```python
import functools

import jax
import jax.numpy as jnp
from jax import lax
from jax.experimental import pallas as pl
from jax.experimental.pallas import tpu as pltpu
from jax.sharding import PartitionSpec as P

EPSILON = 1e-06
TOP_PRECISION = lax.Precision.HIGHEST
MIX_PRECISION = lax.Precision.HIGH
LANES = 128
SUBLANES = 16
VMEM_BYTES = 48 * 1024 * 1024
MESH = pl.DeviceIdType.MESH


def product(left, right):
    return jnp.dot(left, right, preferred_element_type=jnp.float32)


def product_left(left, right):
    return lax.dot_general(
        left, right, (((0,), (0,)), ((), ())), preferred_element_type=jnp.float32
    )


def product_right(left, right):
    return lax.dot_general(
        left, right, (((1,), (1,)), ((), ())), preferred_element_type=jnp.float32
    )


def rms_norm(values, gain):
    return values * lax.rsqrt(jnp.mean(values * values, axis=-1, keepdims=True) + EPSILON) * gain


def swiglu(hidden_pre, up_pre):
    return jax.nn.silu(hidden_pre) * up_pre


def doc_segments(lengths, tokens):
    order = jnp.arange(lengths.shape[0], dtype=jnp.int32)
    upto = order[None, :] <= order[:, None]
    doc_ends = jnp.sum(jnp.where(upto, lengths[None, :], 0), axis=1)
    positions = jnp.arange(tokens, dtype=jnp.int32)
    return jnp.sum((positions[:, None] >= doc_ends[None, :]).astype(jnp.int32), axis=1)


def shifted(values, offset, fill):
    filler = jnp.full((offset,) + values.shape[1:], fill, values.dtype)
    return jnp.concatenate([filler, values[:-offset]], axis=0)


def short_conv(values, kernel, segment):
    summed = values * kernel[0]
    for offset in range(1, kernel.shape[0]):
        same_doc = (shifted(segment, offset, -1) == segment).astype(values.dtype)
        summed = summed + shifted(values, offset, 0.0) * kernel[offset] * same_doc[:, None]
    return summed


def unit_inverse(lower_part):
    width = lower_part.shape[-1]
    index = jnp.arange(width, dtype=jnp.int32)
    inverse = None
    size = 1
    while size < width:
        rows, columns = index[:, None] // size, index[None, :] // size
        pairs = (rows % 2 == 1) & (columns == rows - 1)
        level = jnp.where(pairs[None], lower_part, 0.0)
        if inverse is None:
            inverse = jnp.eye(width, dtype=lower_part.dtype)[None] - level
        else:
            step = jnp.einsum("hij,hjk->hik", level, inverse, precision=MIX_PRECISION)
            inverse = inverse - jnp.einsum("hij,hjk->hik", inverse, step, precision=MIX_PRECISION)
        size = 2 * size
    return inverse


@jax.custom_vjp
def unit_solve(lower_part, sources):
    return jnp.einsum("hij,hjv->hiv", unit_inverse(lower_part), sources, precision=MIX_PRECISION)


def unit_solve_fwd(lower_part, sources):
    inverse = unit_inverse(lower_part)
    solved = jnp.einsum("hij,hjv->hiv", inverse, sources, precision=MIX_PRECISION)
    return solved, (inverse, solved)


def unit_solve_bwd(saved, d_solved):
    inverse, solved = saved
    d_sources = jnp.einsum("hji,hjv->hiv", inverse, d_solved, precision=MIX_PRECISION)
    d_lower = -jnp.einsum("hiv,hjv->hij", d_sources, solved, precision=MIX_PRECISION)
    return d_lower, d_sources


unit_solve.defvjp(unit_solve_fwd, unit_solve_bwd)


def delta_rule(query_rows, key_matrix, value_rows, decays, strength, segment):
    width = segment.shape[0]
    positions = jnp.arange(width, dtype=jnp.int32)
    same_doc = segment[:, None] == segment[None, :]
    lower_mask = same_doc & (positions[:, None] >= positions[None, :])
    strict_mask = same_doc & (positions[:, None] > positions[None, :])
    cumulative = jnp.einsum(
        "ij,hj->hi", lower_mask.astype(decays.dtype), decays, precision=TOP_PRECISION
    )
    spread = jnp.minimum(cumulative[:, :, None] - cumulative[:, None, :], 0.0)
    ratios = jnp.where(lower_mask[None], jnp.exp(spread), 0.0)
    key_inner = jnp.einsum("hid,hjd->hij", key_matrix, key_matrix, precision=MIX_PRECISION)
    lower_part = jnp.where(strict_mask[None], strength[:, :, None] * ratios * key_inner, 0.0)
    delta_rows = unit_solve(lower_part, strength[:, :, None] * value_rows)
    scores = jnp.einsum("hid,hjd->hij", query_rows, key_matrix, precision=MIX_PRECISION) * ratios
    return jnp.einsum("hij,hjv->hiv", scores, delta_rows, precision=MIX_PRECISION)


def delta_mixer(
    query_proj,
    key_proj,
    value_proj,
    gate_proj,
    decay_proj,
    write_proj,
    conv_query,
    conv_key,
    conv_value,
    decay_log,
    decay_bias,
    out_gain,
    segment,
):
    tokens = query_proj.shape[0]
    head_count = decay_log.shape[0]
    key_dim = query_proj.shape[1] // head_count
    value_dim = value_proj.shape[1] // head_count
    query_rows = jax.nn.silu(short_conv(query_proj, conv_query, segment)).reshape(
        tokens, head_count, key_dim
    )
    key_matrix = jax.nn.silu(short_conv(key_proj, conv_key, segment)).reshape(
        tokens, head_count, key_dim
    )
    value_rows = jax.nn.silu(short_conv(value_proj, conv_value, segment)).reshape(
        tokens, head_count, value_dim
    )
    query_rows = (
        query_rows
        * lax.rsqrt(jnp.sum(query_rows * query_rows, axis=2, keepdims=True) + EPSILON)
        * key_dim ** (-0.5)
    )
    key_matrix = key_matrix * lax.rsqrt(
        jnp.sum(key_matrix * key_matrix, axis=2, keepdims=True) + EPSILON
    )
    decays = -jnp.exp(decay_log) * jax.nn.softplus(decay_proj + decay_bias)
    strength = jax.nn.sigmoid(write_proj)

    readout_rows = delta_rule(
        jnp.swapaxes(query_rows, 0, 1),
        jnp.swapaxes(key_matrix, 0, 1),
        jnp.swapaxes(value_rows, 0, 1),
        decays.T,
        strength.T,
        segment,
    )
    readout_rows = jnp.swapaxes(readout_rows, 0, 1)
    readout_rows = (
        readout_rows
        * lax.rsqrt(jnp.mean(readout_rows * readout_rows, axis=2, keepdims=True) + EPSILON)
        * out_gain
    )
    readout_rows = readout_rows * jax.nn.silu(gate_proj.reshape(tokens, head_count, value_dim))
    return readout_rows.reshape(tokens, head_count * value_dim)


def ring_index(place, size):
    half = (size + 1) // 2
    back = place // half
    return (1 - back) * (2 * place) + back * (2 * (size - 1 - place) + 1)


def ring_place(index, size):
    odd = index % 2
    return (1 - odd) * (index // 2) + odd * (size - 1 - index // 2)


def ring_neighbours(size):
    place = ring_place(lax.axis_index("fsdp"), size)
    return (
        place,
        ring_index((place + 1) % size, size),
        ring_index((place + size - 1) % size, size),
    )


def greet(partners):
    barrier = pltpu.get_barrier_semaphore()
    for partner in partners:
        pl.semaphore_signal(barrier, inc=1, device_id=partner, device_id_type=MESH)
    pl.semaphore_wait(barrier, len(partners))


def column_cuts(columns):
    cut = (columns // (2 * LANES)) * LANES
    return ((0, cut), (cut, columns - cut))


def plane_count():
    return 2 if lax.axis_size("rep") % 4 == 0 else 1


def rep_partners():
    rep = lax.axis_index("rep")
    core, plane = rep % 2, (rep // 2) % 2
    return rep, core, plane, rep + 1 - 2 * core, rep + 2 - 4 * plane


def plane_columns(columns, planes, plane):
    if planes == 1:
        cuts = column_cuts(columns)
        return (*cuts, cuts[0])
    third = ((columns // LANES + 1) // 3) * LANES
    own = pl.multiple_of(plane * third, LANES)
    other = pl.multiple_of((1 - plane) * third, LANES)
    return (own, third), (2 * third, columns - 2 * third), (other, third)


OWN, BOTH, OTHER = range(3)


def gather_kernel(size, planes, count, *refs):
    shards, wholes = refs[:count], refs[count : 2 * count]
    ring_out, ring_in, core_out, core_in, plane_out, plane_in, local_sem = refs[2 * count :]
    place, right, left = ring_neighbours(size)
    me = lax.axis_index("fsdp")
    rep, core, plane, sibling, across = rep_partners()
    partners = [(rep, right), (rep, left), (sibling, me)]
    greet(partners + ([(across, me)] if planes == 2 else []))

    def piece(ref, array, kind, base):
        rows, columns = shards[array].shape
        by_rows = (rows // 2) % SUBLANES == 0
        width = columns if by_rows else columns // 2
        first, part = plane_columns(width, planes, plane)[kind]
        if by_rows:
            base, height = base + core * (rows // 2), rows // 2
        else:
            first, height = pl.multiple_of(core * width + first, LANES), rows
        return ref.at[pl.ds(pl.multiple_of(base, SUBLANES), height), pl.ds(first, part)]

    def placed(array, kind, step):
        shift = step if kind == BOTH else (size - step)
        owner = ring_index((place + shift) % size, size)
        return piece(wholes[array], array, kind, owner * shards[array].shape[0])

    def ring_copy(array, way, step):
        block = placed(array, way, step)
        return pltpu.make_async_remote_copy(
            src_ref=block if step else piece(shards[array], array, way, 0),
            dst_ref=block,
            send_sem=ring_out.at[array, way, step],
            recv_sem=ring_in.at[array, way, step],
            device_id=(rep, right if way == OWN else left),
            device_id_type=MESH,
        )

    def core_copy(array, kind, step):
        block = placed(array, kind, step + 1)
        return pltpu.make_async_remote_copy(
            src_ref=block,
            dst_ref=block,
            send_sem=core_out.at[array, kind, step],
            recv_sem=core_in.at[array, kind, step],
            device_id=(sibling, me),
            device_id_type=MESH,
        )

    def plane_copy(array, step):
        block = placed(array, OWN, step + 1)
        return pltpu.make_async_remote_copy(
            src_ref=block,
            dst_ref=block,
            send_sem=plane_out.at[array, step],
            recv_sem=plane_in.at[array, step],
            device_id=(across, me),
            device_id_type=MESH,
        )

    def own_copy(array):
        rows = shards[array].shape[0]
        start = pl.multiple_of(me * rows, SUBLANES)
        return pltpu.make_async_copy(
            shards[array], wholes[array].at[pl.ds(start, rows)], local_sem.at[array]
        )

    def hand_over(step):
        for array in range(count):
            plane_copy(array, step).wait_recv()
            core_copy(array, OTHER, step).start()

    pairs = [(array, way) for array in range(count) for way in (OWN, BOTH)]
    for array, way in pairs:
        ring_copy(array, way, 0).start()
    for array in range(count):
        own_copy(array).start()
    for step in range(size - 1):
        for array, way in pairs:
            ring_copy(array, way, step).wait_recv()
            if step < size - 2:
                ring_copy(array, way, step + 1).start()
            if way == OWN and planes == 2:
                plane_copy(array, step).start()
            core_copy(array, way, step).start()
        if planes == 2 and step:
            hand_over(step - 1)
    if planes == 2:
        hand_over(size - 2)
    for array in range(count):
        own_copy(array).wait()
    for step in range(size - 1):
        for array, way in pairs:
            ring_copy(array, way, step).wait_send()
            core_copy(array, way, step).wait()
        if planes == 2:
            for array in range(count):
                plane_copy(array, step).wait_send()
                core_copy(array, OTHER, step).wait()


def gathered(weights, kernel_id):
    size, reps = lax.axis_size("fsdp"), lax.axis_size("rep")
    if size < 3 or reps % 2:
        return [lax.all_gather(weight, "fsdp", axis=0, tiled=True) for weight in weights]
    count, planes = len(weights), plane_count()
    anywhere = pl.BlockSpec(memory_space=pl.ANY)
    copies = [(count, 2), (count, 2), (count, 3), (count, 3), (count,), (count,)]
    semaphores = [pltpu.SemaphoreType.DMA((*shape, size - 1)) for shape in copies]
    return pl.pallas_call(
        functools.partial(gather_kernel, size, planes, count),
        out_shape=[
            jax.ShapeDtypeStruct((size * weight.shape[0], weight.shape[1]), weight.dtype)
            for weight in weights
        ],
        in_specs=[anywhere] * count,
        out_specs=[anywhere] * count,
        scratch_shapes=semaphores + [pltpu.SemaphoreType.DMA((count,))],
        compiler_params=pltpu.CompilerParams(collective_id=kernel_id, has_side_effects=True),
        name="gather_rows",
    )(*weights)


def swapped(array, axis_size, bit):
    return lax.ppermute(array, "rep", [(rank, rank ^ bit) for rank in range(axis_size)])


def paired(axis_size):
    return axis_size > 1 and axis_size & (axis_size - 1) == 0


def rounded(values):
    return lax.reduce_precision(values, 8, 7).astype(jnp.bfloat16)


def scatter_kernel(size, count, *refs):
    parts, sums = refs[:count], refs[count : 2 * count]
    slots = refs[2 * count : 4 * count]
    ring_out, ring_in = refs[4 * count :]
    place, right, left = ring_neighbours(size)
    rep = lax.axis_index("rep")
    greet(((rep, right), (rep, left)))

    def part(array, way, step):
        shift = (size - 1 - step) if way == 0 else (1 + step)
        owner = ring_index((place + shift) % size, size)
        first, width = column_cuts(parts[array].shape[2])[way]
        return parts[array].at[owner, :, pl.ds(first, width)]

    def slot(array, way, step):
        return slots[2 * array + way].at[step]

    def ring_copy(array, way, step):
        return pltpu.make_async_remote_copy(
            src_ref=slot(array, way, step - 1) if step else part(array, way, 0),
            dst_ref=slot(array, way, step),
            send_sem=ring_out.at[array, way, step],
            recv_sem=ring_in.at[array, way, step],
            device_id=(rep, right if way == 0 else left),
            device_id_type=MESH,
        )

    pairs = [(array, way) for array in range(count) for way in range(2)]
    for array, way in pairs:
        ring_copy(array, way, 0).start()
    for step in range(size - 1):
        for array, way in pairs:
            ring_copy(array, way, step).wait_recv()
            arrived = slot(array, way, step)
            here = part(array, way, step + 1)
            first, width = column_cuts(parts[array].shape[2])[way]
            total = arrived[...].astype(jnp.float32) + here[...].astype(jnp.float32)
            if step < size - 2:
                arrived[...] = total.astype(arrived.dtype)
                ring_copy(array, way, step + 1).start()
            else:
                sums[array][:, pl.ds(first, width)] = total.astype(sums[array].dtype)
    for step in range(size - 1):
        for array, way in pairs:
            ring_copy(array, way, step).wait_send()


def scattered(parts, kernel_id):
    size = lax.axis_size("fsdp")
    count = len(parts)
    on_chip = pl.BlockSpec(memory_space=pltpu.VMEM)
    slots = [
        pltpu.VMEM((size - 1, part.shape[1], width), part.dtype)
        for part in parts
        for _, width in column_cuts(part.shape[2])
    ]
    semaphores = pltpu.SemaphoreType.DMA((count, 2, size - 1))
    return pl.pallas_call(
        functools.partial(scatter_kernel, size, count),
        out_shape=[jax.ShapeDtypeStruct(part.shape[1:], part.dtype) for part in parts],
        in_specs=[on_chip] * count,
        out_specs=[on_chip] * count,
        scratch_shapes=slots + [semaphores] * 2,
        compiler_params=pltpu.CompilerParams(
            collective_id=kernel_id, has_side_effects=True, vmem_limit_bytes=VMEM_BYTES
        ),
        name="scatter_sums",
    )(*parts)


def core_halves(rows):
    size = lax.axis_size("fsdp")
    tokens, features = rows.shape
    split = rows.reshape(tokens, size, 2, features // (2 * size))
    first = split[:, :, 0].reshape(tokens, features // 2)
    second = split[:, :, 1].reshape(tokens, features // 2)
    even = lax.axis_index("rep") % 2 == 0
    return jnp.where(even, first, second), jnp.where(even, second, first)


def chip_tokens(rows):
    return jnp.concatenate([rows, swapped(rows, lax.axis_size("rep"), 1)], axis=0)


def chip_features(rows):
    own, other = core_halves(rows)
    return jnp.concatenate([own, swapped(other, lax.axis_size("rep"), 1)], axis=0)


def weight_grads(lefts, rights, kernel_id):
    size, reps = lax.axis_size("fsdp"), lax.axis_size("rep")
    if size < 3 or not paired(reps):
        totals = []
        for left, right in zip(lefts, rights):
            part = product_left(left, right).astype(jnp.bfloat16)
            part = lax.psum_scatter(part, "fsdp", scatter_dimension=0, tiled=True)
            totals.append(lax.psum(part, "rep").astype(jnp.float32))
        return totals
    parts = []
    for left, right in zip(lefts, rights):
        spare = -right.shape[1] % LANES
        right = jnp.pad(right, ((0, 0), (0, spare)))
        part = product_left(chip_features(left), chip_tokens(right)).astype(jnp.bfloat16)
        parts.append(part.reshape(size, part.shape[0] // size, part.shape[1]))
    totals = []
    for own, right in zip(scattered(parts, kernel_id), rights):
        own = own[:, : right.shape[1]]
        bit = 2
        while bit < reps:
            own = rounded(own.astype(jnp.float32) + swapped(own, reps, bit).astype(jnp.float32))
            bit = 2 * bit
        other = swapped(own, reps, 1)
        even = lax.axis_index("rep") % 2 == 0
        first, second = jnp.where(even, own, other), jnp.where(even, other, own)
        totals.append(jnp.concatenate([first, second], axis=0).astype(jnp.float32))
    return totals


def total_sum(values):
    for name in ("rep", "fsdp"):
        size = lax.axis_size(name)
        if size & (size - 1):
            values = lax.psum(values, name)
            continue
        bit = 1
        while bit < size:
            pairs = [(rank, rank ^ bit) for rank in range(size)]
            values = values + lax.ppermute(values, name, pairs)
            bit = 2 * bit
    return values


def column_parts(array, widths):
    parts, start = [], 0
    for width in widths:
        parts.append(array[:, start : start + width])
        start = start + width
    return parts


def local(
    block_input,
    cotangent,
    doc_lengths,
    gain_mix,
    w_query,
    w_key,
    w_value,
    w_gate,
    w_decay,
    w_write,
    conv_query,
    conv_key,
    conv_value,
    decay_log,
    decay_bias,
    out_gain,
    w_out,
    gain_ffn,
    w_hidden,
    w_up,
    w_down,
):
    tokens = block_input.shape[0]
    segment = doc_segments(doc_lengths[0], tokens)
    mix_weights = (w_query, w_key, w_value, w_gate, w_decay, w_write)
    mix_widths = [weight.shape[1] for weight in mix_weights]
    ffn_widths = [w_hidden.shape[1], w_up.shape[1]]
    mix_width = sum(mix_widths)
    spare = -mix_width % LANES
    filler = jnp.zeros((w_query.shape[0], spare), w_query.dtype)
    (mixing,) = gathered([jnp.concatenate([*mix_weights, filler], axis=1)], 0)
    outward, feeding, downward = gathered(
        [w_out, jnp.concatenate([w_hidden, w_up], axis=1), w_down], 1
    )
    upstream = cotangent.astype(jnp.bfloat16)

    normed, norm_back = jax.vjp(rms_norm, block_input, gain_mix)
    first_input = normed.astype(jnp.bfloat16)
    projections = column_parts(product(first_input, mixing), mix_widths)

    def mix_local(*operands):
        return delta_mixer(*operands, segment)

    mixed_out, mix_back = jax.vjp(
        mix_local, *projections, conv_query, conv_key, conv_value, decay_log, decay_bias, out_gain
    )
    gated_out = mixed_out.astype(jnp.bfloat16)
    residual = block_input + product(gated_out, outward)
    normed_ffn, norm_ffn_back = jax.vjp(rms_norm, residual, gain_ffn)
    second = normed_ffn.astype(jnp.bfloat16)
    swiglu_out, swiglu_back = jax.vjp(swiglu, *column_parts(product(second, feeding), ffn_widths))
    activation = swiglu_out.astype(jnp.bfloat16)
    block_out = residual + product(activation, downward)
    d_hidden, d_up = swiglu_back(product_right(upstream, downward))
    d_ffn = jnp.concatenate([d_hidden.astype(jnp.bfloat16), d_up.astype(jnp.bfloat16)], axis=1)
    d_second = product_right(d_ffn, feeding)
    grad_down, grad_ffn = weight_grads([activation, second], [upstream, d_ffn], 2)
    d_norm_ffn, grad_gain_ffn = norm_ffn_back(d_second)
    d_residual = cotangent + d_norm_ffn
    upstream_mix = d_residual.astype(jnp.bfloat16)
    mix_grads = mix_back(product_right(upstream_mix, outward))
    d_mix = jnp.concatenate([grad.astype(jnp.bfloat16) for grad in mix_grads[:6]], axis=1)
    grad_out, grad_mix = weight_grads([gated_out, first_input], [upstream_mix, d_mix], 3)
    d_first = product_right(d_mix, mixing[:, :mix_width])
    d_norm, grad_gain_mix = norm_back(d_first)
    input_grad = d_residual + d_norm
    small = (grad_gain_mix, *mix_grads[6:12], grad_gain_ffn)
    flat = jnp.concatenate([grad.reshape(-1) for grad in small])
    flat = total_sum(flat)
    small_totals, start = [], 0
    for grad in small:
        small_totals.append(flat[start : start + grad.size].reshape(grad.shape))
        start = start + grad.size
    mixer_totals = column_parts(grad_mix, mix_widths)
    ffn_totals = column_parts(grad_ffn, ffn_widths)
    return (
        block_out,
        input_grad,
        small_totals[0],
        mixer_totals[0],
        mixer_totals[1],
        mixer_totals[2],
        mixer_totals[3],
        mixer_totals[4],
        mixer_totals[5],
        small_totals[1],
        small_totals[2],
        small_totals[3],
        small_totals[4],
        small_totals[5],
        small_totals[6],
        grad_out,
        small_totals[7],
        ffn_totals[0],
        ffn_totals[1],
        grad_down,
    )


def solution(mesh):
    placed = (
        P(("rep", "fsdp"), None),
        P(("rep", "fsdp"), None),
        P(("rep", "fsdp"), None),
        P(),
        P("fsdp", None),
        P("fsdp", None),
        P("fsdp", None),
        P("fsdp", None),
        P("fsdp", None),
        P("fsdp", None),
        P(),
        P(),
        P(),
        P(),
        P(),
        P(),
        P("fsdp", None),
        P(),
        P("fsdp", None),
        P("fsdp", None),
        P("fsdp", None),
    )
    return jax.shard_map(
        local,
        mesh=mesh,
        in_specs=placed,
        out_specs=(
            P(("rep", "fsdp"), None),
            P(("rep", "fsdp"), None),
            P(),
            P("fsdp", None),
            P("fsdp", None),
            P("fsdp", None),
            P("fsdp", None),
            P("fsdp", None),
            P("fsdp", None),
            P(),
            P(),
            P(),
            P(),
            P(),
            P(),
            P("fsdp", None),
            P(),
            P("fsdp", None),
            P("fsdp", None),
            P("fsdp", None),
        ),
        check_vma=False,
    )
```

```python
import functools

import jax
import jax.numpy as jnp
from jax import lax
from jax.experimental import pallas as pl
from jax.experimental.pallas import tpu as pltpu
from jax.sharding import PartitionSpec as P

EPSILON = 1e-06
TOP_PRECISION = lax.Precision.HIGHEST
MIX_PRECISION = lax.Precision.HIGH
LANES = 128
SUBLANES = 16
VMEM_BYTES = 48 * 1024 * 1024
MESH = pl.DeviceIdType.MESH


def product(left, right):
    return jnp.dot(left, right, preferred_element_type=jnp.float32)


def product_left(left, right):
    return lax.dot_general(
        left, right, (((0,), (0,)), ((), ())), preferred_element_type=jnp.float32
    )


def product_right(left, right):
    return lax.dot_general(
        left, right, (((1,), (1,)), ((), ())), preferred_element_type=jnp.float32
    )


def rms_norm(values, gain):
    return values * lax.rsqrt(jnp.mean(values * values, axis=-1, keepdims=True) + EPSILON) * gain


def swiglu(hidden_pre, up_pre):
    return jax.nn.silu(hidden_pre) * up_pre


def doc_segments(lengths, tokens):
    order = jnp.arange(lengths.shape[0], dtype=jnp.int32)
    upto = order[None, :] <= order[:, None]
    doc_ends = jnp.sum(jnp.where(upto, lengths[None, :], 0), axis=1)
    positions = jnp.arange(tokens, dtype=jnp.int32)
    return jnp.sum((positions[:, None] >= doc_ends[None, :]).astype(jnp.int32), axis=1)


def shifted(values, offset, fill):
    filler = jnp.full((offset,) + values.shape[1:], fill, values.dtype)
    return jnp.concatenate([filler, values[:-offset]], axis=0)


def short_conv(values, kernel, segment):
    summed = values * kernel[0]
    for offset in range(1, kernel.shape[0]):
        same_doc = (shifted(segment, offset, -1) == segment).astype(values.dtype)
        summed = summed + shifted(values, offset, 0.0) * kernel[offset] * same_doc[:, None]
    return summed


def unit_inverse(lower_part):
    width = lower_part.shape[-1]
    index = jnp.arange(width, dtype=jnp.int32)
    inverse = None
    size = 1
    while size < width:
        rows, columns = index[:, None] // size, index[None, :] // size
        pairs = (rows % 2 == 1) & (columns == rows - 1)
        level = jnp.where(pairs[None], lower_part, 0.0)
        if inverse is None:
            inverse = jnp.eye(width, dtype=lower_part.dtype)[None] - level
        else:
            step = jnp.einsum("hij,hjk->hik", level, inverse, precision=MIX_PRECISION)
            inverse = inverse - jnp.einsum("hij,hjk->hik", inverse, step, precision=MIX_PRECISION)
        size = 2 * size
    return inverse


@jax.custom_vjp
def unit_solve(lower_part, sources):
    return jnp.einsum("hij,hjv->hiv", unit_inverse(lower_part), sources, precision=MIX_PRECISION)


def unit_solve_fwd(lower_part, sources):
    inverse = unit_inverse(lower_part)
    solved = jnp.einsum("hij,hjv->hiv", inverse, sources, precision=MIX_PRECISION)
    return solved, (inverse, solved)


def unit_solve_bwd(saved, d_solved):
    inverse, solved = saved
    d_sources = jnp.einsum("hji,hjv->hiv", inverse, d_solved, precision=MIX_PRECISION)
    d_lower = -jnp.einsum("hiv,hjv->hij", d_sources, solved, precision=MIX_PRECISION)
    return d_lower, d_sources


unit_solve.defvjp(unit_solve_fwd, unit_solve_bwd)


def delta_rule(query_rows, key_matrix, value_rows, decays, strength, segment):
    width = segment.shape[0]
    positions = jnp.arange(width, dtype=jnp.int32)
    same_doc = segment[:, None] == segment[None, :]
    lower_mask = same_doc & (positions[:, None] >= positions[None, :])
    strict_mask = same_doc & (positions[:, None] > positions[None, :])
    cumulative = jnp.einsum(
        "ij,hj->hi", lower_mask.astype(decays.dtype), decays, precision=TOP_PRECISION
    )
    spread = jnp.minimum(cumulative[:, :, None] - cumulative[:, None, :], 0.0)
    ratios = jnp.where(lower_mask[None], jnp.exp(spread), 0.0)
    key_inner = jnp.einsum("hid,hjd->hij", key_matrix, key_matrix, precision=MIX_PRECISION)
    lower_part = jnp.where(strict_mask[None], strength[:, :, None] * ratios * key_inner, 0.0)
    delta_rows = unit_solve(lower_part, strength[:, :, None] * value_rows)
    scores = jnp.einsum("hid,hjd->hij", query_rows, key_matrix, precision=MIX_PRECISION) * ratios
    return jnp.einsum("hij,hjv->hiv", scores, delta_rows, precision=MIX_PRECISION)


def conv_rows(proj, kernel, segment, head_count):
    rows = jax.nn.silu(short_conv(proj, kernel, segment))
    return jnp.swapaxes(rows.reshape(proj.shape[0], head_count, -1), 0, 1)


def unit_rows(proj, kernel, segment, head_count):
    rows = conv_rows(proj, kernel, segment, head_count)
    return rows * lax.rsqrt(jnp.sum(rows * rows, axis=2, keepdims=True) + EPSILON)


def query_rows_of(proj, kernel, segment, head_count):
    rows = unit_rows(proj, kernel, segment, head_count)
    return rows * rows.shape[2] ** (-0.5)


def head_gates(decay_proj, write_proj, decay_log, decay_bias):
    decays = -jnp.exp(decay_log) * jax.nn.softplus(decay_proj + decay_bias)
    return decays.T, jax.nn.sigmoid(write_proj).T


def gated_norm(readout_rows, gate_proj, out_gain):
    tokens = gate_proj.shape[0]
    rows = jnp.swapaxes(readout_rows, 0, 1)
    rows = rows * lax.rsqrt(jnp.mean(rows * rows, axis=2, keepdims=True) + EPSILON) * out_gain
    return (rows * jax.nn.silu(gate_proj.reshape(rows.shape))).reshape(tokens, -1)


def ring_index(place, size):
    half = (size + 1) // 2
    back = place // half
    return (1 - back) * (2 * place) + back * (2 * (size - 1 - place) + 1)


def ring_place(index, size):
    odd = index % 2
    return (1 - odd) * (index // 2) + odd * (size - 1 - index // 2)


def ring_neighbours(size):
    place = ring_place(lax.axis_index("fsdp"), size)
    return (
        place,
        ring_index((place + 1) % size, size),
        ring_index((place + size - 1) % size, size),
    )


def greet(partners):
    barrier = pltpu.get_barrier_semaphore()
    for partner in partners:
        pl.semaphore_signal(barrier, inc=1, device_id=partner, device_id_type=MESH)
    pl.semaphore_wait(barrier, len(partners))


def column_cuts(columns):
    cut = (columns // (2 * LANES)) * LANES
    return ((0, cut), (cut, columns - cut))


def plane_count():
    return 2 if lax.axis_size("rep") % 4 == 0 else 1


def rep_partners():
    rep = lax.axis_index("rep")
    core, plane = rep % 2, (rep // 2) % 2
    return rep, core, plane, rep + 1 - 2 * core, rep + 2 - 4 * plane


def plane_columns(columns, planes, plane):
    if planes == 1:
        cuts = column_cuts(columns)
        return (*cuts, cuts[0])
    third = ((columns // LANES + 1) // 3) * LANES
    own = pl.multiple_of(plane * third, LANES)
    other = pl.multiple_of((1 - plane) * third, LANES)
    return (own, third), (2 * third, columns - 2 * third), (other, third)


OWN, BOTH, OTHER = range(3)


def gather_kernel(size, planes, count, *refs):
    shards, wholes = refs[:count], refs[count : 2 * count]
    ring_out, ring_in, core_out, core_in, plane_out, plane_in, local_sem = refs[2 * count :]
    place, right, left = ring_neighbours(size)
    me = lax.axis_index("fsdp")
    rep, core, plane, sibling, across = rep_partners()
    partners = [(rep, right), (rep, left), (sibling, me)]
    greet(partners + ([(across, me)] if planes == 2 else []))

    def piece(ref, array, kind, base):
        rows, columns = shards[array].shape
        by_rows = (rows // 2) % SUBLANES == 0
        width = columns if by_rows else columns // 2
        first, part = plane_columns(width, planes, plane)[kind]
        if by_rows:
            base, height = base + core * (rows // 2), rows // 2
        else:
            first, height = pl.multiple_of(core * width + first, LANES), rows
        return ref.at[pl.ds(pl.multiple_of(base, SUBLANES), height), pl.ds(first, part)]

    def placed(array, kind, step):
        shift = step if kind == BOTH else (size - step)
        owner = ring_index((place + shift) % size, size)
        return piece(wholes[array], array, kind, owner * shards[array].shape[0])

    def ring_copy(array, way, step):
        block = placed(array, way, step)
        return pltpu.make_async_remote_copy(
            src_ref=block if step else piece(shards[array], array, way, 0),
            dst_ref=block,
            send_sem=ring_out.at[array, way, step],
            recv_sem=ring_in.at[array, way, step],
            device_id=(rep, right if way == OWN else left),
            device_id_type=MESH,
        )

    def core_copy(array, kind, step):
        block = placed(array, kind, step + 1)
        return pltpu.make_async_remote_copy(
            src_ref=block,
            dst_ref=block,
            send_sem=core_out.at[array, kind, step],
            recv_sem=core_in.at[array, kind, step],
            device_id=(sibling, me),
            device_id_type=MESH,
        )

    def plane_copy(array, step):
        block = placed(array, OWN, step + 1)
        return pltpu.make_async_remote_copy(
            src_ref=block,
            dst_ref=block,
            send_sem=plane_out.at[array, step],
            recv_sem=plane_in.at[array, step],
            device_id=(across, me),
            device_id_type=MESH,
        )

    def own_copy(array):
        rows = shards[array].shape[0]
        start = pl.multiple_of(me * rows, SUBLANES)
        return pltpu.make_async_copy(
            shards[array], wholes[array].at[pl.ds(start, rows)], local_sem.at[array]
        )

    def hand_over(step):
        for array in range(count):
            plane_copy(array, step).wait_recv()
            core_copy(array, OTHER, step).start()

    pairs = [(array, way) for array in range(count) for way in (OWN, BOTH)]
    for array, way in pairs:
        ring_copy(array, way, 0).start()
    for array in range(count):
        own_copy(array).start()
    for step in range(size - 1):
        for array, way in pairs:
            ring_copy(array, way, step).wait_recv()
            if step < size - 2:
                ring_copy(array, way, step + 1).start()
            if way == OWN and planes == 2:
                plane_copy(array, step).start()
            core_copy(array, way, step).start()
        if planes == 2 and step:
            hand_over(step - 1)
    if planes == 2:
        hand_over(size - 2)
    for array in range(count):
        own_copy(array).wait()
    for step in range(size - 1):
        for array, way in pairs:
            ring_copy(array, way, step).wait_send()
            core_copy(array, way, step).wait()
        if planes == 2:
            for array in range(count):
                plane_copy(array, step).wait_send()
                core_copy(array, OTHER, step).wait()


def gathered(weights, kernel_id):
    size, reps = lax.axis_size("fsdp"), lax.axis_size("rep")
    if size < 3 or reps % 2:
        return [lax.all_gather(weight, "fsdp", axis=0, tiled=True) for weight in weights]
    count, planes = len(weights), plane_count()
    anywhere = pl.BlockSpec(memory_space=pl.ANY)
    copies = [(count, 2), (count, 2), (count, 3), (count, 3), (count,), (count,)]
    semaphores = [pltpu.SemaphoreType.DMA((*shape, size - 1)) for shape in copies]
    return pl.pallas_call(
        functools.partial(gather_kernel, size, planes, count),
        out_shape=[
            jax.ShapeDtypeStruct((size * weight.shape[0], weight.shape[1]), weight.dtype)
            for weight in weights
        ],
        in_specs=[anywhere] * count,
        out_specs=[anywhere] * count,
        scratch_shapes=semaphores + [pltpu.SemaphoreType.DMA((count,))],
        compiler_params=pltpu.CompilerParams(collective_id=kernel_id, has_side_effects=True),
        name="gather_rows",
    )(*weights)


def swapped(array, axis_size, bit):
    return lax.ppermute(array, "rep", [(rank, rank ^ bit) for rank in range(axis_size)])


def paired(axis_size):
    return axis_size > 1 and axis_size & (axis_size - 1) == 0


def rounded(values):
    return lax.reduce_precision(values, 8, 7).astype(jnp.bfloat16)


def scatter_kernel(size, count, *refs):
    parts, sums = refs[:count], refs[count : 2 * count]
    slots = refs[2 * count : 4 * count]
    ring_out, ring_in = refs[4 * count :]
    place, right, left = ring_neighbours(size)
    rep = lax.axis_index("rep")
    greet(((rep, right), (rep, left)))

    def part(array, way, step):
        shift = (size - 1 - step) if way == 0 else (1 + step)
        owner = ring_index((place + shift) % size, size)
        first, width = column_cuts(parts[array].shape[2])[way]
        return parts[array].at[owner, :, pl.ds(first, width)]

    def slot(array, way, step):
        return slots[2 * array + way].at[step]

    def ring_copy(array, way, step):
        return pltpu.make_async_remote_copy(
            src_ref=slot(array, way, step - 1) if step else part(array, way, 0),
            dst_ref=slot(array, way, step),
            send_sem=ring_out.at[array, way, step],
            recv_sem=ring_in.at[array, way, step],
            device_id=(rep, right if way == 0 else left),
            device_id_type=MESH,
        )

    pairs = [(array, way) for array in range(count) for way in range(2)]
    for array, way in pairs:
        ring_copy(array, way, 0).start()
    for step in range(size - 1):
        for array, way in pairs:
            ring_copy(array, way, step).wait_recv()
            arrived = slot(array, way, step)
            here = part(array, way, step + 1)
            first, width = column_cuts(parts[array].shape[2])[way]
            total = arrived[...].astype(jnp.float32) + here[...].astype(jnp.float32)
            if step < size - 2:
                arrived[...] = total.astype(arrived.dtype)
                ring_copy(array, way, step + 1).start()
            else:
                sums[array][:, pl.ds(first, width)] = total.astype(sums[array].dtype)
    for step in range(size - 1):
        for array, way in pairs:
            ring_copy(array, way, step).wait_send()


def scattered(parts, kernel_id):
    size = lax.axis_size("fsdp")
    if not ringed():
        return [lax.psum_scatter(part, "fsdp", scatter_dimension=0, tiled=True) for part in parts]
    count = len(parts)
    on_chip = pl.BlockSpec(memory_space=pltpu.VMEM)
    slots = [
        pltpu.VMEM((size - 1, part.shape[1], width), part.dtype)
        for part in parts
        for _, width in column_cuts(part.shape[2])
    ]
    semaphores = pltpu.SemaphoreType.DMA((count, 2, size - 1))
    return pl.pallas_call(
        functools.partial(scatter_kernel, size, count),
        out_shape=[jax.ShapeDtypeStruct(part.shape[1:], part.dtype) for part in parts],
        in_specs=[on_chip] * count,
        out_specs=[on_chip] * count,
        scratch_shapes=slots + [semaphores] * 2,
        compiler_params=pltpu.CompilerParams(
            collective_id=kernel_id, has_side_effects=True, vmem_limit_bytes=VMEM_BYTES
        ),
        name="scatter_sums",
    )(*parts)


def core_halves(rows):
    size = lax.axis_size("fsdp")
    tokens, features = rows.shape
    split = rows.reshape(tokens, size, 2, features // (2 * size))
    first = split[:, :, 0].reshape(tokens, features // 2)
    second = split[:, :, 1].reshape(tokens, features // 2)
    even = lax.axis_index("rep") % 2 == 0
    return jnp.where(even, first, second), jnp.where(even, second, first)


def chip_rows(mine, theirs):
    return jnp.concatenate([mine, swapped(theirs, lax.axis_size("rep"), 1)], axis=0)


def ringed():
    return lax.axis_size("fsdp") > 2 and paired(lax.axis_size("rep"))


def chip_parts(pairs):
    size = lax.axis_size("fsdp")
    if not ringed():
        return [product_left(left, right).astype(jnp.bfloat16) for left, right in pairs]
    lefts, rights, parts = {}, {}, []
    for left, right in pairs:
        if id(left) not in lefts:
            lefts[id(left)] = chip_rows(*core_halves(left))
        if id(right) not in rights:
            rights[id(right)] = chip_rows(right, right)
        part = product_left(lefts[id(left)], rights[id(right)]).astype(jnp.bfloat16)
        parts.append(part.reshape(size, part.shape[0] // size, part.shape[1]))
    return parts


def ring_pairs(size, way):
    hop = 1 if way == 0 else size - 1
    return [
        (ring_index(place, size), ring_index((place + hop) % size, size)) for place in range(size)
    ]


def part_block(part, way, step):
    size = lax.axis_size("fsdp")
    place = ring_place(lax.axis_index("fsdp"), size)
    shift = (size - 1 - step) if way == 0 else (1 + step)
    owner = ring_index((place + shift) % size, size)
    first, width = column_cuts(part.shape[2])[way]
    return lax.dynamic_index_in_dim(part[:, :, first : first + width], owner, keepdims=False)


def beside(parts, stages):
    results, value = [], None
    if not ringed():
        for stage in stages:
            value = stage(value)
        summed = [lax.psum_scatter(part, "fsdp", scatter_dimension=0, tiled=True) for part in parts]
        return summed, value
    size = lax.axis_size("fsdp")
    chains = [(part, way) for part in parts for way in range(2)]
    held = [part_block(part, way, 0) for part, way in chains]
    done = 0
    for index, stage in enumerate(stages):
        upto = ((index + 1) * (size - 1)) // len(stages)
        moved = held
        for step in range(done, upto):
            moved = [
                lax.ppermute(rows, "fsdp", ring_pairs(size, way))
                for rows, (part, way) in zip(moved, chains)
            ]
            if step + 1 < upto:
                moved = added(moved, chains, step + 1)
        value = stage(value)
        moved, value = lax.optimization_barrier((moved, value))
        held = added(moved, chains, upto) if upto > done else moved
        done = upto
    return [jnp.concatenate(held[2 * at : 2 * at + 2], axis=1) for at in range(len(parts))], value


def added(moved, chains, step):
    return [
        rounded(rows.astype(jnp.float32) + part_block(part, way, step).astype(jnp.float32))
        for rows, (part, way) in zip(moved, chains)
    ]


def rep_total(own):
    reps = lax.axis_size("rep")
    if not ringed():
        return lax.psum(own, "rep").astype(jnp.float32)
    bit = 2
    while bit < reps:
        own = rounded(own.astype(jnp.float32) + swapped(own, reps, bit).astype(jnp.float32))
        bit = 2 * bit
    other = swapped(own, reps, 1)
    even = lax.axis_index("rep") % 2 == 0
    first, second = jnp.where(even, own, other), jnp.where(even, other, own)
    return jnp.concatenate([first, second], axis=0).astype(jnp.float32)


def total_sum(values):
    for name in ("rep", "fsdp"):
        size = lax.axis_size(name)
        if size & (size - 1):
            values = lax.psum(values, name)
            continue
        bit = 1
        while bit < size:
            pairs = [(rank, rank ^ bit) for rank in range(size)]
            values = values + lax.ppermute(values, name, pairs)
            bit = 2 * bit
    return values


def column_parts(array, widths):
    parts, start = [], 0
    for width in widths:
        parts.append(array[:, start : start + width])
        start = start + width
    return parts


def local(
    block_input,
    cotangent,
    doc_lengths,
    gain_mix,
    w_query,
    w_key,
    w_value,
    w_gate,
    w_decay,
    w_write,
    conv_query,
    conv_key,
    conv_value,
    decay_log,
    decay_bias,
    out_gain,
    w_out,
    gain_ffn,
    w_hidden,
    w_up,
    w_down,
):
    tokens = block_input.shape[0]
    segment = doc_segments(doc_lengths[0], tokens)
    head_count = decay_log.shape[0]
    narrow_widths = [w_query.shape[1], head_count, head_count]
    spare = -sum(narrow_widths) % LANES
    narrow = jnp.concatenate([w_query, w_decay, w_write], axis=1)
    narrow = jnp.pad(narrow, ((0, 0), (0, spare)))
    mixing = gathered([narrow, w_key, w_value, w_gate], 0)
    outward, hidden, up, downward = gathered([w_out, w_hidden, w_up, w_down], 1)
    upstream = cotangent.astype(jnp.bfloat16)

    normed, norm_back = jax.vjp(rms_norm, block_input, gain_mix)
    first_input = normed.astype(jnp.bfloat16)
    narrow_proj, key_proj, value_proj, gate_proj = [
        product(first_input, weight) for weight in mixing
    ]
    query_proj, decay_proj, write_proj = column_parts(narrow_proj, narrow_widths)

    def rows_of(maker):
        return lambda proj, kernel: maker(proj, kernel, segment, head_count)

    queries, query_back = jax.vjp(rows_of(query_rows_of), query_proj, conv_query)
    key_rows, key_back = jax.vjp(rows_of(unit_rows), key_proj, conv_key)
    value_rows, value_back = jax.vjp(rows_of(conv_rows), value_proj, conv_value)
    (decays, strength), gates_back = jax.vjp(
        head_gates, decay_proj, write_proj, decay_log, decay_bias
    )
    readout, readout_back = jax.vjp(
        lambda *operands: delta_rule(*operands, segment),
        queries,
        key_rows,
        value_rows,
        decays,
        strength,
    )
    mixed_out, mixed_back = jax.vjp(gated_norm, readout, gate_proj, out_gain)
    gated_out = mixed_out.astype(jnp.bfloat16)
    residual = block_input + product(gated_out, outward)
    normed_ffn, norm_ffn_back = jax.vjp(rms_norm, residual, gain_ffn)
    second = normed_ffn.astype(jnp.bfloat16)
    swiglu_out, swiglu_back = jax.vjp(swiglu, product(second, hidden), product(second, up))
    activation = swiglu_out.astype(jnp.bfloat16)
    block_out = residual + product(activation, downward)
    d_hidden, d_up = [
        grad.astype(jnp.bfloat16) for grad in swiglu_back(product_right(upstream, downward))
    ]
    d_second = product_right(d_hidden, hidden) + product_right(d_up, up)
    ffn_parts = chip_parts([(activation, upstream), (second, d_hidden), (second, d_up)])
    d_norm_ffn, grad_gain_ffn = norm_ffn_back(d_second)
    d_residual = cotangent + d_norm_ffn
    upstream_mix = d_residual.astype(jnp.bfloat16)
    d_mixed = product_right(upstream_mix, outward)
    ffn_parts, d_mixed = lax.optimization_barrier((ffn_parts, d_mixed))
    small = {}

    def output_stage(_):
        d_readout, d_gate, small["out_gain"] = mixed_back(d_mixed)
        return d_readout, d_gate.astype(jnp.bfloat16)

    def recurrence_stage(value):
        d_readout, d_gate = value
        return readout_back(d_readout), d_gate

    def value_stage(value):
        (d_queries, d_keys, d_values, *d_gates), d_gate = value
        d_value, grad_conv = value_back(d_values)
        return d_queries, d_keys, d_gates, d_value.astype(jnp.bfloat16), grad_conv, d_gate

    def narrow_stage(value):
        d_queries, d_keys, d_gates, d_value, grad_conv_value, d_gate = value
        d_query, grad_conv_query = query_back(d_queries)
        d_key, grad_conv_key = key_back(d_keys)
        d_decay, d_write, grad_log, grad_bias = gates_back(tuple(d_gates))
        d_narrow = jnp.concatenate([d_query, d_decay, d_write], axis=1).astype(jnp.bfloat16)
        d_narrow = jnp.pad(d_narrow, ((0, 0), (0, spare)))
        d_mix = (d_narrow, d_key.astype(jnp.bfloat16), d_value, d_gate)
        grads = (grad_conv_query, grad_conv_key, grad_conv_value, grad_log, grad_bias)
        return d_mix, grads

    def input_stage(value):
        d_mix, grads = value
        d_first = sum(product_right(rows, weight) for rows, weight in zip(d_mix, mixing))
        d_norm, grad_gain = norm_back(d_first)
        return d_mix, grads, d_residual + d_norm, grad_gain

    def parts_stage(value):
        d_mix, grads, input_rows, grad_gain = value
        parts = chip_parts([(gated_out, upstream_mix), *((first_input, rows) for rows in d_mix)])
        return parts, grads, input_rows, grad_gain

    def last_stage(value):
        parts, *others = value
        return scattered(parts, 2), *others

    stages = [output_stage, recurrence_stage, value_stage, narrow_stage, input_stage, parts_stage]
    ffn_sums, (mix_sums, grads, input_grad, grad_gain_mix) = beside(
        ffn_parts, stages + [last_stage]
    )
    grad_down, grad_hidden, grad_up = [rep_total(rows) for rows in ffn_sums]
    grad_out, grad_narrow, grad_key, grad_value, grad_gate = [rep_total(rows) for rows in mix_sums]
    grad_query, grad_decay, grad_write = column_parts(grad_narrow, narrow_widths)
    small = (grad_gain_mix, *grads, small["out_gain"], grad_gain_ffn)
    flat = jnp.concatenate([grad.reshape(-1) for grad in small])
    flat = total_sum(flat)
    small_totals, start = [], 0
    for grad in small:
        small_totals.append(flat[start : start + grad.size].reshape(grad.shape))
        start = start + grad.size
    return (
        block_out,
        input_grad,
        small_totals[0],
        grad_query,
        grad_key,
        grad_value,
        grad_gate,
        grad_decay,
        grad_write,
        *small_totals[1:7],
        grad_out,
        small_totals[7],
        grad_hidden,
        grad_up,
        grad_down,
    )


def solution(mesh):
    placed = (
        P(("rep", "fsdp"), None),
        P(("rep", "fsdp"), None),
        P(("rep", "fsdp"), None),
        P(),
        P("fsdp", None),
        P("fsdp", None),
        P("fsdp", None),
        P("fsdp", None),
        P("fsdp", None),
        P("fsdp", None),
        P(),
        P(),
        P(),
        P(),
        P(),
        P(),
        P("fsdp", None),
        P(),
        P("fsdp", None),
        P("fsdp", None),
        P("fsdp", None),
    )
    return jax.shard_map(
        local,
        mesh=mesh,
        in_specs=placed,
        out_specs=(
            P(("rep", "fsdp"), None),
            P(("rep", "fsdp"), None),
            P(),
            P("fsdp", None),
            P("fsdp", None),
            P("fsdp", None),
            P("fsdp", None),
            P("fsdp", None),
            P("fsdp", None),
            P(),
            P(),
            P(),
            P(),
            P(),
            P(),
            P("fsdp", None),
            P(),
            P("fsdp", None),
            P("fsdp", None),
            P("fsdp", None),
        ),
        check_vma=False,
    )
```

```python
import functools

import jax
import jax.numpy as jnp
from jax import lax
from jax.experimental import pallas as pl
from jax.experimental.pallas import tpu as pltpu
from jax.sharding import PartitionSpec as P

EPSILON = 1e-06
TOP_PRECISION = lax.Precision.HIGHEST
MIX_PRECISION = lax.Precision.HIGH
LANES = 128
SUBLANES = 16
LATE_STEPS = 3
VMEM_BYTES = 48 * 1024 * 1024
MESH = pl.DeviceIdType.MESH


def product(left, right):
    return jnp.dot(left, right, preferred_element_type=jnp.float32)


def product_left(left, right):
    return lax.dot_general(
        left, right, (((0,), (0,)), ((), ())), preferred_element_type=jnp.float32
    )


def product_right(left, right):
    return lax.dot_general(
        left, right, (((1,), (1,)), ((), ())), preferred_element_type=jnp.float32
    )


def rms_norm(values, gain):
    return values * lax.rsqrt(jnp.mean(values * values, axis=-1, keepdims=True) + EPSILON) * gain


def swiglu(hidden_pre, up_pre):
    return jax.nn.silu(hidden_pre) * up_pre


def doc_segments(lengths, tokens):
    order = jnp.arange(lengths.shape[0], dtype=jnp.int32)
    upto = order[None, :] <= order[:, None]
    doc_ends = jnp.sum(jnp.where(upto, lengths[None, :], 0), axis=1)
    positions = jnp.arange(tokens, dtype=jnp.int32)
    return jnp.sum((positions[:, None] >= doc_ends[None, :]).astype(jnp.int32), axis=1)


def shifted(values, offset, fill):
    filler = jnp.full((offset,) + values.shape[1:], fill, values.dtype)
    return jnp.concatenate([filler, values[:-offset]], axis=0)


def short_conv(values, kernel, segment):
    summed = values * kernel[0]
    for offset in range(1, kernel.shape[0]):
        same_doc = (shifted(segment, offset, -1) == segment).astype(values.dtype)
        summed = summed + shifted(values, offset, 0.0) * kernel[offset] * same_doc[:, None]
    return summed


def unit_inverse(lower_part):
    width = lower_part.shape[-1]
    index = jnp.arange(width, dtype=jnp.int32)
    inverse = None
    size = 1
    while size < width:
        rows, columns = index[:, None] // size, index[None, :] // size
        pairs = (rows % 2 == 1) & (columns == rows - 1)
        level = jnp.where(pairs[None], lower_part, 0.0)
        if inverse is None:
            inverse = jnp.eye(width, dtype=lower_part.dtype)[None] - level
        else:
            step = jnp.einsum("hij,hjk->hik", level, inverse, precision=MIX_PRECISION)
            inverse = inverse - jnp.einsum("hij,hjk->hik", inverse, step, precision=MIX_PRECISION)
        size = 2 * size
    return inverse


@jax.custom_vjp
def unit_solve(lower_part, sources):
    return jnp.einsum("hij,hjv->hiv", unit_inverse(lower_part), sources, precision=MIX_PRECISION)


def unit_solve_fwd(lower_part, sources):
    inverse = unit_inverse(lower_part)
    solved = jnp.einsum("hij,hjv->hiv", inverse, sources, precision=MIX_PRECISION)
    return solved, (inverse, solved)


def unit_solve_bwd(saved, d_solved):
    inverse, solved = saved
    d_sources = jnp.einsum("hji,hjv->hiv", inverse, d_solved, precision=MIX_PRECISION)
    d_lower = -jnp.einsum("hiv,hjv->hij", d_sources, solved, precision=MIX_PRECISION)
    return d_lower, d_sources


unit_solve.defvjp(unit_solve_fwd, unit_solve_bwd)


def delta_rule(query_rows, key_matrix, value_rows, decays, strength, segment):
    width = segment.shape[0]
    positions = jnp.arange(width, dtype=jnp.int32)
    same_doc = segment[:, None] == segment[None, :]
    lower_mask = same_doc & (positions[:, None] >= positions[None, :])
    strict_mask = same_doc & (positions[:, None] > positions[None, :])
    cumulative = jnp.einsum(
        "ij,hj->hi", lower_mask.astype(decays.dtype), decays, precision=TOP_PRECISION
    )
    spread = jnp.minimum(cumulative[:, :, None] - cumulative[:, None, :], 0.0)
    ratios = jnp.where(lower_mask[None], jnp.exp(spread), 0.0)
    key_inner = jnp.einsum("hid,hjd->hij", key_matrix, key_matrix, precision=MIX_PRECISION)
    lower_part = jnp.where(strict_mask[None], strength[:, :, None] * ratios * key_inner, 0.0)
    delta_rows = unit_solve(lower_part, strength[:, :, None] * value_rows)
    scores = jnp.einsum("hid,hjd->hij", query_rows, key_matrix, precision=MIX_PRECISION) * ratios
    return jnp.einsum("hij,hjv->hiv", scores, delta_rows, precision=MIX_PRECISION)


def conv_rows(proj, kernel, segment, head_count):
    rows = jax.nn.silu(short_conv(proj, kernel, segment))
    return jnp.swapaxes(rows.reshape(proj.shape[0], head_count, -1), 0, 1)


def unit_rows(proj, kernel, segment, head_count):
    rows = conv_rows(proj, kernel, segment, head_count)
    return rows * lax.rsqrt(jnp.sum(rows * rows, axis=2, keepdims=True) + EPSILON)


def query_rows_of(proj, kernel, segment, head_count):
    rows = unit_rows(proj, kernel, segment, head_count)
    return rows * rows.shape[2] ** (-0.5)


def head_gates(decay_proj, write_proj, decay_log, decay_bias):
    decays = -jnp.exp(decay_log) * jax.nn.softplus(decay_proj + decay_bias)
    return decays.T, jax.nn.sigmoid(write_proj).T


def gated_norm(readout_rows, gate_proj, out_gain):
    tokens = gate_proj.shape[0]
    rows = jnp.swapaxes(readout_rows, 0, 1)
    rows = rows * lax.rsqrt(jnp.mean(rows * rows, axis=2, keepdims=True) + EPSILON) * out_gain
    return (rows * jax.nn.silu(gate_proj.reshape(rows.shape))).reshape(tokens, -1)


def ring_index(place, size):
    half = (size + 1) // 2
    back = place // half
    return (1 - back) * (2 * place) + back * (2 * (size - 1 - place) + 1)


def ring_place(index, size):
    odd = index % 2
    return (1 - odd) * (index // 2) + odd * (size - 1 - index // 2)


def ring_neighbours(size):
    place = ring_place(lax.axis_index("fsdp"), size)
    return (
        place,
        ring_index((place + 1) % size, size),
        ring_index((place + size - 1) % size, size),
    )


def greet(partners):
    barrier = pltpu.get_barrier_semaphore()
    for partner in partners:
        pl.semaphore_signal(barrier, inc=1, device_id=partner, device_id_type=MESH)
    pl.semaphore_wait(barrier, len(partners))


def column_cuts(columns):
    cut = (columns // (2 * LANES)) * LANES
    return ((0, cut), (cut, columns - cut))


def plane_count():
    return 2 if lax.axis_size("rep") % 4 == 0 else 1


def rep_partners():
    rep = lax.axis_index("rep")
    core, plane = rep % 2, (rep // 2) % 2
    return rep, core, plane, rep + 1 - 2 * core, rep + 2 - 4 * plane


def plane_columns(columns, planes, plane):
    if planes == 1:
        cuts = column_cuts(columns)
        return (*cuts, cuts[0])
    third = ((columns // LANES + 1) // 3) * LANES
    own = pl.multiple_of(plane * third, LANES)
    other = pl.multiple_of((1 - plane) * third, LANES)
    return (own, third), (2 * third, columns - 2 * third), (other, third)


OWN, BOTH, OTHER = range(3)


def gather_kernel(size, planes, count, *refs):
    shards, wholes = refs[:count], refs[count : 2 * count]
    ring_out, ring_in, core_out, core_in, plane_out, plane_in, local_sem = refs[2 * count :]
    place, right, left = ring_neighbours(size)
    me = lax.axis_index("fsdp")
    rep, core, plane, sibling, across = rep_partners()
    partners = [(rep, right), (rep, left), (sibling, me)]
    greet(partners + ([(across, me)] if planes == 2 else []))

    def piece(ref, array, kind, base):
        rows, columns = shards[array].shape
        by_rows = (rows // 2) % SUBLANES == 0
        width = columns if by_rows else columns // 2
        first, part = plane_columns(width, planes, plane)[kind]
        if by_rows:
            base, height = base + core * (rows // 2), rows // 2
        else:
            first, height = pl.multiple_of(core * width + first, LANES), rows
        return ref.at[pl.ds(pl.multiple_of(base, SUBLANES), height), pl.ds(first, part)]

    def placed(array, kind, step):
        shift = step if kind == BOTH else (size - step)
        owner = ring_index((place + shift) % size, size)
        return piece(wholes[array], array, kind, owner * shards[array].shape[0])

    def ring_copy(array, way, step):
        block = placed(array, way, step)
        return pltpu.make_async_remote_copy(
            src_ref=block if step else piece(shards[array], array, way, 0),
            dst_ref=block,
            send_sem=ring_out.at[array, way, step],
            recv_sem=ring_in.at[array, way, step],
            device_id=(rep, right if way == OWN else left),
            device_id_type=MESH,
        )

    def core_copy(array, kind, step):
        block = placed(array, kind, step + 1)
        return pltpu.make_async_remote_copy(
            src_ref=block,
            dst_ref=block,
            send_sem=core_out.at[array, kind, step],
            recv_sem=core_in.at[array, kind, step],
            device_id=(sibling, me),
            device_id_type=MESH,
        )

    def plane_copy(array, step):
        block = placed(array, OWN, step + 1)
        return pltpu.make_async_remote_copy(
            src_ref=block,
            dst_ref=block,
            send_sem=plane_out.at[array, step],
            recv_sem=plane_in.at[array, step],
            device_id=(across, me),
            device_id_type=MESH,
        )

    def own_copy(array):
        rows = shards[array].shape[0]
        start = pl.multiple_of(me * rows, SUBLANES)
        return pltpu.make_async_copy(
            shards[array], wholes[array].at[pl.ds(start, rows)], local_sem.at[array]
        )

    def hand_over(step):
        for array in range(count):
            plane_copy(array, step).wait_recv()
            core_copy(array, OTHER, step).start()

    pairs = [(array, way) for array in range(count) for way in (OWN, BOTH)]
    for array, way in pairs:
        ring_copy(array, way, 0).start()
    for array in range(count):
        own_copy(array).start()
    for step in range(size - 1):
        for array, way in pairs:
            ring_copy(array, way, step).wait_recv()
            if step < size - 2:
                ring_copy(array, way, step + 1).start()
            if way == OWN and planes == 2:
                plane_copy(array, step).start()
            core_copy(array, way, step).start()
        if planes == 2 and step:
            hand_over(step - 1)
    if planes == 2:
        hand_over(size - 2)
    for array in range(count):
        own_copy(array).wait()
    for step in range(size - 1):
        for array, way in pairs:
            ring_copy(array, way, step).wait_send()
            core_copy(array, way, step).wait()
        if planes == 2:
            for array in range(count):
                plane_copy(array, step).wait_send()
                core_copy(array, OTHER, step).wait()


def gathered(weights, kernel_id):
    size, reps = lax.axis_size("fsdp"), lax.axis_size("rep")
    if size < 3 or reps % 2:
        return [lax.all_gather(weight, "fsdp", axis=0, tiled=True) for weight in weights]
    count, planes = len(weights), plane_count()
    anywhere = pl.BlockSpec(memory_space=pl.ANY)
    copies = [(count, 2), (count, 2), (count, 3), (count, 3), (count,), (count,)]
    semaphores = [pltpu.SemaphoreType.DMA((*shape, size - 1)) for shape in copies]
    return pl.pallas_call(
        functools.partial(gather_kernel, size, planes, count),
        out_shape=[
            jax.ShapeDtypeStruct((size * weight.shape[0], weight.shape[1]), weight.dtype)
            for weight in weights
        ],
        in_specs=[anywhere] * count,
        out_specs=[anywhere] * count,
        scratch_shapes=semaphores + [pltpu.SemaphoreType.DMA((count,))],
        compiler_params=pltpu.CompilerParams(collective_id=kernel_id, has_side_effects=True),
        name="gather_rows",
    )(*weights)


def swapped(array, axis_size, bit):
    return lax.ppermute(array, "rep", [(rank, rank ^ bit) for rank in range(axis_size)])


def paired(axis_size):
    return axis_size > 1 and axis_size & (axis_size - 1) == 0


def rounded(values):
    return lax.reduce_precision(values, 8, 7).astype(jnp.bfloat16)


def scatter_kernel(size, planes, wide, late, *refs):
    count = len(wide)
    parts, sums = refs[:count], refs[count : 2 * count]
    slots, ends = refs[2 * count : 4 * count], refs[4 * count : 5 * count]
    ring_out, ring_in, plane_out, plane_in, core_out, core_in = refs[5 * count :]
    place, right, left = ring_neighbours(size)
    me = lax.axis_index("fsdp")
    rep, core, plane, sibling, across = rep_partners()
    partners = [(rep, right), (rep, left), (sibling, me)]
    greet(partners + ([(across, me)] if planes == 2 else []))

    def columns(array, way):
        first, width = column_cuts(parts[array].shape[2])[way]
        return pl.ds(first, width)

    def part(array, way, step):
        shift = (size - 1 - step) if way == 0 else (1 + step)
        owner = ring_index((place + shift) % size, size)
        return parts[array].at[owner, :, columns(array, way)]

    def slot(array, way, step):
        return slots[2 * array + way].at[step]

    def ring_copy(array, way, step):
        return pltpu.make_async_remote_copy(
            src_ref=slot(array, way, step - 1) if step else part(array, way, 0),
            dst_ref=slot(array, way, step),
            send_sem=ring_out.at[array, way, step],
            recv_sem=ring_in.at[array, way, step],
            device_id=(rep, right if way == 0 else left),
            device_id_type=MESH,
        )

    def result(array, second=False):
        if not wide[array]:
            return sums[array].at[core]
        return sums[array].at[2 * ((1 - plane) if second else plane) + core]

    def added_over_planes(array):
        return planes == 2 and not wide[array]

    def plane_copy(array):
        added = added_over_planes(array)
        return pltpu.make_async_remote_copy(
            src_ref=ends[array].at[0] if added else result(array),
            dst_ref=ends[array].at[1] if added else result(array),
            send_sem=plane_out.at[array],
            recv_sem=plane_in.at[array],
            device_id=(across, me),
            device_id_type=MESH,
        )

    def core_copy(array, second=False):
        block = result(array, second)
        return pltpu.make_async_remote_copy(
            src_ref=block,
            dst_ref=block,
            send_sem=core_out.at[array, int(second)],
            recv_sem=core_in.at[array, int(second)],
            device_id=(sibling, me),
            device_id_type=MESH,
        )

    def take(array, way, step):
        ring_copy(array, way, step).wait_recv()
        arrived, here = slot(array, way, step), part(array, way, step + 1)
        total = arrived[...].astype(jnp.float32) + here[...].astype(jnp.float32)
        total = total.astype(arrived.dtype)
        if step < size - 2:
            arrived[...] = total
            ring_copy(array, way, step + 1).start()
        elif added_over_planes(array):
            ends[array][0, :, columns(array, way)] = total
        else:
            index = 2 * plane + core if wide[array] else core
            sums[array][index, :, columns(array, way)] = total

    def hand_out(array):
        if planes == 2:
            plane_copy(array).start()
        if not added_over_planes(array):
            core_copy(array).start()

    def finish(array):
        if planes == 1:
            return
        plane_copy(array).wait_recv()
        if wide[array]:
            core_copy(array, True).start()
            return
        both = ends[array][0].astype(jnp.float32) + ends[array][1].astype(jnp.float32)
        sums[array][core] = both.astype(sums[array].dtype)
        core_copy(array).start()

    pairs = [(array, way) for array in range(count) for way in range(2)]
    for array, way in pairs:
        if late[array] == 0:
            ring_copy(array, way, 0).start()
    for turn in range(size + max(late) + 1):
        for array in range(count):
            step = turn - late[array]
            for way in range(2):
                if step == -1:
                    ring_copy(array, way, 0).start()
                if 0 <= step < size - 1:
                    take(array, way, step)
            if step == size - 2:
                hand_out(array)
            if step == size:
                finish(array)
    for array in range(count):
        for way in range(2):
            for step in range(size - 1):
                ring_copy(array, way, step).wait_send()
        core_copy(array).wait()
        if planes == 2:
            plane_copy(array).wait_send()
            if wide[array]:
                core_copy(array, True).wait()


def scattered(parts, wide, late, kernel_id):
    size, planes = lax.axis_size("fsdp"), plane_count()
    count = len(parts)
    on_chip = pl.BlockSpec(memory_space=pltpu.VMEM)
    slots = [
        pltpu.VMEM((size - 1, part.shape[1], width), part.dtype)
        for part in parts
        for _, width in column_cuts(part.shape[2])
    ]
    ends = [
        pltpu.VMEM((2, SUBLANES, LANES) if spread else (2, *part.shape[1:]), part.dtype)
        for part, spread in zip(parts, wide)
    ]
    copies = [(count, 2, size - 1)] * 2 + [(count,)] * 2 + [(count, 2)] * 2
    return pl.pallas_call(
        functools.partial(scatter_kernel, size, planes, wide, late),
        out_shape=[
            jax.ShapeDtypeStruct((4 if spread else 2, *part.shape[1:]), part.dtype)
            for part, spread in zip(parts, wide)
        ],
        in_specs=[on_chip] * count,
        out_specs=[on_chip] * count,
        scratch_shapes=slots + ends + [pltpu.SemaphoreType.DMA(shape) for shape in copies],
        compiler_params=pltpu.CompilerParams(
            collective_id=kernel_id, has_side_effects=True, vmem_limit_bytes=VMEM_BYTES
        ),
        name="scatter_sums",
    )(*parts)


def ringed():
    return lax.axis_size("fsdp") > 2 and paired(lax.axis_size("rep"))


def met(mine, theirs, bit):
    return jnp.concatenate([mine, swapped(theirs, lax.axis_size("rep"), bit)], axis=0)


def dealt(rows, bits):
    size = lax.axis_size("fsdp")
    for bit in bits:
        tokens, features = rows.shape
        split = rows.reshape(tokens, size, 2, features // (2 * size))
        first = split[:, :, 0].reshape(tokens, features // 2)
        second = split[:, :, 1].reshape(tokens, features // 2)
        even = (lax.axis_index("rep") // bit) % 2 == 0
        rows = met(jnp.where(even, first, second), jnp.where(even, second, first), bit)
    return rows


def met_all(rows, bits):
    for bit in bits:
        rows = met(rows, rows, bit)
    return rows


def owner_parts(lefts, rights, bits):
    size = lax.axis_size("fsdp")
    if not ringed():
        return [product_left(left, right).astype(jnp.bfloat16) for left, right in zip(lefts, rights)]
    dealt_lefts, parts = {}, []
    for left, right in zip(lefts, rights):
        if id(left) not in dealt_lefts:
            dealt_lefts[id(left)] = dealt(left, bits)
        part = product_left(dealt_lefts[id(left)], met_all(right, bits)).astype(jnp.bfloat16)
        parts.append(part.reshape(size, part.shape[0] // size, part.shape[1]))
    return parts


def weight_sums(ffn_parts, mix_parts, kernel_id):
    parts, reps = mix_parts + ffn_parts, lax.axis_size("rep")
    if not ringed():
        totals = [lax.psum_scatter(part, "fsdp", scatter_dimension=0, tiled=True) for part in parts]
        return [lax.psum(rows, "rep").astype(jnp.float32) for rows in totals]
    wide = [False] * len(mix_parts) + [plane_count() == 2] * len(ffn_parts)
    late = [0] * len(mix_parts) + [LATE_STEPS] * len(ffn_parts)
    totals = []
    for own in scattered(parts, wide, late, kernel_id):
        own = own.reshape(-1, own.shape[2])
        bit = 2 * plane_count()
        while bit < reps:
            own = rounded(own.astype(jnp.float32) + swapped(own, reps, bit).astype(jnp.float32))
            bit = 2 * bit
        totals.append(own.astype(jnp.float32))
    return totals


def total_sum(values):
    for name in ("rep", "fsdp"):
        size = lax.axis_size(name)
        if size & (size - 1):
            values = lax.psum(values, name)
            continue
        bit = 1
        while bit < size:
            pairs = [(rank, rank ^ bit) for rank in range(size)]
            values = values + lax.ppermute(values, name, pairs)
            bit = 2 * bit
    return values


def column_parts(array, widths):
    parts, start = [], 0
    for width in widths:
        parts.append(array[:, start : start + width])
        start = start + width
    return parts


def local(
    block_input,
    cotangent,
    doc_lengths,
    gain_mix,
    w_query,
    w_key,
    w_value,
    w_gate,
    w_decay,
    w_write,
    conv_query,
    conv_key,
    conv_value,
    decay_log,
    decay_bias,
    out_gain,
    w_out,
    gain_ffn,
    w_hidden,
    w_up,
    w_down,
):
    tokens = block_input.shape[0]
    segment = doc_segments(doc_lengths[0], tokens)
    head_count = decay_log.shape[0]
    narrow_widths = [w_query.shape[1], head_count, head_count]
    spare = -sum(narrow_widths) % LANES
    narrow = jnp.concatenate([w_query, w_decay, w_write], axis=1)
    narrow = jnp.pad(narrow, ((0, 0), (0, spare)))
    mixing = gathered([narrow, w_key, w_value, w_gate], 0)
    outward, hidden, up, downward = gathered([w_out, w_hidden, w_up, w_down], 1)
    upstream = cotangent.astype(jnp.bfloat16)

    normed, norm_back = jax.vjp(rms_norm, block_input, gain_mix)
    first_input = normed.astype(jnp.bfloat16)
    narrow_proj, key_proj, value_proj, gate_proj = [
        product(first_input, weight) for weight in mixing
    ]
    query_proj, decay_proj, write_proj = column_parts(narrow_proj, narrow_widths)

    def rows_of(maker):
        return lambda proj, kernel: maker(proj, kernel, segment, head_count)

    queries, query_back = jax.vjp(rows_of(query_rows_of), query_proj, conv_query)
    key_rows, key_back = jax.vjp(rows_of(unit_rows), key_proj, conv_key)
    value_rows, value_back = jax.vjp(rows_of(conv_rows), value_proj, conv_value)
    (decays, strength), gates_back = jax.vjp(
        head_gates, decay_proj, write_proj, decay_log, decay_bias
    )
    readout, readout_back = jax.vjp(
        lambda *operands: delta_rule(*operands, segment),
        queries,
        key_rows,
        value_rows,
        decays,
        strength,
    )
    mixed_out, mixed_back = jax.vjp(gated_norm, readout, gate_proj, out_gain)
    gated_out = mixed_out.astype(jnp.bfloat16)
    residual = block_input + product(gated_out, outward)
    normed_ffn, norm_ffn_back = jax.vjp(rms_norm, residual, gain_ffn)
    second = normed_ffn.astype(jnp.bfloat16)
    swiglu_out, swiglu_back = jax.vjp(swiglu, product(second, hidden), product(second, up))
    activation = swiglu_out.astype(jnp.bfloat16)
    block_out = residual + product(activation, downward)
    d_hidden, d_up = [
        grad.astype(jnp.bfloat16) for grad in swiglu_back(product_right(upstream, downward))
    ]
    d_second = product_right(d_hidden, hidden) + product_right(d_up, up)
    ffn_parts = owner_parts(
        [activation, second, second],
        [upstream, d_hidden, d_up],
        (2, 1) if plane_count() == 2 else (1,),
    )
    d_norm_ffn, grad_gain_ffn = norm_ffn_back(d_second)
    d_residual = cotangent + d_norm_ffn
    upstream_mix = d_residual.astype(jnp.bfloat16)
    d_mixed = product_right(upstream_mix, outward)
    d_readout, d_gate, grad_out_gain = mixed_back(d_mixed)
    d_queries, d_keys, d_values, d_decays, d_strength = readout_back(d_readout)
    d_value, grad_conv_value = value_back(d_values)
    d_query, grad_conv_query = query_back(d_queries)
    d_key, grad_conv_key = key_back(d_keys)
    d_decay, d_write, grad_decay_log, grad_decay_bias = gates_back((d_decays, d_strength))
    d_narrow = jnp.concatenate([d_query, d_decay, d_write], axis=1).astype(jnp.bfloat16)
    d_narrow = jnp.pad(d_narrow, ((0, 0), (0, spare)))
    d_mix = [d_narrow, *(rows.astype(jnp.bfloat16) for rows in (d_key, d_value, d_gate))]
    mix_parts = owner_parts([gated_out] + [first_input] * 4, [upstream_mix] + d_mix, (1,))
    d_first = sum(product_right(rows, weight) for rows, weight in zip(d_mix, mixing))
    d_norm, grad_gain_mix = norm_back(d_first)
    input_grad = d_residual + d_norm
    sums = weight_sums(ffn_parts, mix_parts, 2)
    grad_out, grad_narrow, grad_key, grad_value, grad_gate = sums[:5]
    grad_down, grad_hidden, grad_up = sums[5:]
    grad_query, grad_decay, grad_write = column_parts(grad_narrow, narrow_widths)
    small = (
        grad_gain_mix,
        grad_conv_query,
        grad_conv_key,
        grad_conv_value,
        grad_decay_log,
        grad_decay_bias,
        grad_out_gain,
        grad_gain_ffn,
    )
    flat = jnp.concatenate([grad.reshape(-1) for grad in small])
    flat = total_sum(flat)
    small_totals, start = [], 0
    for grad in small:
        small_totals.append(flat[start : start + grad.size].reshape(grad.shape))
        start = start + grad.size
    return (
        block_out,
        input_grad,
        small_totals[0],
        grad_query,
        grad_key,
        grad_value,
        grad_gate,
        grad_decay,
        grad_write,
        *small_totals[1:7],
        grad_out,
        small_totals[7],
        grad_hidden,
        grad_up,
        grad_down,
    )


def solution(mesh):
    placed = (
        P(("rep", "fsdp"), None),
        P(("rep", "fsdp"), None),
        P(("rep", "fsdp"), None),
        P(),
        P("fsdp", None),
        P("fsdp", None),
        P("fsdp", None),
        P("fsdp", None),
        P("fsdp", None),
        P("fsdp", None),
        P(),
        P(),
        P(),
        P(),
        P(),
        P(),
        P("fsdp", None),
        P(),
        P("fsdp", None),
        P("fsdp", None),
        P("fsdp", None),
    )
    return jax.shard_map(
        local,
        mesh=mesh,
        in_specs=placed,
        out_specs=(
            P(("rep", "fsdp"), None),
            P(("rep", "fsdp"), None),
            P(),
            P("fsdp", None),
            P("fsdp", None),
            P("fsdp", None),
            P("fsdp", None),
            P("fsdp", None),
            P("fsdp", None),
            P(),
            P(),
            P(),
            P(),
            P(),
            P(),
            P("fsdp", None),
            P(),
            P("fsdp", None),
            P("fsdp", None),
            P("fsdp", None),
        ),
        check_vma=False,
    )
```

```python
import functools

import jax
import jax.numpy as jnp
from jax import lax
from jax.experimental import pallas as pl
from jax.experimental.pallas import tpu as pltpu
from jax.sharding import PartitionSpec as P

EPSILON = 1e-06
TOP_PRECISION = lax.Precision.HIGHEST
MIX_PRECISION = lax.Precision.HIGH
LANES = 128
SUBLANES = 16
LATE_STEPS = 3
VMEM_BYTES = 48 * 1024 * 1024
MESH = pl.DeviceIdType.MESH


def product(left, right):
    return jnp.dot(left, right, preferred_element_type=jnp.float32)


def product_left(left, right):
    return lax.dot_general(
        left, right, (((0,), (0,)), ((), ())), preferred_element_type=jnp.float32
    )


def product_right(left, right):
    return lax.dot_general(
        left, right, (((1,), (1,)), ((), ())), preferred_element_type=jnp.float32
    )


def rms_norm(values, gain):
    return values * lax.rsqrt(jnp.mean(values * values, axis=-1, keepdims=True) + EPSILON) * gain


def swiglu(hidden_pre, up_pre):
    return jax.nn.silu(hidden_pre) * up_pre


def doc_segments(lengths, tokens):
    order = jnp.arange(lengths.shape[0], dtype=jnp.int32)
    upto = order[None, :] <= order[:, None]
    doc_ends = jnp.sum(jnp.where(upto, lengths[None, :], 0), axis=1)
    positions = jnp.arange(tokens, dtype=jnp.int32)
    return jnp.sum((positions[:, None] >= doc_ends[None, :]).astype(jnp.int32), axis=1)


def shifted(values, offset, fill):
    filler = jnp.full((offset,) + values.shape[1:], fill, values.dtype)
    return jnp.concatenate([filler, values[:-offset]], axis=0)


def short_conv(values, kernel, segment):
    summed = values * kernel[0]
    for offset in range(1, kernel.shape[0]):
        same_doc = (shifted(segment, offset, -1) == segment).astype(values.dtype)
        summed = summed + shifted(values, offset, 0.0) * kernel[offset] * same_doc[:, None]
    return summed


def unit_inverse(lower_part):
    width = lower_part.shape[-1]
    index = jnp.arange(width, dtype=jnp.int32)
    inverse = None
    size = 1
    while size < width:
        rows, columns = index[:, None] // size, index[None, :] // size
        pairs = (rows % 2 == 1) & (columns == rows - 1)
        level = jnp.where(pairs[None], lower_part, 0.0)
        if inverse is None:
            inverse = jnp.eye(width, dtype=lower_part.dtype)[None] - level
        else:
            step = jnp.einsum("hij,hjk->hik", level, inverse, precision=MIX_PRECISION)
            inverse = inverse - jnp.einsum("hij,hjk->hik", inverse, step, precision=MIX_PRECISION)
        size = 2 * size
    return inverse


@jax.custom_vjp
def unit_solve(lower_part, sources):
    return jnp.einsum("hij,hjv->hiv", unit_inverse(lower_part), sources, precision=MIX_PRECISION)


def unit_solve_fwd(lower_part, sources):
    inverse = unit_inverse(lower_part)
    solved = jnp.einsum("hij,hjv->hiv", inverse, sources, precision=MIX_PRECISION)
    return solved, (inverse, solved)


def unit_solve_bwd(saved, d_solved):
    inverse, solved = saved
    d_sources = jnp.einsum("hji,hjv->hiv", inverse, d_solved, precision=MIX_PRECISION)
    d_lower = -jnp.einsum("hiv,hjv->hij", d_sources, solved, precision=MIX_PRECISION)
    return d_lower, d_sources


unit_solve.defvjp(unit_solve_fwd, unit_solve_bwd)


def delta_rule(query_rows, key_matrix, value_rows, decays, strength, segment):
    width = segment.shape[0]
    positions = jnp.arange(width, dtype=jnp.int32)
    same_doc = segment[:, None] == segment[None, :]
    lower_mask = same_doc & (positions[:, None] >= positions[None, :])
    strict_mask = same_doc & (positions[:, None] > positions[None, :])
    cumulative = jnp.einsum(
        "ij,hj->hi", lower_mask.astype(decays.dtype), decays, precision=TOP_PRECISION
    )
    spread = jnp.minimum(cumulative[:, :, None] - cumulative[:, None, :], 0.0)
    ratios = jnp.where(lower_mask[None], jnp.exp(spread), 0.0)
    key_inner = jnp.einsum("hid,hjd->hij", key_matrix, key_matrix, precision=MIX_PRECISION)
    lower_part = jnp.where(strict_mask[None], strength[:, :, None] * ratios * key_inner, 0.0)
    delta_rows = unit_solve(lower_part, strength[:, :, None] * value_rows)
    scores = jnp.einsum("hid,hjd->hij", query_rows, key_matrix, precision=MIX_PRECISION) * ratios
    return jnp.einsum("hij,hjv->hiv", scores, delta_rows, precision=MIX_PRECISION)


def conv_rows(proj, kernel, segment, head_count):
    rows = jax.nn.silu(short_conv(proj, kernel, segment))
    return jnp.swapaxes(rows.reshape(proj.shape[0], head_count, -1), 0, 1)


def unit_rows(proj, kernel, segment, head_count):
    rows = conv_rows(proj, kernel, segment, head_count)
    return rows * lax.rsqrt(jnp.sum(rows * rows, axis=2, keepdims=True) + EPSILON)


def query_rows_of(proj, kernel, segment, head_count):
    rows = unit_rows(proj, kernel, segment, head_count)
    return rows * rows.shape[2] ** (-0.5)


def head_gates(decay_proj, write_proj, decay_log, decay_bias):
    decays = -jnp.exp(decay_log) * jax.nn.softplus(decay_proj + decay_bias)
    return decays.T, jax.nn.sigmoid(write_proj).T


def gated_norm(readout_rows, gate_proj, out_gain):
    tokens = gate_proj.shape[0]
    rows = jnp.swapaxes(readout_rows, 0, 1)
    rows = rows * lax.rsqrt(jnp.mean(rows * rows, axis=2, keepdims=True) + EPSILON) * out_gain
    return (rows * jax.nn.silu(gate_proj.reshape(rows.shape))).reshape(tokens, -1)


def ring_index(place, size):
    half = (size + 1) // 2
    back = place // half
    return (1 - back) * (2 * place) + back * (2 * (size - 1 - place) + 1)


def ring_place(index, size):
    odd = index % 2
    return (1 - odd) * (index // 2) + odd * (size - 1 - index // 2)


def ring_neighbours(size):
    place = ring_place(lax.axis_index("fsdp"), size)
    return (
        place,
        ring_index((place + 1) % size, size),
        ring_index((place + size - 1) % size, size),
    )


def greet(partners):
    barrier = pltpu.get_barrier_semaphore()
    for partner in partners:
        pl.semaphore_signal(barrier, inc=1, device_id=partner, device_id_type=MESH)
    pl.semaphore_wait(barrier, len(partners))


def column_cuts(columns):
    cut = (columns // (2 * LANES)) * LANES
    return ((0, cut), (cut, columns - cut))


def plane_count():
    return 2 if lax.axis_size("rep") % 4 == 0 else 1


def rep_partners():
    rep = lax.axis_index("rep")
    core, plane = rep % 2, (rep // 2) % 2
    return rep, core, plane, rep + 1 - 2 * core, rep + 2 - 4 * plane


def plane_columns(columns, planes, plane):
    if planes == 1:
        cuts = column_cuts(columns)
        return (*cuts, cuts[0])
    third = ((columns // LANES + 1) // 3) * LANES
    own = pl.multiple_of(plane * third, LANES)
    other = pl.multiple_of((1 - plane) * third, LANES)
    return (own, third), (2 * third, columns - 2 * third), (other, third)


OWN, BOTH, OTHER = range(3)


def gather_kernel(size, planes, count, *refs):
    shards, wholes = refs[:count], refs[count : 2 * count]
    ring_out, ring_in, core_out, core_in, plane_out, plane_in, local_sem = refs[2 * count :]
    place, right, left = ring_neighbours(size)
    me = lax.axis_index("fsdp")
    rep, core, plane, sibling, across = rep_partners()
    partners = [(rep, right), (rep, left), (sibling, me)]
    greet(partners + ([(across, me)] if planes == 2 else []))

    def piece(ref, array, kind, base):
        rows, columns = shards[array].shape
        by_rows = (rows // 2) % SUBLANES == 0
        width = columns if by_rows else columns // 2
        first, part = plane_columns(width, planes, plane)[kind]
        if by_rows:
            base, height = base + core * (rows // 2), rows // 2
        else:
            first, height = pl.multiple_of(core * width + first, LANES), rows
        return ref.at[pl.ds(pl.multiple_of(base, SUBLANES), height), pl.ds(first, part)]

    def placed(array, kind, step):
        shift = step if kind == BOTH else (size - step)
        owner = ring_index((place + shift) % size, size)
        return piece(wholes[array], array, kind, owner * shards[array].shape[0])

    def ring_copy(array, way, step):
        block = placed(array, way, step)
        return pltpu.make_async_remote_copy(
            src_ref=block if step else piece(shards[array], array, way, 0),
            dst_ref=block,
            send_sem=ring_out.at[array, way, step],
            recv_sem=ring_in.at[array, way, step],
            device_id=(rep, right if way == OWN else left),
            device_id_type=MESH,
        )

    def core_copy(array, kind, step):
        block = placed(array, kind, step + 1)
        return pltpu.make_async_remote_copy(
            src_ref=block,
            dst_ref=block,
            send_sem=core_out.at[array, kind, step],
            recv_sem=core_in.at[array, kind, step],
            device_id=(sibling, me),
            device_id_type=MESH,
        )

    def plane_copy(array, step):
        block = placed(array, OWN, step + 1)
        return pltpu.make_async_remote_copy(
            src_ref=block,
            dst_ref=block,
            send_sem=plane_out.at[array, step],
            recv_sem=plane_in.at[array, step],
            device_id=(across, me),
            device_id_type=MESH,
        )

    def own_copy(array):
        rows = shards[array].shape[0]
        start = pl.multiple_of(me * rows, SUBLANES)
        return pltpu.make_async_copy(
            shards[array], wholes[array].at[pl.ds(start, rows)], local_sem.at[array]
        )

    def hand_over(step):
        for array in range(count):
            plane_copy(array, step).wait_recv()
            core_copy(array, OTHER, step).start()

    pairs = [(array, way) for array in range(count) for way in (OWN, BOTH)]
    for array, way in pairs:
        ring_copy(array, way, 0).start()
    for array in range(count):
        own_copy(array).start()
    for step in range(size - 1):
        for array, way in pairs:
            ring_copy(array, way, step).wait_recv()
            if step < size - 2:
                ring_copy(array, way, step + 1).start()
            if way == OWN and planes == 2:
                plane_copy(array, step).start()
            core_copy(array, way, step).start()
        if planes == 2 and step:
            hand_over(step - 1)
    if planes == 2:
        hand_over(size - 2)
    for array in range(count):
        own_copy(array).wait()
    for step in range(size - 1):
        for array, way in pairs:
            ring_copy(array, way, step).wait_send()
            core_copy(array, way, step).wait()
        if planes == 2:
            for array in range(count):
                plane_copy(array, step).wait_send()
                core_copy(array, OTHER, step).wait()


def gathered(weights, kernel_id):
    size, reps = lax.axis_size("fsdp"), lax.axis_size("rep")
    if size < 3 or reps % 2:
        return [lax.all_gather(weight, "fsdp", axis=0, tiled=True) for weight in weights]
    count, planes = len(weights), plane_count()
    anywhere = pl.BlockSpec(memory_space=pl.ANY)
    copies = [(count, 2), (count, 2), (count, 3), (count, 3), (count,), (count,)]
    semaphores = [pltpu.SemaphoreType.DMA((*shape, size - 1)) for shape in copies]
    return pl.pallas_call(
        functools.partial(gather_kernel, size, planes, count),
        out_shape=[
            jax.ShapeDtypeStruct((size * weight.shape[0], weight.shape[1]), weight.dtype)
            for weight in weights
        ],
        in_specs=[anywhere] * count,
        out_specs=[anywhere] * count,
        scratch_shapes=semaphores + [pltpu.SemaphoreType.DMA((count,))],
        compiler_params=pltpu.CompilerParams(collective_id=kernel_id, has_side_effects=True),
        name="gather_rows",
    )(*weights)


def swapped(array, axis_size, bit):
    return lax.ppermute(array, "rep", [(rank, rank ^ bit) for rank in range(axis_size)])


def paired(axis_size):
    return axis_size > 1 and axis_size & (axis_size - 1) == 0


def rounded(values):
    return lax.reduce_precision(values, 8, 7).astype(jnp.bfloat16)


def scatter_kernel(size, planes, wide, late, *refs):
    count = len(wide)
    parts, sums = refs[:count], refs[count : 2 * count]
    slots, ends = refs[2 * count : 4 * count], refs[4 * count : 5 * count]
    ring_out, ring_in, plane_out, plane_in, core_out, core_in = refs[5 * count :]
    place, right, left = ring_neighbours(size)
    me = lax.axis_index("fsdp")
    rep, core, plane, sibling, across = rep_partners()
    partners = [(rep, right), (rep, left), (sibling, me)]
    greet(partners + ([(across, me)] if planes == 2 else []))

    def columns(array, way):
        first, width = column_cuts(parts[array].shape[2])[way]
        return pl.ds(first, width)

    def part(array, way, step):
        shift = (size - 1 - step) if way == 0 else (1 + step)
        owner = ring_index((place + shift) % size, size)
        return parts[array].at[owner, :, columns(array, way)]

    def slot(array, way, step):
        return slots[2 * array + way].at[step]

    def ring_copy(array, way, step):
        return pltpu.make_async_remote_copy(
            src_ref=slot(array, way, step - 1) if step else part(array, way, 0),
            dst_ref=slot(array, way, step),
            send_sem=ring_out.at[array, way, step],
            recv_sem=ring_in.at[array, way, step],
            device_id=(rep, right if way == 0 else left),
            device_id_type=MESH,
        )

    def result(array, second=False):
        if not wide[array]:
            return sums[array].at[core]
        return sums[array].at[2 * ((1 - plane) if second else plane) + core]

    def added_over_planes(array):
        return planes == 2 and not wide[array]

    def plane_copy(array):
        added = added_over_planes(array)
        return pltpu.make_async_remote_copy(
            src_ref=ends[array].at[0] if added else result(array),
            dst_ref=ends[array].at[1] if added else result(array),
            send_sem=plane_out.at[array],
            recv_sem=plane_in.at[array],
            device_id=(across, me),
            device_id_type=MESH,
        )

    def core_copy(array, second=False):
        block = result(array, second)
        return pltpu.make_async_remote_copy(
            src_ref=block,
            dst_ref=block,
            send_sem=core_out.at[array, int(second)],
            recv_sem=core_in.at[array, int(second)],
            device_id=(sibling, me),
            device_id_type=MESH,
        )

    def take(array, way, step):
        ring_copy(array, way, step).wait_recv()
        arrived, here = slot(array, way, step), part(array, way, step + 1)
        total = arrived[...].astype(jnp.float32) + here[...].astype(jnp.float32)
        total = total.astype(arrived.dtype)
        if step < size - 2:
            arrived[...] = total
            ring_copy(array, way, step + 1).start()
        elif added_over_planes(array):
            ends[array][0, :, columns(array, way)] = total
        else:
            index = 2 * plane + core if wide[array] else core
            sums[array][index, :, columns(array, way)] = total

    def hand_out(array):
        if planes == 2:
            plane_copy(array).start()
        if not added_over_planes(array):
            core_copy(array).start()

    def finish(array):
        if planes == 1:
            return
        plane_copy(array).wait_recv()
        if wide[array]:
            core_copy(array, True).start()
            return
        both = ends[array][0].astype(jnp.float32) + ends[array][1].astype(jnp.float32)
        sums[array][core] = both.astype(sums[array].dtype)
        core_copy(array).start()

    pairs = [(array, way) for array in range(count) for way in range(2)]
    for array, way in pairs:
        if late[array] == 0:
            ring_copy(array, way, 0).start()
    for turn in range(size + max(late) + 1):
        for array in range(count):
            step = turn - late[array]
            for way in range(2):
                if step == -1:
                    ring_copy(array, way, 0).start()
                if 0 <= step < size - 1:
                    take(array, way, step)
            if step == size - 2:
                hand_out(array)
            if step == size:
                finish(array)
    for array in range(count):
        for way in range(2):
            for step in range(size - 1):
                ring_copy(array, way, step).wait_send()
        core_copy(array).wait()
        if planes == 2:
            plane_copy(array).wait_send()
            if wide[array]:
                core_copy(array, True).wait()


def scattered(parts, wide, late, kernel_id):
    size, planes = lax.axis_size("fsdp"), plane_count()
    count = len(parts)
    on_chip = pl.BlockSpec(memory_space=pltpu.VMEM)
    slots = [
        pltpu.VMEM((size - 1, part.shape[1], width), part.dtype)
        for part in parts
        for _, width in column_cuts(part.shape[2])
    ]
    ends = [
        pltpu.VMEM((2, SUBLANES, LANES) if spread else (2, *part.shape[1:]), part.dtype)
        for part, spread in zip(parts, wide)
    ]
    copies = [(count, 2, size - 1)] * 2 + [(count,)] * 2 + [(count, 2)] * 2
    return pl.pallas_call(
        functools.partial(scatter_kernel, size, planes, wide, late),
        out_shape=[
            jax.ShapeDtypeStruct((4 if spread else 2, *part.shape[1:]), part.dtype)
            for part, spread in zip(parts, wide)
        ],
        in_specs=[on_chip] * count,
        out_specs=[on_chip] * count,
        scratch_shapes=slots + ends + [pltpu.SemaphoreType.DMA(shape) for shape in copies],
        compiler_params=pltpu.CompilerParams(
            collective_id=kernel_id, has_side_effects=True, vmem_limit_bytes=VMEM_BYTES
        ),
        cost_estimate=pl.CostEstimate(
            flops=2 * sum(part.size for part in parts),
            bytes_accessed=4 * size * sum(part.size for part in parts),
            transcendentals=0,
        ),
        name="scatter_sums",
    )(*parts)


def ringed():
    return lax.axis_size("fsdp") > 2 and paired(lax.axis_size("rep"))


def met(mine, theirs, bit):
    return jnp.concatenate([mine, swapped(theirs, lax.axis_size("rep"), bit)], axis=0)


def dealt(rows, bit):
    size = lax.axis_size("fsdp")
    tokens, features = rows.shape
    split = rows.reshape(tokens, size, 2, features // (2 * size))
    first = split[:, :, 0].reshape(tokens, features // 2)
    second = split[:, :, 1].reshape(tokens, features // 2)
    even = (lax.axis_index("rep") // bit) % 2 == 0
    return met(jnp.where(even, first, second), jnp.where(even, second, first), bit)


def exchanged(lefts, rights, bit):
    return [dealt(rows, bit) for rows in lefts], [met(rows, rows, bit) for rows in rights]


def owner_parts(lefts, rights):
    size = lax.axis_size("fsdp")
    parts = [product_left(left, right).astype(jnp.bfloat16) for left, right in zip(lefts, rights)]
    if not ringed():
        return parts
    return [part.reshape(size, part.shape[0] // size, part.shape[1]) for part in parts]


def weight_sums(ffn_parts, mix_parts, kernel_id):
    parts, reps = mix_parts + ffn_parts, lax.axis_size("rep")
    if not ringed():
        totals = [lax.psum_scatter(part, "fsdp", scatter_dimension=0, tiled=True) for part in parts]
        return [lax.psum(rows, "rep").astype(jnp.float32) for rows in totals]
    wide = [False] * len(mix_parts) + [plane_count() == 2] * len(ffn_parts)
    late = [0] * len(mix_parts) + [LATE_STEPS] * len(ffn_parts)
    totals = []
    for own in scattered(parts, wide, late, kernel_id):
        own = own.reshape(-1, own.shape[2])
        bit = 2 * plane_count()
        while bit < reps:
            own = rounded(own.astype(jnp.float32) + swapped(own, reps, bit).astype(jnp.float32))
            bit = 2 * bit
        totals.append(own.astype(jnp.float32))
    return totals


def column_parts(array, widths):
    parts, start = [], 0
    for width in widths:
        parts.append(array[:, start : start + width])
        start = start + width
    return parts


def local(
    block_input,
    cotangent,
    doc_lengths,
    gain_mix,
    w_query,
    w_key,
    w_value,
    w_gate,
    w_decay,
    w_write,
    conv_query,
    conv_key,
    conv_value,
    decay_log,
    decay_bias,
    out_gain,
    w_out,
    gain_ffn,
    w_hidden,
    w_up,
    w_down,
):
    tokens = block_input.shape[0]
    segment = doc_segments(doc_lengths[0], tokens)
    head_count = decay_log.shape[0]
    narrow_widths = [w_query.shape[1], head_count, head_count]
    spare = -sum(narrow_widths) % LANES
    narrow = jnp.concatenate([w_query, w_decay, w_write], axis=1)
    narrow = jnp.pad(narrow, ((0, 0), (0, spare)))
    mixing = gathered([narrow, w_key, w_value, w_gate], 0)
    outward, hidden, up, downward = gathered([w_out, w_hidden, w_up, w_down], 1)
    upstream = cotangent.astype(jnp.bfloat16)

    normed, norm_back = jax.vjp(rms_norm, block_input, gain_mix)
    first_input = normed.astype(jnp.bfloat16)
    narrow_proj, key_proj, value_proj, gate_proj = [
        product(first_input, weight) for weight in mixing
    ]
    query_proj, decay_proj, write_proj = column_parts(narrow_proj, narrow_widths)

    def rows_of(maker):
        return lambda proj, kernel: maker(proj, kernel, segment, head_count)

    queries, query_back = jax.vjp(rows_of(query_rows_of), query_proj, conv_query)
    key_rows, key_back = jax.vjp(rows_of(unit_rows), key_proj, conv_key)
    value_rows, value_back = jax.vjp(rows_of(conv_rows), value_proj, conv_value)
    (decays, strength), gates_back = jax.vjp(
        head_gates, decay_proj, write_proj, decay_log, decay_bias
    )
    readout, readout_back = jax.vjp(
        lambda *operands: delta_rule(*operands, segment),
        queries,
        key_rows,
        value_rows,
        decays,
        strength,
    )
    mixed_out, mixed_back = jax.vjp(gated_norm, readout, gate_proj, out_gain)
    gated_out = mixed_out.astype(jnp.bfloat16)
    residual = block_input + product(gated_out, outward)
    normed_ffn, norm_ffn_back = jax.vjp(rms_norm, residual, gain_ffn)
    second = normed_ffn.astype(jnp.bfloat16)
    swiglu_out, swiglu_back = jax.vjp(swiglu, product(second, hidden), product(second, up))
    activation = swiglu_out.astype(jnp.bfloat16)
    block_out = residual + product(activation, downward)
    d_hidden, d_up = [
        grad.astype(jnp.bfloat16) for grad in swiglu_back(product_right(upstream, downward))
    ]
    d_second = product_right(d_hidden, hidden) + product_right(d_up, up)
    ffn_lefts, ffn_rights = [activation, second], [upstream, d_hidden, d_up]
    if plane_count() == 2 and ringed():
        ffn_lefts, ffn_rights = exchanged(ffn_lefts, ffn_rights, 2)
    d_norm_ffn, grad_gain_ffn = norm_ffn_back(d_second)
    d_residual = cotangent + d_norm_ffn
    upstream_mix = d_residual.astype(jnp.bfloat16)
    d_mixed = product_right(upstream_mix, outward)
    d_readout, d_gate, grad_out_gain = mixed_back(d_mixed)
    d_queries, d_keys, d_values, d_decays, d_strength = readout_back(d_readout)
    d_value, grad_conv_value = value_back(d_values)
    (d_value, d_queries, d_keys), ffn_lefts, ffn_rights = lax.optimization_barrier(
        ((d_value, d_queries, d_keys), ffn_lefts, ffn_rights)
    )
    if ringed():
        ffn_lefts, ffn_rights = exchanged(ffn_lefts, ffn_rights, 1)
    d_query, grad_conv_query = query_back(d_queries)
    d_key, grad_conv_key = key_back(d_keys)
    d_decay, d_write, grad_decay_log, grad_decay_bias = gates_back((d_decays, d_strength))
    d_narrow = jnp.concatenate([d_query, d_decay, d_write], axis=1).astype(jnp.bfloat16)
    d_narrow = jnp.pad(d_narrow, ((0, 0), (0, spare)))
    d_mix = [d_narrow, *(rows.astype(jnp.bfloat16) for rows in (d_key, d_value, d_gate))]
    d_mix, ffn_lefts, ffn_rights = lax.optimization_barrier((d_mix, ffn_lefts, ffn_rights))
    mix_lefts, mix_rights = [gated_out, first_input], [upstream_mix, *d_mix]
    if ringed():
        mix_lefts, mix_rights = exchanged(mix_lefts, mix_rights, 1)
    ffn_parts = owner_parts([ffn_lefts[0]] + [ffn_lefts[1]] * 2, ffn_rights)
    mix_parts = owner_parts([mix_lefts[0]] + [mix_lefts[1]] * 4, mix_rights)
    d_first = sum(product_right(rows, weight) for rows, weight in zip(d_mix, mixing))
    d_norm, grad_gain_mix = norm_back(d_first)
    input_grad = d_residual + d_norm
    sums = weight_sums(ffn_parts, mix_parts, 2)
    grad_out, grad_narrow, grad_key, grad_value, grad_gate = sums[:5]
    grad_down, grad_hidden, grad_up = sums[5:]
    grad_query, grad_decay, grad_write = column_parts(grad_narrow, narrow_widths)
    small = (
        grad_gain_mix,
        grad_conv_query,
        grad_conv_key,
        grad_conv_value,
        grad_decay_log,
        grad_decay_bias,
        grad_out_gain,
        grad_gain_ffn,
    )
    flat = jnp.concatenate([grad.reshape(-1) for grad in small])
    flat = lax.psum(flat, ("rep", "fsdp"))
    small_totals, start = [], 0
    for grad in small:
        small_totals.append(flat[start : start + grad.size].reshape(grad.shape))
        start = start + grad.size
    return (
        block_out,
        input_grad,
        small_totals[0],
        grad_query,
        grad_key,
        grad_value,
        grad_gate,
        grad_decay,
        grad_write,
        *small_totals[1:7],
        grad_out,
        small_totals[7],
        grad_hidden,
        grad_up,
        grad_down,
    )


def solution(mesh):
    placed = (
        P(("rep", "fsdp"), None),
        P(("rep", "fsdp"), None),
        P(("rep", "fsdp"), None),
        P(),
        P("fsdp", None),
        P("fsdp", None),
        P("fsdp", None),
        P("fsdp", None),
        P("fsdp", None),
        P("fsdp", None),
        P(),
        P(),
        P(),
        P(),
        P(),
        P(),
        P("fsdp", None),
        P(),
        P("fsdp", None),
        P("fsdp", None),
        P("fsdp", None),
    )
    return jax.shard_map(
        local,
        mesh=mesh,
        in_specs=placed,
        out_specs=(
            P(("rep", "fsdp"), None),
            P(("rep", "fsdp"), None),
            P(),
            P("fsdp", None),
            P("fsdp", None),
            P("fsdp", None),
            P("fsdp", None),
            P("fsdp", None),
            P("fsdp", None),
            P(),
            P(),
            P(),
            P(),
            P(),
            P(),
            P("fsdp", None),
            P(),
            P("fsdp", None),
            P("fsdp", None),
            P("fsdp", None),
        ),
        check_vma=False,
    )
```

```python
import functools

import jax
import jax.numpy as jnp
from jax import lax
from jax.experimental import pallas as pl
from jax.experimental.pallas import tpu as pltpu
from jax.sharding import PartitionSpec as P

EPSILON = 1e-06
TOP_PRECISION = lax.Precision.HIGHEST
MIX_PRECISION = lax.Precision.HIGH
LANES = 128
SUBLANES = 16
LATE_STEPS = 3
VMEM_BYTES = 48 * 1024 * 1024
MESH = pl.DeviceIdType.MESH


def product(left, right):
    return jnp.dot(left, right, preferred_element_type=jnp.float32)


def product_left(left, right):
    return lax.dot_general(
        left, right, (((0,), (0,)), ((), ())), preferred_element_type=jnp.float32
    )


def product_right(left, right):
    return lax.dot_general(
        left, right, (((1,), (1,)), ((), ())), preferred_element_type=jnp.float32
    )


def rms_norm(values, gain):
    return values * lax.rsqrt(jnp.mean(values * values, axis=-1, keepdims=True) + EPSILON) * gain


def swiglu(hidden_pre, up_pre):
    return jax.nn.silu(hidden_pre) * up_pre


def doc_segments(lengths, tokens):
    order = jnp.arange(lengths.shape[0], dtype=jnp.int32)
    upto = order[None, :] <= order[:, None]
    doc_ends = jnp.sum(jnp.where(upto, lengths[None, :], 0), axis=1)
    positions = jnp.arange(tokens, dtype=jnp.int32)
    return jnp.sum((positions[:, None] >= doc_ends[None, :]).astype(jnp.int32), axis=1)


def shifted(values, offset, fill):
    filler = jnp.full((offset,) + values.shape[1:], fill, values.dtype)
    return jnp.concatenate([filler, values[:-offset]], axis=0)


def short_conv(values, kernel, segment):
    summed = values * kernel[0]
    for offset in range(1, kernel.shape[0]):
        same_doc = (shifted(segment, offset, -1) == segment).astype(values.dtype)
        summed = summed + shifted(values, offset, 0.0) * kernel[offset] * same_doc[:, None]
    return summed


def unit_inverse(lower_part):
    width = lower_part.shape[-1]
    index = jnp.arange(width, dtype=jnp.int32)
    inverse = None
    size = 1
    while size < width:
        rows, columns = index[:, None] // size, index[None, :] // size
        pairs = (rows % 2 == 1) & (columns == rows - 1)
        level = jnp.where(pairs[None], lower_part, 0.0)
        if inverse is None:
            inverse = jnp.eye(width, dtype=lower_part.dtype)[None] - level
        else:
            step = jnp.einsum("hij,hjk->hik", level, inverse, precision=MIX_PRECISION)
            inverse = inverse - jnp.einsum("hij,hjk->hik", inverse, step, precision=MIX_PRECISION)
        size = 2 * size
    return inverse


@jax.custom_vjp
def unit_solve(lower_part, sources):
    return jnp.einsum("hij,hjv->hiv", unit_inverse(lower_part), sources, precision=MIX_PRECISION)


def unit_solve_fwd(lower_part, sources):
    inverse = unit_inverse(lower_part)
    solved = jnp.einsum("hij,hjv->hiv", inverse, sources, precision=MIX_PRECISION)
    return solved, (inverse, solved)


def unit_solve_bwd(saved, d_solved):
    inverse, solved = saved
    d_sources = jnp.einsum("hji,hjv->hiv", inverse, d_solved, precision=MIX_PRECISION)
    d_lower = -jnp.einsum("hiv,hjv->hij", d_sources, solved, precision=MIX_PRECISION)
    return d_lower, d_sources


unit_solve.defvjp(unit_solve_fwd, unit_solve_bwd)


def delta_rule(query_rows, key_matrix, value_rows, decays, strength, segment):
    width = segment.shape[0]
    positions = jnp.arange(width, dtype=jnp.int32)
    same_doc = segment[:, None] == segment[None, :]
    lower_mask = same_doc & (positions[:, None] >= positions[None, :])
    strict_mask = same_doc & (positions[:, None] > positions[None, :])
    cumulative = jnp.einsum(
        "ij,hj->hi", lower_mask.astype(decays.dtype), decays, precision=TOP_PRECISION
    )
    spread = jnp.minimum(cumulative[:, :, None] - cumulative[:, None, :], 0.0)
    ratios = jnp.where(lower_mask[None], jnp.exp(spread), 0.0)
    key_inner = jnp.einsum("hid,hjd->hij", key_matrix, key_matrix, precision=MIX_PRECISION)
    lower_part = jnp.where(strict_mask[None], strength[:, :, None] * ratios * key_inner, 0.0)
    delta_rows = unit_solve(lower_part, strength[:, :, None] * value_rows)
    scores = jnp.einsum("hid,hjd->hij", query_rows, key_matrix, precision=MIX_PRECISION) * ratios
    return jnp.einsum("hij,hjv->hiv", scores, delta_rows, precision=MIX_PRECISION)


def conv_rows(proj, kernel, segment, head_count):
    rows = jax.nn.silu(short_conv(proj, kernel, segment))
    return jnp.swapaxes(rows.reshape(proj.shape[0], head_count, -1), 0, 1)


def unit_rows(proj, kernel, segment, head_count):
    rows = conv_rows(proj, kernel, segment, head_count)
    return rows * lax.rsqrt(jnp.sum(rows * rows, axis=2, keepdims=True) + EPSILON)


def query_rows_of(proj, kernel, segment, head_count):
    rows = unit_rows(proj, kernel, segment, head_count)
    return rows * rows.shape[2] ** (-0.5)


def head_gates(decay_proj, write_proj, decay_log, decay_bias):
    decays = -jnp.exp(decay_log) * jax.nn.softplus(decay_proj + decay_bias)
    return decays.T, jax.nn.sigmoid(write_proj).T


def gated_norm(readout_rows, gate_proj, out_gain):
    tokens = gate_proj.shape[0]
    rows = jnp.swapaxes(readout_rows, 0, 1)
    rows = rows * lax.rsqrt(jnp.mean(rows * rows, axis=2, keepdims=True) + EPSILON) * out_gain
    return (rows * jax.nn.silu(gate_proj.reshape(rows.shape))).reshape(tokens, -1)


def ring_index(place, size):
    half = (size + 1) // 2
    back = place // half
    return (1 - back) * (2 * place) + back * (2 * (size - 1 - place) + 1)


def ring_place(index, size):
    odd = index % 2
    return (1 - odd) * (index // 2) + odd * (size - 1 - index // 2)


def ring_neighbours(size):
    place = ring_place(lax.axis_index("fsdp"), size)
    return (
        place,
        ring_index((place + 1) % size, size),
        ring_index((place + size - 1) % size, size),
    )


def greet(partners):
    barrier = pltpu.get_barrier_semaphore()
    for partner in partners:
        pl.semaphore_signal(barrier, inc=1, device_id=partner, device_id_type=MESH)
    pl.semaphore_wait(barrier, len(partners))


def column_cuts(columns):
    cut = (columns // (2 * LANES)) * LANES
    return ((0, cut), (cut, columns - cut))


def plane_count():
    return 2 if lax.axis_size("rep") % 4 == 0 else 1


def rep_partners():
    rep = lax.axis_index("rep")
    core, plane = rep % 2, (rep // 2) % 2
    return rep, core, plane, rep + 1 - 2 * core, rep + 2 - 4 * plane


def plane_columns(columns, planes, plane):
    if planes == 1:
        cuts = column_cuts(columns)
        return (*cuts, cuts[0])
    third = ((columns // LANES + 1) // 3) * LANES
    own = pl.multiple_of(plane * third, LANES)
    other = pl.multiple_of((1 - plane) * third, LANES)
    return (own, third), (2 * third, columns - 2 * third), (other, third)


OWN, BOTH, OTHER = range(3)


def gather_kernel(size, planes, count, *refs):
    shards, wholes = refs[:count], refs[count : 2 * count]
    ring_out, ring_in, core_out, core_in, plane_out, plane_in, local_sem = refs[2 * count :]
    place, right, left = ring_neighbours(size)
    me = lax.axis_index("fsdp")
    rep, core, plane, sibling, across = rep_partners()
    partners = [(rep, right), (rep, left), (sibling, me)]
    greet(partners + ([(across, me)] if planes == 2 else []))

    def piece(ref, array, kind, base):
        rows, columns = shards[array].shape
        by_rows = (rows // 2) % SUBLANES == 0
        width = columns if by_rows else columns // 2
        first, part = plane_columns(width, planes, plane)[kind]
        if by_rows:
            base, height = base + core * (rows // 2), rows // 2
        else:
            first, height = pl.multiple_of(core * width + first, LANES), rows
        return ref.at[pl.ds(pl.multiple_of(base, SUBLANES), height), pl.ds(first, part)]

    def placed(array, kind, step):
        shift = step if kind == BOTH else (size - step)
        owner = ring_index((place + shift) % size, size)
        return piece(wholes[array], array, kind, owner * shards[array].shape[0])

    def ring_copy(array, way, step):
        block = placed(array, way, step)
        return pltpu.make_async_remote_copy(
            src_ref=block if step else piece(shards[array], array, way, 0),
            dst_ref=block,
            send_sem=ring_out.at[array, way, step],
            recv_sem=ring_in.at[array, way, step],
            device_id=(rep, right if way == OWN else left),
            device_id_type=MESH,
        )

    def core_copy(array, kind, step):
        block = placed(array, kind, step + 1)
        return pltpu.make_async_remote_copy(
            src_ref=block,
            dst_ref=block,
            send_sem=core_out.at[array, kind, step],
            recv_sem=core_in.at[array, kind, step],
            device_id=(sibling, me),
            device_id_type=MESH,
        )

    def plane_copy(array, step):
        block = placed(array, OWN, step + 1)
        return pltpu.make_async_remote_copy(
            src_ref=block,
            dst_ref=block,
            send_sem=plane_out.at[array, step],
            recv_sem=plane_in.at[array, step],
            device_id=(across, me),
            device_id_type=MESH,
        )

    def own_copy(array):
        rows = shards[array].shape[0]
        start = pl.multiple_of(me * rows, SUBLANES)
        return pltpu.make_async_copy(
            shards[array], wholes[array].at[pl.ds(start, rows)], local_sem.at[array]
        )

    def hand_over(step):
        for array in range(count):
            plane_copy(array, step).wait_recv()
            core_copy(array, OTHER, step).start()

    pairs = [(array, way) for array in range(count) for way in (OWN, BOTH)]
    for array, way in pairs:
        ring_copy(array, way, 0).start()
    for array in range(count):
        own_copy(array).start()
    for step in range(size - 1):
        for array, way in pairs:
            ring_copy(array, way, step).wait_recv()
            if step < size - 2:
                ring_copy(array, way, step + 1).start()
            if way == OWN and planes == 2:
                plane_copy(array, step).start()
            core_copy(array, way, step).start()
        if planes == 2 and step:
            hand_over(step - 1)
    if planes == 2:
        hand_over(size - 2)
    for array in range(count):
        own_copy(array).wait()
    for step in range(size - 1):
        for array, way in pairs:
            ring_copy(array, way, step).wait_send()
            core_copy(array, way, step).wait()
        if planes == 2:
            for array in range(count):
                plane_copy(array, step).wait_send()
                core_copy(array, OTHER, step).wait()


def gathered(weights, kernel_id):
    size, reps = lax.axis_size("fsdp"), lax.axis_size("rep")
    if size < 3 or reps % 2:
        return [lax.all_gather(weight, "fsdp", axis=0, tiled=True) for weight in weights]
    count, planes = len(weights), plane_count()
    anywhere = pl.BlockSpec(memory_space=pl.ANY)
    copies = [(count, 2), (count, 2), (count, 3), (count, 3), (count,), (count,)]
    semaphores = [pltpu.SemaphoreType.DMA((*shape, size - 1)) for shape in copies]
    return pl.pallas_call(
        functools.partial(gather_kernel, size, planes, count),
        out_shape=[
            jax.ShapeDtypeStruct((size * weight.shape[0], weight.shape[1]), weight.dtype)
            for weight in weights
        ],
        in_specs=[anywhere] * count,
        out_specs=[anywhere] * count,
        scratch_shapes=semaphores + [pltpu.SemaphoreType.DMA((count,))],
        compiler_params=pltpu.CompilerParams(collective_id=kernel_id, has_side_effects=True),
        name="gather_rows",
    )(*weights)


def swapped(array, axis_size, bit):
    return lax.ppermute(array, "rep", [(rank, rank ^ bit) for rank in range(axis_size)])


def paired(axis_size):
    return axis_size > 1 and axis_size & (axis_size - 1) == 0


def rounded(values):
    return lax.reduce_precision(values, 8, 7).astype(jnp.bfloat16)


def flipped(index, bit):
    return index + bit - 2 * bit * ((index // bit) % 2)


def bits_below(size):
    return [1 << power for power in range(size.bit_length() - 1)]


def scatter_kernel(size, reps, planes, wide, late, *refs):
    count = len(wide)
    parts, small, refs = refs[:count], refs[count], refs[count + 1 :]
    sums, small_total, refs = refs[:count], refs[count], refs[count + 1 :]
    slots, ends, refs = refs[: 2 * count], refs[2 * count : 3 * count], refs[3 * count :]
    subtotals, inbox, small_out, small_in = refs[:4]
    ring_out, ring_in, plane_out, plane_in, core_out, core_in = refs[4:]
    place, right, left = ring_neighbours(size)
    me = lax.axis_index("fsdp")
    rep, core, plane, sibling, across = rep_partners()
    exchanges = [(flipped(rep, bit), me) for bit in bits_below(reps)]
    exchanges += [(rep, flipped(me, bit)) for bit in bits_below(size)]
    greet([(rep, right), (rep, left), *exchanges])

    def small_copy(turn):
        return pltpu.make_async_remote_copy(
            src_ref=subtotals.at[turn - 1] if turn else small,
            dst_ref=inbox.at[turn],
            send_sem=small_out.at[turn],
            recv_sem=small_in.at[turn],
            device_id=exchanges[turn],
            device_id_type=MESH,
        )

    def small_take(turn):
        small_copy(turn).wait_recv()
        own = subtotals[turn - 1] if turn else small[...]
        if turn < len(exchanges) - 1:
            subtotals[turn] = own + inbox[turn]
            small_copy(turn + 1).start()
        else:
            small_total[...] = own + inbox[turn]

    def columns(array, way):
        first, width = column_cuts(parts[array].shape[2])[way]
        return pl.ds(first, width)

    def part(array, way, step):
        shift = (size - 1 - step) if way == 0 else (1 + step)
        owner = ring_index((place + shift) % size, size)
        return parts[array].at[owner, :, columns(array, way)]

    def slot(array, way, step):
        return slots[2 * array + way].at[step]

    def ring_copy(array, way, step):
        return pltpu.make_async_remote_copy(
            src_ref=slot(array, way, step - 1) if step else part(array, way, 0),
            dst_ref=slot(array, way, step),
            send_sem=ring_out.at[array, way, step],
            recv_sem=ring_in.at[array, way, step],
            device_id=(rep, right if way == 0 else left),
            device_id_type=MESH,
        )

    def result(array, second=False):
        if not wide[array]:
            return sums[array].at[core]
        return sums[array].at[2 * ((1 - plane) if second else plane) + core]

    def added_over_planes(array):
        return planes == 2 and not wide[array]

    def plane_copy(array):
        added = added_over_planes(array)
        return pltpu.make_async_remote_copy(
            src_ref=ends[array].at[0] if added else result(array),
            dst_ref=ends[array].at[1] if added else result(array),
            send_sem=plane_out.at[array],
            recv_sem=plane_in.at[array],
            device_id=(across, me),
            device_id_type=MESH,
        )

    def core_copy(array, second=False):
        block = result(array, second)
        return pltpu.make_async_remote_copy(
            src_ref=block,
            dst_ref=block,
            send_sem=core_out.at[array, int(second)],
            recv_sem=core_in.at[array, int(second)],
            device_id=(sibling, me),
            device_id_type=MESH,
        )

    def take(array, way, step):
        ring_copy(array, way, step).wait_recv()
        arrived, here = slot(array, way, step), part(array, way, step + 1)
        total = arrived[...].astype(jnp.float32) + here[...].astype(jnp.float32)
        total = total.astype(arrived.dtype)
        if step < size - 2:
            arrived[...] = total
            ring_copy(array, way, step + 1).start()
        elif added_over_planes(array):
            ends[array][0, :, columns(array, way)] = total
        else:
            index = 2 * plane + core if wide[array] else core
            sums[array][index, :, columns(array, way)] = total

    def hand_out(array):
        if planes == 2:
            plane_copy(array).start()
        if not added_over_planes(array):
            core_copy(array).start()

    def finish(array):
        if planes == 1:
            return
        plane_copy(array).wait_recv()
        if wide[array]:
            core_copy(array, True).start()
            return
        both = ends[array][0].astype(jnp.float32) + ends[array][1].astype(jnp.float32)
        sums[array][core] = both.astype(sums[array].dtype)
        core_copy(array).start()

    pairs = [(array, way) for array in range(count) for way in range(2)]
    for array, way in pairs:
        if late[array] == 0:
            ring_copy(array, way, 0).start()
    small_copy(0).start()
    for turn in range(max(size + max(late) + 1, len(exchanges))):
        for array in range(count):
            step = turn - late[array]
            for way in range(2):
                if step == -1:
                    ring_copy(array, way, 0).start()
                if 0 <= step < size - 1:
                    take(array, way, step)
            if step == size - 2:
                hand_out(array)
            if step == size:
                finish(array)
        if turn < len(exchanges):
            small_take(turn)
    for turn in range(len(exchanges)):
        small_copy(turn).wait_send()
    for array in range(count):
        for way in range(2):
            for step in range(size - 1):
                ring_copy(array, way, step).wait_send()
        core_copy(array).wait()
        if planes == 2:
            plane_copy(array).wait_send()
            if wide[array]:
                core_copy(array, True).wait()


def scattered(parts, small, wide, late, kernel_id):
    size, reps, planes = lax.axis_size("fsdp"), lax.axis_size("rep"), plane_count()
    rounds = len(bits_below(size)) + len(bits_below(reps))
    count = len(parts)
    on_chip = pl.BlockSpec(memory_space=pltpu.VMEM)
    slots = [
        pltpu.VMEM((size - 1, part.shape[1], width), part.dtype)
        for part in parts
        for _, width in column_cuts(part.shape[2])
    ]
    ends = [
        pltpu.VMEM((2, SUBLANES, LANES) if spread else (2, *part.shape[1:]), part.dtype)
        for part, spread in zip(parts, wide)
    ]
    copies = [(count, 2, size - 1)] * 2 + [(count,)] * 2 + [(count, 2)] * 2
    return pl.pallas_call(
        functools.partial(scatter_kernel, size, reps, planes, wide, late),
        out_shape=[
            jax.ShapeDtypeStruct((4 if spread else 2, *part.shape[1:]), part.dtype)
            for part, spread in zip(parts, wide)
        ]
        + [jax.ShapeDtypeStruct(small.shape, small.dtype)],
        in_specs=[on_chip] * (count + 1),
        out_specs=[on_chip] * (count + 1),
        scratch_shapes=slots
        + ends
        + [pltpu.VMEM((rounds, *small.shape), small.dtype)] * 2
        + [pltpu.SemaphoreType.DMA((rounds,))] * 2
        + [pltpu.SemaphoreType.DMA(shape) for shape in copies],
        compiler_params=pltpu.CompilerParams(
            collective_id=kernel_id, has_side_effects=True, vmem_limit_bytes=VMEM_BYTES
        ),
        name="scatter_sums",
    )(*parts, small)


def ringed():
    size = lax.axis_size("fsdp")
    return size > 2 and paired(size) and paired(lax.axis_size("rep"))


def met(mine, theirs, bit):
    return jnp.concatenate([mine, swapped(theirs, lax.axis_size("rep"), bit)], axis=0)


def dealt(rows, bits):
    size = lax.axis_size("fsdp")
    for bit in bits:
        tokens, features = rows.shape
        split = rows.reshape(tokens, size, 2, features // (2 * size))
        first = split[:, :, 0].reshape(tokens, features // 2)
        second = split[:, :, 1].reshape(tokens, features // 2)
        even = (lax.axis_index("rep") // bit) % 2 == 0
        rows = met(jnp.where(even, first, second), jnp.where(even, second, first), bit)
    return rows


def met_all(rows, bits):
    for bit in bits:
        rows = met(rows, rows, bit)
    return rows


def owner_parts(lefts, rights, bits):
    size = lax.axis_size("fsdp")
    if not ringed():
        return [product_left(left, right).astype(jnp.bfloat16) for left, right in zip(lefts, rights)]
    dealt_lefts, parts = {}, []
    for left, right in zip(lefts, rights):
        if id(left) not in dealt_lefts:
            dealt_lefts[id(left)] = dealt(left, bits)
        part = product_left(dealt_lefts[id(left)], met_all(right, bits)).astype(jnp.bfloat16)
        parts.append(part.reshape(size, part.shape[0] // size, part.shape[1]))
    return parts


def all_sums(ffn_parts, mix_parts, flat, kernel_id):
    parts, reps = mix_parts + ffn_parts, lax.axis_size("rep")
    if not ringed():
        totals = [lax.psum_scatter(part, "fsdp", scatter_dimension=0, tiled=True) for part in parts]
        totals = [lax.psum(rows, "rep").astype(jnp.float32) for rows in totals]
        return totals, lax.psum(flat, ("rep", "fsdp"))
    wide = [False] * len(mix_parts) + [plane_count() == 2] * len(ffn_parts)
    late = [0] * len(mix_parts) + [LATE_STEPS] * len(ffn_parts)
    tile = 8 * LANES
    small = jnp.pad(flat, (0, -flat.size % tile)).reshape(-1, LANES)
    *summed, small = scattered(parts, small, wide, late, kernel_id)
    totals = []
    for own in summed:
        own = own.reshape(-1, own.shape[2])
        bit = 2 * plane_count()
        while bit < reps:
            own = rounded(own.astype(jnp.float32) + swapped(own, reps, bit).astype(jnp.float32))
            bit = 2 * bit
        totals.append(own.astype(jnp.float32))
    return totals, small.reshape(-1)[: flat.size]


def column_parts(array, widths):
    parts, start = [], 0
    for width in widths:
        parts.append(array[:, start : start + width])
        start = start + width
    return parts


def local(
    block_input,
    cotangent,
    doc_lengths,
    gain_mix,
    w_query,
    w_key,
    w_value,
    w_gate,
    w_decay,
    w_write,
    conv_query,
    conv_key,
    conv_value,
    decay_log,
    decay_bias,
    out_gain,
    w_out,
    gain_ffn,
    w_hidden,
    w_up,
    w_down,
):
    tokens = block_input.shape[0]
    segment = doc_segments(doc_lengths[0], tokens)
    head_count = decay_log.shape[0]
    narrow_widths = [w_query.shape[1], head_count, head_count]
    spare = -sum(narrow_widths) % LANES
    narrow = jnp.concatenate([w_query, w_decay, w_write], axis=1)
    narrow = jnp.pad(narrow, ((0, 0), (0, spare)))
    mixing = gathered([narrow, w_key, w_value, w_gate], 0)
    outward, hidden, up, downward = gathered([w_out, w_hidden, w_up, w_down], 1)
    upstream = cotangent.astype(jnp.bfloat16)

    normed, norm_back = jax.vjp(rms_norm, block_input, gain_mix)
    first_input = normed.astype(jnp.bfloat16)
    narrow_proj, key_proj, value_proj, gate_proj = [
        product(first_input, weight) for weight in mixing
    ]
    query_proj, decay_proj, write_proj = column_parts(narrow_proj, narrow_widths)

    def rows_of(maker):
        return lambda proj, kernel: maker(proj, kernel, segment, head_count)

    queries, query_back = jax.vjp(rows_of(query_rows_of), query_proj, conv_query)
    key_rows, key_back = jax.vjp(rows_of(unit_rows), key_proj, conv_key)
    value_rows, value_back = jax.vjp(rows_of(conv_rows), value_proj, conv_value)
    (decays, strength), gates_back = jax.vjp(
        head_gates, decay_proj, write_proj, decay_log, decay_bias
    )
    readout, readout_back = jax.vjp(
        lambda *operands: delta_rule(*operands, segment),
        queries,
        key_rows,
        value_rows,
        decays,
        strength,
    )
    mixed_out, mixed_back = jax.vjp(gated_norm, readout, gate_proj, out_gain)
    gated_out = mixed_out.astype(jnp.bfloat16)
    residual = block_input + product(gated_out, outward)
    normed_ffn, norm_ffn_back = jax.vjp(rms_norm, residual, gain_ffn)
    second = normed_ffn.astype(jnp.bfloat16)
    swiglu_out, swiglu_back = jax.vjp(swiglu, product(second, hidden), product(second, up))
    activation = swiglu_out.astype(jnp.bfloat16)
    block_out = residual + product(activation, downward)
    d_hidden, d_up = [
        grad.astype(jnp.bfloat16) for grad in swiglu_back(product_right(upstream, downward))
    ]
    d_second = product_right(d_hidden, hidden) + product_right(d_up, up)
    ffn_parts = owner_parts(
        [activation, second, second],
        [upstream, d_hidden, d_up],
        (2, 1) if plane_count() == 2 else (1,),
    )
    d_norm_ffn, grad_gain_ffn = norm_ffn_back(d_second)
    d_residual = cotangent + d_norm_ffn
    upstream_mix = d_residual.astype(jnp.bfloat16)
    d_mixed = product_right(upstream_mix, outward)
    d_readout, d_gate, grad_out_gain = mixed_back(d_mixed)
    d_queries, d_keys, d_values, d_decays, d_strength = readout_back(d_readout)
    d_value, grad_conv_value = value_back(d_values)
    d_query, grad_conv_query = query_back(d_queries)
    d_key, grad_conv_key = key_back(d_keys)
    d_decay, d_write, grad_decay_log, grad_decay_bias = gates_back((d_decays, d_strength))
    d_narrow = jnp.concatenate([d_query, d_decay, d_write], axis=1).astype(jnp.bfloat16)
    d_narrow = jnp.pad(d_narrow, ((0, 0), (0, spare)))
    d_mix = [d_narrow, *(rows.astype(jnp.bfloat16) for rows in (d_key, d_value, d_gate))]
    mix_parts = owner_parts([gated_out] + [first_input] * 4, [upstream_mix] + d_mix, (1,))
    d_first = sum(product_right(rows, weight) for rows, weight in zip(d_mix, mixing))
    d_norm, grad_gain_mix = norm_back(d_first)
    input_grad = d_residual + d_norm
    small = (
        grad_gain_mix,
        grad_conv_query,
        grad_conv_key,
        grad_conv_value,
        grad_decay_log,
        grad_decay_bias,
        grad_out_gain,
        grad_gain_ffn,
    )
    flat = jnp.concatenate([grad.reshape(-1) for grad in small])
    sums, flat = all_sums(ffn_parts, mix_parts, flat, 2)
    grad_out, grad_narrow, grad_key, grad_value, grad_gate = sums[:5]
    grad_down, grad_hidden, grad_up = sums[5:]
    grad_query, grad_decay, grad_write = column_parts(grad_narrow, narrow_widths)
    small_totals, start = [], 0
    for grad in small:
        small_totals.append(flat[start : start + grad.size].reshape(grad.shape))
        start = start + grad.size
    return (
        block_out,
        input_grad,
        small_totals[0],
        grad_query,
        grad_key,
        grad_value,
        grad_gate,
        grad_decay,
        grad_write,
        *small_totals[1:7],
        grad_out,
        small_totals[7],
        grad_hidden,
        grad_up,
        grad_down,
    )


def solution(mesh):
    placed = (
        P(("rep", "fsdp"), None),
        P(("rep", "fsdp"), None),
        P(("rep", "fsdp"), None),
        P(),
        P("fsdp", None),
        P("fsdp", None),
        P("fsdp", None),
        P("fsdp", None),
        P("fsdp", None),
        P("fsdp", None),
        P(),
        P(),
        P(),
        P(),
        P(),
        P(),
        P("fsdp", None),
        P(),
        P("fsdp", None),
        P("fsdp", None),
        P("fsdp", None),
    )
    return jax.shard_map(
        local,
        mesh=mesh,
        in_specs=placed,
        out_specs=(
            P(("rep", "fsdp"), None),
            P(("rep", "fsdp"), None),
            P(),
            P("fsdp", None),
            P("fsdp", None),
            P("fsdp", None),
            P("fsdp", None),
            P("fsdp", None),
            P("fsdp", None),
            P(),
            P(),
            P(),
            P(),
            P(),
            P(),
            P("fsdp", None),
            P(),
            P("fsdp", None),
            P("fsdp", None),
            P("fsdp", None),
        ),
        check_vma=False,
    )
```

```python
import functools

import jax
import jax.numpy as jnp
from jax import lax
from jax.experimental import pallas as pl
from jax.experimental.pallas import tpu as pltpu
from jax.sharding import PartitionSpec as P

EPSILON = 1e-06
TOP_PRECISION = lax.Precision.HIGHEST
MIX_PRECISION = lax.Precision.HIGH
LANES = 128
SUBLANES = 16
LATE_STEPS = 3
VMEM_BYTES = 48 * 1024 * 1024
MESH = pl.DeviceIdType.MESH


def product(left, right):
    return jnp.dot(left, right, preferred_element_type=jnp.float32)


def product_left(left, right):
    return lax.dot_general(
        left, right, (((0,), (0,)), ((), ())), preferred_element_type=jnp.float32
    )


def product_right(left, right):
    return lax.dot_general(
        left, right, (((1,), (1,)), ((), ())), preferred_element_type=jnp.float32
    )


def rms_norm(values, gain):
    return values * lax.rsqrt(jnp.mean(values * values, axis=-1, keepdims=True) + EPSILON) * gain


def swiglu(hidden_pre, up_pre):
    return jax.nn.silu(hidden_pre) * up_pre


def doc_segments(lengths, tokens):
    order = jnp.arange(lengths.shape[0], dtype=jnp.int32)
    upto = order[None, :] <= order[:, None]
    doc_ends = jnp.sum(jnp.where(upto, lengths[None, :], 0), axis=1)
    positions = jnp.arange(tokens, dtype=jnp.int32)
    return jnp.sum((positions[:, None] >= doc_ends[None, :]).astype(jnp.int32), axis=1)


def shifted(values, offset, fill):
    filler = jnp.full((offset,) + values.shape[1:], fill, values.dtype)
    return jnp.concatenate([filler, values[:-offset]], axis=0)


def short_conv(values, kernel, segment):
    summed = values * kernel[0]
    for offset in range(1, kernel.shape[0]):
        same_doc = (shifted(segment, offset, -1) == segment).astype(values.dtype)
        summed = summed + shifted(values, offset, 0.0) * kernel[offset] * same_doc[:, None]
    return summed


def unit_inverse(lower_part):
    width = lower_part.shape[-1]
    index = jnp.arange(width, dtype=jnp.int32)
    inverse = None
    size = 1
    while size < width:
        rows, columns = index[:, None] // size, index[None, :] // size
        pairs = (rows % 2 == 1) & (columns == rows - 1)
        level = jnp.where(pairs[None], lower_part, 0.0)
        if inverse is None:
            inverse = jnp.eye(width, dtype=lower_part.dtype)[None] - level
        else:
            step = jnp.einsum("hij,hjk->hik", level, inverse, precision=MIX_PRECISION)
            inverse = inverse - jnp.einsum("hij,hjk->hik", inverse, step, precision=MIX_PRECISION)
        size = 2 * size
    return inverse


@jax.custom_vjp
def unit_solve(lower_part, sources):
    return jnp.einsum("hij,hjv->hiv", unit_inverse(lower_part), sources, precision=MIX_PRECISION)


def unit_solve_fwd(lower_part, sources):
    inverse = unit_inverse(lower_part)
    solved = jnp.einsum("hij,hjv->hiv", inverse, sources, precision=MIX_PRECISION)
    return solved, (inverse, solved)


def unit_solve_bwd(saved, d_solved):
    inverse, solved = saved
    d_sources = jnp.einsum("hji,hjv->hiv", inverse, d_solved, precision=MIX_PRECISION)
    d_lower = -jnp.einsum("hiv,hjv->hij", d_sources, solved, precision=MIX_PRECISION)
    return d_lower, d_sources


unit_solve.defvjp(unit_solve_fwd, unit_solve_bwd)


def delta_rule(query_rows, key_matrix, value_rows, decays, strength, segment):
    width = segment.shape[0]
    positions = jnp.arange(width, dtype=jnp.int32)
    same_doc = segment[:, None] == segment[None, :]
    lower_mask = same_doc & (positions[:, None] >= positions[None, :])
    strict_mask = same_doc & (positions[:, None] > positions[None, :])
    cumulative = jnp.einsum(
        "ij,hj->hi", lower_mask.astype(decays.dtype), decays, precision=TOP_PRECISION
    )
    spread = jnp.minimum(cumulative[:, :, None] - cumulative[:, None, :], 0.0)
    ratios = jnp.where(lower_mask[None], jnp.exp(spread), 0.0)
    key_inner = jnp.einsum("hid,hjd->hij", key_matrix, key_matrix, precision=MIX_PRECISION)
    lower_part = jnp.where(strict_mask[None], strength[:, :, None] * ratios * key_inner, 0.0)
    delta_rows = unit_solve(lower_part, strength[:, :, None] * value_rows)
    scores = jnp.einsum("hid,hjd->hij", query_rows, key_matrix, precision=MIX_PRECISION) * ratios
    return jnp.einsum("hij,hjv->hiv", scores, delta_rows, precision=MIX_PRECISION)


def conv_rows(proj, kernel, segment, head_count):
    rows = jax.nn.silu(short_conv(proj, kernel, segment))
    return jnp.swapaxes(rows.reshape(proj.shape[0], head_count, -1), 0, 1)


def unit_rows(proj, kernel, segment, head_count):
    rows = conv_rows(proj, kernel, segment, head_count)
    return rows * lax.rsqrt(jnp.sum(rows * rows, axis=2, keepdims=True) + EPSILON)


def query_rows_of(proj, kernel, segment, head_count):
    rows = unit_rows(proj, kernel, segment, head_count)
    return rows * rows.shape[2] ** (-0.5)


def head_gates(decay_proj, write_proj, decay_log, decay_bias):
    decays = -jnp.exp(decay_log) * jax.nn.softplus(decay_proj + decay_bias)
    return decays.T, jax.nn.sigmoid(write_proj).T


def gated_norm(readout_rows, gate_proj, out_gain):
    tokens = gate_proj.shape[0]
    rows = jnp.swapaxes(readout_rows, 0, 1)
    rows = rows * lax.rsqrt(jnp.mean(rows * rows, axis=2, keepdims=True) + EPSILON) * out_gain
    return (rows * jax.nn.silu(gate_proj.reshape(rows.shape))).reshape(tokens, -1)


def ring_index(place, size):
    half = (size + 1) // 2
    back = place // half
    return (1 - back) * (2 * place) + back * (2 * (size - 1 - place) + 1)


def ring_place(index, size):
    odd = index % 2
    return (1 - odd) * (index // 2) + odd * (size - 1 - index // 2)


def ring_neighbours(size):
    place = ring_place(lax.axis_index("fsdp"), size)
    return (
        place,
        ring_index((place + 1) % size, size),
        ring_index((place + size - 1) % size, size),
    )


def greet(partners):
    barrier = pltpu.get_barrier_semaphore()
    for partner in partners:
        pl.semaphore_signal(barrier, inc=1, device_id=partner, device_id_type=MESH)
    pl.semaphore_wait(barrier, len(partners))


def column_cuts(columns):
    cut = (columns // (2 * LANES)) * LANES
    return ((0, cut), (cut, columns - cut))


def plane_count():
    return 2 if lax.axis_size("rep") % 4 == 0 else 1


def rep_partners():
    rep = lax.axis_index("rep")
    core, plane = rep % 2, (rep // 2) % 2
    return rep, core, plane, rep + 1 - 2 * core, rep + 2 - 4 * plane


def plane_columns(columns, planes, plane):
    if planes == 1:
        cuts = column_cuts(columns)
        return (*cuts, cuts[0])
    third = ((columns // LANES + 1) // 3) * LANES
    own = pl.multiple_of(plane * third, LANES)
    other = pl.multiple_of((1 - plane) * third, LANES)
    return (own, third), (2 * third, columns - 2 * third), (other, third)


OWN, BOTH, OTHER = range(3)


def gather_kernel(size, planes, count, *refs):
    shards, wholes = refs[:count], refs[count : 2 * count]
    ring_out, ring_in, core_out, core_in, plane_out, plane_in, local_sem = refs[2 * count :]
    place, right, left = ring_neighbours(size)
    me = lax.axis_index("fsdp")
    rep, core, plane, sibling, across = rep_partners()
    partners = [(rep, right), (rep, left), (sibling, me)]
    greet(partners + ([(across, me)] if planes == 2 else []))

    def piece(ref, array, kind, base):
        rows, columns = shards[array].shape
        by_rows = (rows // 2) % SUBLANES == 0
        width = columns if by_rows else columns // 2
        first, part = plane_columns(width, planes, plane)[kind]
        if by_rows:
            base, height = base + core * (rows // 2), rows // 2
        else:
            first, height = pl.multiple_of(core * width + first, LANES), rows
        return ref.at[pl.ds(pl.multiple_of(base, SUBLANES), height), pl.ds(first, part)]

    def placed(array, kind, step):
        shift = step if kind == BOTH else (size - step)
        owner = ring_index((place + shift) % size, size)
        return piece(wholes[array], array, kind, owner * shards[array].shape[0])

    def ring_copy(array, way, step):
        block = placed(array, way, step)
        return pltpu.make_async_remote_copy(
            src_ref=block if step else piece(shards[array], array, way, 0),
            dst_ref=block,
            send_sem=ring_out.at[array, way, step],
            recv_sem=ring_in.at[array, way, step],
            device_id=(rep, right if way == OWN else left),
            device_id_type=MESH,
        )

    def core_copy(array, kind, step):
        block = placed(array, kind, step + 1)
        return pltpu.make_async_remote_copy(
            src_ref=block,
            dst_ref=block,
            send_sem=core_out.at[array, kind, step],
            recv_sem=core_in.at[array, kind, step],
            device_id=(sibling, me),
            device_id_type=MESH,
        )

    def plane_copy(array, step):
        block = placed(array, OWN, step + 1)
        return pltpu.make_async_remote_copy(
            src_ref=block,
            dst_ref=block,
            send_sem=plane_out.at[array, step],
            recv_sem=plane_in.at[array, step],
            device_id=(across, me),
            device_id_type=MESH,
        )

    def own_copy(array):
        rows = shards[array].shape[0]
        start = pl.multiple_of(me * rows, SUBLANES)
        return pltpu.make_async_copy(
            shards[array], wholes[array].at[pl.ds(start, rows)], local_sem.at[array]
        )

    def hand_over(step):
        for array in range(count):
            plane_copy(array, step).wait_recv()
            core_copy(array, OTHER, step).start()

    pairs = [(array, way) for array in range(count) for way in (OWN, BOTH)]
    for array, way in pairs:
        ring_copy(array, way, 0).start()
    for array in range(count):
        own_copy(array).start()
    for step in range(size - 1):
        for array, way in pairs:
            ring_copy(array, way, step).wait_recv()
            if step < size - 2:
                ring_copy(array, way, step + 1).start()
            if way == OWN and planes == 2:
                plane_copy(array, step).start()
            core_copy(array, way, step).start()
        if planes == 2 and step:
            hand_over(step - 1)
    if planes == 2:
        hand_over(size - 2)
    for array in range(count):
        own_copy(array).wait()
    for step in range(size - 1):
        for array, way in pairs:
            ring_copy(array, way, step).wait_send()
            core_copy(array, way, step).wait()
        if planes == 2:
            for array in range(count):
                plane_copy(array, step).wait_send()
                core_copy(array, OTHER, step).wait()


def gathered(weights, kernel_id):
    size, reps = lax.axis_size("fsdp"), lax.axis_size("rep")
    if size < 3 or reps % 2:
        return [lax.all_gather(weight, "fsdp", axis=0, tiled=True) for weight in weights]
    count, planes = len(weights), plane_count()
    anywhere = pl.BlockSpec(memory_space=pl.ANY)
    copies = [(count, 2), (count, 2), (count, 3), (count, 3), (count,), (count,)]
    semaphores = [pltpu.SemaphoreType.DMA((*shape, size - 1)) for shape in copies]
    return pl.pallas_call(
        functools.partial(gather_kernel, size, planes, count),
        out_shape=[
            jax.ShapeDtypeStruct((size * weight.shape[0], weight.shape[1]), weight.dtype)
            for weight in weights
        ],
        in_specs=[anywhere] * count,
        out_specs=[anywhere] * count,
        scratch_shapes=semaphores + [pltpu.SemaphoreType.DMA((count,))],
        compiler_params=pltpu.CompilerParams(collective_id=kernel_id, has_side_effects=True),
        name="gather_rows",
    )(*weights)


def swapped(array, axis_size, bit):
    return lax.ppermute(array, "rep", [(rank, rank ^ bit) for rank in range(axis_size)])


def paired(axis_size):
    return axis_size > 1 and axis_size & (axis_size - 1) == 0


def rounded(values):
    return lax.reduce_precision(values, 8, 7).astype(jnp.bfloat16)


def flipped(index, bit):
    return index + bit - 2 * bit * ((index // bit) % 2)


def bits_below(size):
    return [1 << power for power in range(size.bit_length() - 1)]


def scatter_kernel(size, reps, planes, wide, late, *refs):
    count = len(wide)
    parts, small, refs = refs[:count], refs[count], refs[count + 1 :]
    sums, small_total, refs = refs[:count], refs[count], refs[count + 1 :]
    slots, ends, refs = refs[: 2 * count], refs[2 * count : 3 * count], refs[3 * count :]
    subtotals, inbox, small_out, small_in = refs[:4]
    ring_out, ring_in, plane_out, plane_in, core_out, core_in = refs[4:]
    place, right, left = ring_neighbours(size)
    me = lax.axis_index("fsdp")
    rep, core, plane, sibling, across = rep_partners()
    exchanges = [(flipped(rep, bit), me) for bit in bits_below(reps)]
    exchanges += [(rep, flipped(me, bit)) for bit in bits_below(size)]
    greet([(rep, right), (rep, left), *exchanges])

    def small_copy(turn):
        return pltpu.make_async_remote_copy(
            src_ref=subtotals.at[turn - 1] if turn else small,
            dst_ref=inbox.at[turn],
            send_sem=small_out.at[turn],
            recv_sem=small_in.at[turn],
            device_id=exchanges[turn],
            device_id_type=MESH,
        )

    def small_take(turn):
        small_copy(turn).wait_recv()
        own = subtotals[turn - 1] if turn else small[...]
        if turn < len(exchanges) - 1:
            subtotals[turn] = own + inbox[turn]
            small_copy(turn + 1).start()
        else:
            small_total[...] = own + inbox[turn]

    def columns(array, way):
        first, width = column_cuts(parts[array].shape[2])[way]
        return pl.ds(first, width)

    def part(array, way, step):
        shift = (size - 1 - step) if way == 0 else (1 + step)
        owner = ring_index((place + shift) % size, size)
        return parts[array].at[owner, :, columns(array, way)]

    def slot(array, way, step):
        return slots[2 * array + way].at[step]

    def ring_copy(array, way, step):
        return pltpu.make_async_remote_copy(
            src_ref=slot(array, way, step - 1) if step else part(array, way, 0),
            dst_ref=slot(array, way, step),
            send_sem=ring_out.at[array, way, step],
            recv_sem=ring_in.at[array, way, step],
            device_id=(rep, right if way == 0 else left),
            device_id_type=MESH,
        )

    def result(array, second=False):
        if not wide[array]:
            return sums[array].at[core]
        return sums[array].at[2 * ((1 - plane) if second else plane) + core]

    def added_over_planes(array):
        return planes == 2 and not wide[array]

    def plane_copy(array):
        added = added_over_planes(array)
        return pltpu.make_async_remote_copy(
            src_ref=ends[array].at[0] if added else result(array),
            dst_ref=ends[array].at[1] if added else result(array),
            send_sem=plane_out.at[array],
            recv_sem=plane_in.at[array],
            device_id=(across, me),
            device_id_type=MESH,
        )

    def core_copy(array, second=False):
        block = result(array, second)
        return pltpu.make_async_remote_copy(
            src_ref=block,
            dst_ref=block,
            send_sem=core_out.at[array, int(second)],
            recv_sem=core_in.at[array, int(second)],
            device_id=(sibling, me),
            device_id_type=MESH,
        )

    def take(array, way, step):
        ring_copy(array, way, step).wait_recv()
        arrived, here = slot(array, way, step), part(array, way, step + 1)
        total = arrived[...].astype(jnp.float32) + here[...].astype(jnp.float32)
        total = total.astype(arrived.dtype)
        if step < size - 2:
            arrived[...] = total
            ring_copy(array, way, step + 1).start()
        elif added_over_planes(array):
            ends[array][0, :, columns(array, way)] = total
        else:
            index = 2 * plane + core if wide[array] else core
            sums[array][index, :, columns(array, way)] = total

    def hand_out(array):
        if planes == 2:
            plane_copy(array).start()
        if not added_over_planes(array):
            core_copy(array).start()

    def finish(array):
        if planes == 1:
            return
        plane_copy(array).wait_recv()
        if wide[array]:
            core_copy(array, True).start()
            return
        both = ends[array][0].astype(jnp.float32) + ends[array][1].astype(jnp.float32)
        sums[array][core] = both.astype(sums[array].dtype)
        core_copy(array).start()

    pairs = [(array, way) for array in range(count) for way in range(2)]
    for array, way in pairs:
        if late[array] == 0:
            ring_copy(array, way, 0).start()
    small_copy(0).start()
    for turn in range(max(size + max(late) + 1, len(exchanges))):
        for array in range(count):
            step = turn - late[array]
            for way in range(2):
                if step == -1:
                    ring_copy(array, way, 0).start()
                if 0 <= step < size - 1:
                    take(array, way, step)
            if step == size - 2:
                hand_out(array)
            if turn == size - 1 + max(late) + (late[array] > 0):
                finish(array)
        if turn < len(exchanges):
            small_take(turn)
    for turn in range(len(exchanges)):
        small_copy(turn).wait_send()
    for array in range(count):
        for way in range(2):
            for step in range(size - 1):
                ring_copy(array, way, step).wait_send()
        core_copy(array).wait()
        if planes == 2:
            plane_copy(array).wait_send()
            if wide[array]:
                core_copy(array, True).wait()


def scattered(parts, small, wide, late, kernel_id):
    size, reps, planes = lax.axis_size("fsdp"), lax.axis_size("rep"), plane_count()
    rounds = len(bits_below(size)) + len(bits_below(reps))
    count = len(parts)
    on_chip = pl.BlockSpec(memory_space=pltpu.VMEM)
    slots = [
        pltpu.VMEM((size - 1, part.shape[1], width), part.dtype)
        for part in parts
        for _, width in column_cuts(part.shape[2])
    ]
    ends = [
        pltpu.VMEM((2, SUBLANES, LANES) if spread else (2, *part.shape[1:]), part.dtype)
        for part, spread in zip(parts, wide)
    ]
    copies = [(count, 2, size - 1)] * 2 + [(count,)] * 2 + [(count, 2)] * 2
    return pl.pallas_call(
        functools.partial(scatter_kernel, size, reps, planes, wide, late),
        out_shape=[
            jax.ShapeDtypeStruct((4 if spread else 2, *part.shape[1:]), part.dtype)
            for part, spread in zip(parts, wide)
        ]
        + [jax.ShapeDtypeStruct(small.shape, small.dtype)],
        in_specs=[on_chip] * (count + 1),
        out_specs=[on_chip] * (count + 1),
        scratch_shapes=slots
        + ends
        + [pltpu.VMEM((rounds, *small.shape), small.dtype)] * 2
        + [pltpu.SemaphoreType.DMA((rounds,))] * 2
        + [pltpu.SemaphoreType.DMA(shape) for shape in copies],
        compiler_params=pltpu.CompilerParams(
            collective_id=kernel_id, has_side_effects=True, vmem_limit_bytes=VMEM_BYTES
        ),
        name="scatter_sums",
    )(*parts, small)


def ringed():
    size = lax.axis_size("fsdp")
    return size > 2 and paired(size) and paired(lax.axis_size("rep"))


def met(mine, theirs, bit):
    return jnp.concatenate([mine, swapped(theirs, lax.axis_size("rep"), bit)], axis=0)


def dealt(rows, bits):
    size = lax.axis_size("fsdp")
    for bit in bits:
        tokens, features = rows.shape
        split = rows.reshape(tokens, size, 2, features // (2 * size))
        first = split[:, :, 0].reshape(tokens, features // 2)
        second = split[:, :, 1].reshape(tokens, features // 2)
        even = (lax.axis_index("rep") // bit) % 2 == 0
        rows = met(jnp.where(even, first, second), jnp.where(even, second, first), bit)
    return rows


def met_all(rows, bits):
    for bit in bits:
        rows = met(rows, rows, bit)
    return rows


def owner_parts(lefts, rights, bits):
    size = lax.axis_size("fsdp")
    if not ringed():
        return [product_left(left, right).astype(jnp.bfloat16) for left, right in zip(lefts, rights)]
    dealt_lefts, parts = {}, []
    for left, right in zip(lefts, rights):
        if id(left) not in dealt_lefts:
            dealt_lefts[id(left)] = dealt(left, bits)
        part = product_left(dealt_lefts[id(left)], met_all(right, bits)).astype(jnp.bfloat16)
        parts.append(part.reshape(size, part.shape[0] // size, part.shape[1]))
    return parts


def all_sums(ffn_parts, mix_parts, flat, kernel_id):
    parts, reps = mix_parts + ffn_parts, lax.axis_size("rep")
    if not ringed():
        totals = [lax.psum_scatter(part, "fsdp", scatter_dimension=0, tiled=True) for part in parts]
        totals = [lax.psum(rows, "rep").astype(jnp.float32) for rows in totals]
        return totals, lax.psum(flat, ("rep", "fsdp"))
    wide = [False] * len(mix_parts) + [plane_count() == 2] * len(ffn_parts)
    late = [0] * len(mix_parts) + [LATE_STEPS] * len(ffn_parts)
    tile = 8 * LANES
    small = jnp.pad(flat, (0, -flat.size % tile)).reshape(-1, LANES)
    *summed, small = scattered(parts, small, wide, late, kernel_id)
    totals = []
    for own in summed:
        own = own.reshape(-1, own.shape[2])
        bit = 2 * plane_count()
        while bit < reps:
            own = rounded(own.astype(jnp.float32) + swapped(own, reps, bit).astype(jnp.float32))
            bit = 2 * bit
        totals.append(own.astype(jnp.float32))
    return totals, small.reshape(-1)[: flat.size]


def column_parts(array, widths):
    parts, start = [], 0
    for width in widths:
        parts.append(array[:, start : start + width])
        start = start + width
    return parts


def local(
    block_input,
    cotangent,
    doc_lengths,
    gain_mix,
    w_query,
    w_key,
    w_value,
    w_gate,
    w_decay,
    w_write,
    conv_query,
    conv_key,
    conv_value,
    decay_log,
    decay_bias,
    out_gain,
    w_out,
    gain_ffn,
    w_hidden,
    w_up,
    w_down,
):
    tokens = block_input.shape[0]
    segment = doc_segments(doc_lengths[0], tokens)
    head_count = decay_log.shape[0]
    narrow_widths = [w_query.shape[1], head_count, head_count]
    spare = -sum(narrow_widths) % LANES
    narrow = jnp.concatenate([w_query, w_decay, w_write], axis=1)
    narrow = jnp.pad(narrow, ((0, 0), (0, spare)))
    mixing = gathered([narrow, w_key, w_value, w_gate], 0)
    outward, hidden, up, downward = gathered([w_out, w_hidden, w_up, w_down], 1)
    upstream = cotangent.astype(jnp.bfloat16)

    normed, norm_back = jax.vjp(rms_norm, block_input, gain_mix)
    first_input = normed.astype(jnp.bfloat16)
    narrow_proj, key_proj, value_proj, gate_proj = [
        product(first_input, weight) for weight in mixing
    ]
    query_proj, decay_proj, write_proj = column_parts(narrow_proj, narrow_widths)

    def rows_of(maker):
        return lambda proj, kernel: maker(proj, kernel, segment, head_count)

    queries, query_back = jax.vjp(rows_of(query_rows_of), query_proj, conv_query)
    key_rows, key_back = jax.vjp(rows_of(unit_rows), key_proj, conv_key)
    value_rows, value_back = jax.vjp(rows_of(conv_rows), value_proj, conv_value)
    (decays, strength), gates_back = jax.vjp(
        head_gates, decay_proj, write_proj, decay_log, decay_bias
    )
    readout, readout_back = jax.vjp(
        lambda *operands: delta_rule(*operands, segment),
        queries,
        key_rows,
        value_rows,
        decays,
        strength,
    )
    mixed_out, mixed_back = jax.vjp(gated_norm, readout, gate_proj, out_gain)
    gated_out = mixed_out.astype(jnp.bfloat16)
    residual = block_input + product(gated_out, outward)
    normed_ffn, norm_ffn_back = jax.vjp(rms_norm, residual, gain_ffn)
    second = normed_ffn.astype(jnp.bfloat16)
    swiglu_out, swiglu_back = jax.vjp(swiglu, product(second, hidden), product(second, up))
    activation = swiglu_out.astype(jnp.bfloat16)
    block_out = residual + product(activation, downward)
    d_hidden, d_up = [
        grad.astype(jnp.bfloat16) for grad in swiglu_back(product_right(upstream, downward))
    ]
    d_second = product_right(d_hidden, hidden) + product_right(d_up, up)
    ffn_parts = owner_parts(
        [activation, second, second],
        [upstream, d_hidden, d_up],
        (2, 1) if plane_count() == 2 else (1,),
    )
    d_norm_ffn, grad_gain_ffn = norm_ffn_back(d_second)
    d_residual = cotangent + d_norm_ffn
    upstream_mix = d_residual.astype(jnp.bfloat16)
    d_mixed = product_right(upstream_mix, outward)
    d_readout, d_gate, grad_out_gain = mixed_back(d_mixed)
    d_queries, d_keys, d_values, d_decays, d_strength = readout_back(d_readout)
    d_value, grad_conv_value = value_back(d_values)
    d_query, grad_conv_query = query_back(d_queries)
    d_key, grad_conv_key = key_back(d_keys)
    d_decay, d_write, grad_decay_log, grad_decay_bias = gates_back((d_decays, d_strength))
    d_narrow = jnp.concatenate([d_query, d_decay, d_write], axis=1).astype(jnp.bfloat16)
    d_narrow = jnp.pad(d_narrow, ((0, 0), (0, spare)))
    d_mix = [d_narrow, *(rows.astype(jnp.bfloat16) for rows in (d_key, d_value, d_gate))]
    mix_parts = owner_parts([gated_out] + [first_input] * 4, [upstream_mix] + d_mix, (1,))
    d_first = sum(product_right(rows, weight) for rows, weight in zip(d_mix, mixing))
    d_norm, grad_gain_mix = norm_back(d_first)
    input_grad = d_residual + d_norm
    small = (
        grad_gain_mix,
        grad_conv_query,
        grad_conv_key,
        grad_conv_value,
        grad_decay_log,
        grad_decay_bias,
        grad_out_gain,
        grad_gain_ffn,
    )
    flat = jnp.concatenate([grad.reshape(-1) for grad in small])
    sums, flat = all_sums(ffn_parts, mix_parts, flat, 2)
    grad_out, grad_narrow, grad_key, grad_value, grad_gate = sums[:5]
    grad_down, grad_hidden, grad_up = sums[5:]
    grad_query, grad_decay, grad_write = column_parts(grad_narrow, narrow_widths)
    small_totals, start = [], 0
    for grad in small:
        small_totals.append(flat[start : start + grad.size].reshape(grad.shape))
        start = start + grad.size
    return (
        block_out,
        input_grad,
        small_totals[0],
        grad_query,
        grad_key,
        grad_value,
        grad_gate,
        grad_decay,
        grad_write,
        *small_totals[1:7],
        grad_out,
        small_totals[7],
        grad_hidden,
        grad_up,
        grad_down,
    )


def solution(mesh):
    placed = (
        P(("rep", "fsdp"), None),
        P(("rep", "fsdp"), None),
        P(("rep", "fsdp"), None),
        P(),
        P("fsdp", None),
        P("fsdp", None),
        P("fsdp", None),
        P("fsdp", None),
        P("fsdp", None),
        P("fsdp", None),
        P(),
        P(),
        P(),
        P(),
        P(),
        P(),
        P("fsdp", None),
        P(),
        P("fsdp", None),
        P("fsdp", None),
        P("fsdp", None),
    )
    return jax.shard_map(
        local,
        mesh=mesh,
        in_specs=placed,
        out_specs=(
            P(("rep", "fsdp"), None),
            P(("rep", "fsdp"), None),
            P(),
            P("fsdp", None),
            P("fsdp", None),
            P("fsdp", None),
            P("fsdp", None),
            P("fsdp", None),
            P("fsdp", None),
            P(),
            P(),
            P(),
            P(),
            P(),
            P(),
            P("fsdp", None),
            P(),
            P("fsdp", None),
            P("fsdp", None),
            P("fsdp", None),
        ),
        check_vma=False,
    )
```

```python
import functools

import jax
import jax.numpy as jnp
from jax import lax
from jax.experimental import pallas as pl
from jax.experimental.pallas import tpu as pltpu
from jax.sharding import PartitionSpec as P

EPSILON = 1e-06
TOP_PRECISION = lax.Precision.HIGHEST
MIX_PRECISION = lax.Precision.HIGH
LANES = 128
SUBLANES = 16
LATE_STEPS = 3
VMEM_BYTES = 48 * 1024 * 1024
MESH = pl.DeviceIdType.MESH


def product(left, right):
    return jnp.dot(left, right, preferred_element_type=jnp.float32)


def product_left(left, right):
    return lax.dot_general(
        left, right, (((0,), (0,)), ((), ())), preferred_element_type=jnp.float32
    )


def product_right(left, right):
    return lax.dot_general(
        left, right, (((1,), (1,)), ((), ())), preferred_element_type=jnp.float32
    )


def rms_norm(values, gain):
    return values * lax.rsqrt(jnp.mean(values * values, axis=-1, keepdims=True) + EPSILON) * gain


def swiglu(hidden_pre, up_pre):
    return jax.nn.silu(hidden_pre) * up_pre


def doc_segments(lengths, tokens):
    order = jnp.arange(lengths.shape[0], dtype=jnp.int32)
    upto = order[None, :] <= order[:, None]
    doc_ends = jnp.sum(jnp.where(upto, lengths[None, :], 0), axis=1)
    positions = jnp.arange(tokens, dtype=jnp.int32)
    return jnp.sum((positions[:, None] >= doc_ends[None, :]).astype(jnp.int32), axis=1)


def shifted(values, offset, fill):
    filler = jnp.full((offset,) + values.shape[1:], fill, values.dtype)
    return jnp.concatenate([filler, values[:-offset]], axis=0)


def short_conv(values, kernel, segment):
    summed = values * kernel[0]
    for offset in range(1, kernel.shape[0]):
        same_doc = (shifted(segment, offset, -1) == segment).astype(values.dtype)
        summed = summed + shifted(values, offset, 0.0) * kernel[offset] * same_doc[:, None]
    return summed


def unit_inverse(lower_part):
    width = lower_part.shape[-1]
    index = jnp.arange(width, dtype=jnp.int32)
    inverse = None
    size = 1
    while size < width:
        rows, columns = index[:, None] // size, index[None, :] // size
        pairs = (rows % 2 == 1) & (columns == rows - 1)
        level = jnp.where(pairs[None], lower_part, 0.0)
        if inverse is None:
            inverse = jnp.eye(width, dtype=lower_part.dtype)[None] - level
        else:
            step = jnp.einsum("hij,hjk->hik", level, inverse, precision=MIX_PRECISION)
            inverse = inverse - jnp.einsum("hij,hjk->hik", inverse, step, precision=MIX_PRECISION)
        size = 2 * size
    return inverse


@jax.custom_vjp
def unit_solve(lower_part, sources):
    return jnp.einsum("hij,hjv->hiv", unit_inverse(lower_part), sources, precision=MIX_PRECISION)


def unit_solve_fwd(lower_part, sources):
    inverse = unit_inverse(lower_part)
    solved = jnp.einsum("hij,hjv->hiv", inverse, sources, precision=MIX_PRECISION)
    return solved, (inverse, solved)


def unit_solve_bwd(saved, d_solved):
    inverse, solved = saved
    d_sources = jnp.einsum("hji,hjv->hiv", inverse, d_solved, precision=MIX_PRECISION)
    d_lower = -jnp.einsum("hiv,hjv->hij", d_sources, solved, precision=MIX_PRECISION)
    return d_lower, d_sources


unit_solve.defvjp(unit_solve_fwd, unit_solve_bwd)


def delta_rule(query_rows, key_matrix, value_rows, decays, strength, segment):
    width = segment.shape[0]
    positions = jnp.arange(width, dtype=jnp.int32)
    same_doc = segment[:, None] == segment[None, :]
    lower_mask = same_doc & (positions[:, None] >= positions[None, :])
    strict_mask = same_doc & (positions[:, None] > positions[None, :])
    cumulative = jnp.einsum(
        "ij,hj->hi", lower_mask.astype(decays.dtype), decays, precision=TOP_PRECISION
    )
    spread = jnp.minimum(cumulative[:, :, None] - cumulative[:, None, :], 0.0)
    ratios = jnp.where(lower_mask[None], jnp.exp(spread), 0.0)
    key_inner = jnp.einsum("hid,hjd->hij", key_matrix, key_matrix, precision=MIX_PRECISION)
    lower_part = jnp.where(strict_mask[None], strength[:, :, None] * ratios * key_inner, 0.0)
    delta_rows = unit_solve(lower_part, strength[:, :, None] * value_rows)
    scores = jnp.einsum("hid,hjd->hij", query_rows, key_matrix, precision=MIX_PRECISION) * ratios
    return jnp.einsum("hij,hjv->hiv", scores, delta_rows, precision=MIX_PRECISION)


def conv_rows(proj, kernel, segment, head_count):
    rows = jax.nn.silu(short_conv(proj, kernel, segment))
    return jnp.swapaxes(rows.reshape(proj.shape[0], head_count, -1), 0, 1)


def unit_rows(proj, kernel, segment, head_count):
    rows = conv_rows(proj, kernel, segment, head_count)
    return rows * lax.rsqrt(jnp.sum(rows * rows, axis=2, keepdims=True) + EPSILON)


def query_rows_of(proj, kernel, segment, head_count):
    rows = unit_rows(proj, kernel, segment, head_count)
    return rows * rows.shape[2] ** (-0.5)


def head_gates(decay_proj, write_proj, decay_log, decay_bias):
    decays = -jnp.exp(decay_log) * jax.nn.softplus(decay_proj + decay_bias)
    return decays.T, jax.nn.sigmoid(write_proj).T


def gated_norm(readout_rows, gate_proj, out_gain):
    tokens = gate_proj.shape[0]
    rows = jnp.swapaxes(readout_rows, 0, 1)
    rows = rows * lax.rsqrt(jnp.mean(rows * rows, axis=2, keepdims=True) + EPSILON) * out_gain
    return (rows * jax.nn.silu(gate_proj.reshape(rows.shape))).reshape(tokens, -1)


def ring_index(place, size):
    half = (size + 1) // 2
    back = place // half
    return (1 - back) * (2 * place) + back * (2 * (size - 1 - place) + 1)


def ring_place(index, size):
    odd = index % 2
    return (1 - odd) * (index // 2) + odd * (size - 1 - index // 2)


def ring_neighbours(size):
    place = ring_place(lax.axis_index("fsdp"), size)
    return (
        place,
        ring_index((place + 1) % size, size),
        ring_index((place + size - 1) % size, size),
    )


def greet(partners):
    barrier = pltpu.get_barrier_semaphore()
    for partner in partners:
        pl.semaphore_signal(barrier, inc=1, device_id=partner, device_id_type=MESH)
    pl.semaphore_wait(barrier, len(partners))


def column_cuts(columns):
    cut = (columns // (2 * LANES)) * LANES
    return ((0, cut), (cut, columns - cut))


def plane_count():
    return 2 if lax.axis_size("rep") % 4 == 0 else 1


def rep_partners():
    rep = lax.axis_index("rep")
    core, plane = rep % 2, (rep // 2) % 2
    return rep, core, plane, rep + 1 - 2 * core, rep + 2 - 4 * plane


def plane_columns(columns, planes, plane):
    if planes == 1:
        cuts = column_cuts(columns)
        return (*cuts, cuts[0])
    third = ((columns // LANES + 1) // 3) * LANES
    own = pl.multiple_of(plane * third, LANES)
    other = pl.multiple_of((1 - plane) * third, LANES)
    return (own, third), (2 * third, columns - 2 * third), (other, third)


OWN, BOTH, OTHER = range(3)


def gather_kernel(size, planes, count, *refs):
    shards, wholes = refs[:count], refs[count : 2 * count]
    ring_out, ring_in, core_out, core_in, plane_out, plane_in, local_sem = refs[2 * count :]
    place, right, left = ring_neighbours(size)
    me = lax.axis_index("fsdp")
    rep, core, plane, sibling, across = rep_partners()
    partners = [(rep, right), (rep, left), (sibling, me)]
    greet(partners + ([(across, me)] if planes == 2 else []))

    def piece(ref, array, kind, base):
        rows, columns = shards[array].shape
        by_rows = (rows // 2) % SUBLANES == 0
        width = columns if by_rows else columns // 2
        first, part = plane_columns(width, planes, plane)[kind]
        if by_rows:
            base, height = base + core * (rows // 2), rows // 2
        else:
            first, height = pl.multiple_of(core * width + first, LANES), rows
        return ref.at[pl.ds(pl.multiple_of(base, SUBLANES), height), pl.ds(first, part)]

    def placed(array, kind, step):
        shift = step if kind == BOTH else (size - step)
        owner = ring_index((place + shift) % size, size)
        return piece(wholes[array], array, kind, owner * shards[array].shape[0])

    def ring_copy(array, way, step):
        block = placed(array, way, step)
        return pltpu.make_async_remote_copy(
            src_ref=block if step else piece(shards[array], array, way, 0),
            dst_ref=block,
            send_sem=ring_out.at[array, way, step],
            recv_sem=ring_in.at[array, way, step],
            device_id=(rep, right if way == OWN else left),
            device_id_type=MESH,
        )

    def core_copy(array, kind, step):
        block = placed(array, kind, step + 1)
        return pltpu.make_async_remote_copy(
            src_ref=block,
            dst_ref=block,
            send_sem=core_out.at[array, kind, step],
            recv_sem=core_in.at[array, kind, step],
            device_id=(sibling, me),
            device_id_type=MESH,
        )

    def plane_copy(array, step):
        block = placed(array, OWN, step + 1)
        return pltpu.make_async_remote_copy(
            src_ref=block,
            dst_ref=block,
            send_sem=plane_out.at[array, step],
            recv_sem=plane_in.at[array, step],
            device_id=(across, me),
            device_id_type=MESH,
        )

    def own_copy(array):
        rows = shards[array].shape[0]
        start = pl.multiple_of(me * rows, SUBLANES)
        return pltpu.make_async_copy(
            shards[array], wholes[array].at[pl.ds(start, rows)], local_sem.at[array]
        )

    def hand_over(step):
        for array in range(count):
            plane_copy(array, step).wait_recv()
            core_copy(array, OTHER, step).start()

    pairs = [(array, way) for array in range(count) for way in (OWN, BOTH)]
    for array, way in pairs:
        ring_copy(array, way, 0).start()
    for array in range(count):
        own_copy(array).start()
    for step in range(size - 1):
        for array, way in pairs:
            ring_copy(array, way, step).wait_recv()
            if step < size - 2:
                ring_copy(array, way, step + 1).start()
            if way == OWN and planes == 2:
                plane_copy(array, step).start()
            core_copy(array, way, step).start()
        if planes == 2 and step:
            hand_over(step - 1)
    if planes == 2:
        hand_over(size - 2)
    for array in range(count):
        own_copy(array).wait()
    for step in range(size - 1):
        for array, way in pairs:
            ring_copy(array, way, step).wait_send()
            core_copy(array, way, step).wait()
        if planes == 2:
            for array in range(count):
                plane_copy(array, step).wait_send()
                core_copy(array, OTHER, step).wait()


def gathered(weights, kernel_id):
    size, reps = lax.axis_size("fsdp"), lax.axis_size("rep")
    if size < 3 or reps % 2:
        return [lax.all_gather(weight, "fsdp", axis=0, tiled=True) for weight in weights]
    count, planes = len(weights), plane_count()
    anywhere = pl.BlockSpec(memory_space=pl.ANY)
    copies = [(count, 2), (count, 2), (count, 3), (count, 3), (count,), (count,)]
    semaphores = [pltpu.SemaphoreType.DMA((*shape, size - 1)) for shape in copies]
    return pl.pallas_call(
        functools.partial(gather_kernel, size, planes, count),
        out_shape=[
            jax.ShapeDtypeStruct((size * weight.shape[0], weight.shape[1]), weight.dtype)
            for weight in weights
        ],
        in_specs=[anywhere] * count,
        out_specs=[anywhere] * count,
        scratch_shapes=semaphores + [pltpu.SemaphoreType.DMA((count,))],
        compiler_params=pltpu.CompilerParams(collective_id=kernel_id, has_side_effects=True),
        name="gather_rows",
    )(*weights)


def swapped(array, axis_size, bit):
    return lax.ppermute(array, "rep", [(rank, rank ^ bit) for rank in range(axis_size)])


def paired(axis_size):
    return axis_size > 1 and axis_size & (axis_size - 1) == 0


def rounded(values):
    return lax.reduce_precision(values, 8, 7).astype(jnp.bfloat16)


def flipped(index, bit):
    return index + bit - 2 * bit * ((index // bit) % 2)


def bits_below(size):
    return [1 << power for power in range(size.bit_length() - 1)]


def scatter_kernel(size, reps, planes, wide, late, *refs):
    count = len(wide)
    parts, small, refs = refs[:count], refs[count], refs[count + 1 :]
    sums, small_total, refs = refs[:count], refs[count], refs[count + 1 :]
    slots, ends, refs = refs[: 2 * count], refs[2 * count : 3 * count], refs[3 * count :]
    subtotals, inbox, small_out, small_in = refs[:4]
    ring_out, ring_in, plane_out, plane_in, core_out, core_in = refs[4:]
    place, right, left = ring_neighbours(size)
    me = lax.axis_index("fsdp")
    rep, core, plane, sibling, across = rep_partners()
    exchanges = [(flipped(rep, bit), me) for bit in bits_below(reps)]
    exchanges += [(rep, flipped(me, bit)) for bit in bits_below(size)]
    greet([(rep, right), (rep, left), *exchanges])

    def small_copy(turn):
        return pltpu.make_async_remote_copy(
            src_ref=subtotals.at[turn - 1] if turn else small,
            dst_ref=inbox.at[turn],
            send_sem=small_out.at[turn],
            recv_sem=small_in.at[turn],
            device_id=exchanges[turn],
            device_id_type=MESH,
        )

    def small_take(turn):
        small_copy(turn).wait_recv()
        own = subtotals[turn - 1] if turn else small[...]
        if turn < len(exchanges) - 1:
            subtotals[turn] = own + inbox[turn]
            small_copy(turn + 1).start()
        else:
            small_total[...] = own + inbox[turn]

    def columns(array, way):
        first, width = column_cuts(parts[array].shape[2])[way]
        return pl.ds(first, width)

    def part(array, way, step):
        shift = (size - 1 - step) if way == 0 else (1 + step)
        owner = ring_index((place + shift) % size, size)
        return parts[array].at[owner, :, columns(array, way)]

    def slot(array, way, step):
        return slots[2 * array + way].at[step]

    def ring_copy(array, way, step):
        return pltpu.make_async_remote_copy(
            src_ref=slot(array, way, step - 1) if step else part(array, way, 0),
            dst_ref=slot(array, way, step),
            send_sem=ring_out.at[array, way, step],
            recv_sem=ring_in.at[array, way, step],
            device_id=(rep, right if way == 0 else left),
            device_id_type=MESH,
        )

    def result(array, second=False):
        if not wide[array]:
            return sums[array].at[core]
        return sums[array].at[2 * ((1 - plane) if second else plane) + core]

    def added_over_planes(array):
        return planes == 2 and not wide[array]

    def plane_copy(array):
        added = added_over_planes(array)
        return pltpu.make_async_remote_copy(
            src_ref=ends[array].at[0] if added else result(array),
            dst_ref=ends[array].at[1] if added else result(array),
            send_sem=plane_out.at[array],
            recv_sem=plane_in.at[array],
            device_id=(across, me),
            device_id_type=MESH,
        )

    def core_copy(array, second=False):
        block = result(array, second)
        return pltpu.make_async_remote_copy(
            src_ref=block,
            dst_ref=block,
            send_sem=core_out.at[array, int(second)],
            recv_sem=core_in.at[array, int(second)],
            device_id=(sibling, me),
            device_id_type=MESH,
        )

    def take(array, way, step):
        ring_copy(array, way, step).wait_recv()
        arrived, here = slot(array, way, step), part(array, way, step + 1)
        total = arrived[...].astype(jnp.float32) + here[...].astype(jnp.float32)
        total = total.astype(arrived.dtype)
        if step < size - 2:
            arrived[...] = total
            ring_copy(array, way, step + 1).start()
        elif added_over_planes(array):
            ends[array][0, :, columns(array, way)] = total
        else:
            index = 2 * plane + core if wide[array] else core
            sums[array][index, :, columns(array, way)] = total

    def hand_out(array):
        if planes == 2:
            plane_copy(array).start()
        if not added_over_planes(array):
            core_copy(array).start()

    def finish(array):
        if planes == 1:
            return
        plane_copy(array).wait_recv()
        if wide[array]:
            core_copy(array, True).start()
            return
        both = ends[array][0].astype(jnp.float32) + ends[array][1].astype(jnp.float32)
        sums[array][core] = both.astype(sums[array].dtype)
        core_copy(array).start()

    pairs = [(array, way) for array in range(count) for way in range(2)]
    for array, way in pairs:
        if late[array] == 0:
            ring_copy(array, way, 0).start()
    small_copy(0).start()
    for turn in range(max(size + max(late) + 1, 2 * len(exchanges))):
        for array in range(count):
            step = turn - late[array]
            for way in range(2):
                if step == -1:
                    ring_copy(array, way, 0).start()
                if 0 <= step < size - 1:
                    take(array, way, step)
            if step == size - 2:
                hand_out(array)
            if turn == size - 1 + max(late) + (late[array] > 0):
                finish(array)
        if turn % 2 == 1 and turn // 2 < len(exchanges):
            small_take(turn // 2)
    for turn in range(len(exchanges)):
        small_copy(turn).wait_send()
    for array in range(count):
        for way in range(2):
            for step in range(size - 1):
                ring_copy(array, way, step).wait_send()
        core_copy(array).wait()
        if planes == 2:
            plane_copy(array).wait_send()
            if wide[array]:
                core_copy(array, True).wait()


def scattered(parts, small, wide, late, kernel_id):
    size, reps, planes = lax.axis_size("fsdp"), lax.axis_size("rep"), plane_count()
    rounds = len(bits_below(size)) + len(bits_below(reps))
    count = len(parts)
    on_chip = pl.BlockSpec(memory_space=pltpu.VMEM)
    slots = [
        pltpu.VMEM((size - 1, part.shape[1], width), part.dtype)
        for part in parts
        for _, width in column_cuts(part.shape[2])
    ]
    ends = [
        pltpu.VMEM((2, SUBLANES, LANES) if spread else (2, *part.shape[1:]), part.dtype)
        for part, spread in zip(parts, wide)
    ]
    copies = [(count, 2, size - 1)] * 2 + [(count,)] * 2 + [(count, 2)] * 2
    return pl.pallas_call(
        functools.partial(scatter_kernel, size, reps, planes, wide, late),
        out_shape=[
            jax.ShapeDtypeStruct((4 if spread else 2, *part.shape[1:]), part.dtype)
            for part, spread in zip(parts, wide)
        ]
        + [jax.ShapeDtypeStruct(small.shape, small.dtype)],
        in_specs=[on_chip] * (count + 1),
        out_specs=[on_chip] * (count + 1),
        scratch_shapes=slots
        + ends
        + [pltpu.VMEM((rounds, *small.shape), small.dtype)] * 2
        + [pltpu.SemaphoreType.DMA((rounds,))] * 2
        + [pltpu.SemaphoreType.DMA(shape) for shape in copies],
        compiler_params=pltpu.CompilerParams(
            collective_id=kernel_id, has_side_effects=True, vmem_limit_bytes=VMEM_BYTES
        ),
        name="scatter_sums",
    )(*parts, small)


def ringed():
    size = lax.axis_size("fsdp")
    return size > 2 and paired(size) and paired(lax.axis_size("rep"))


def met(mine, theirs, bit):
    return jnp.concatenate([mine, swapped(theirs, lax.axis_size("rep"), bit)], axis=0)


def dealt(rows, bits):
    size = lax.axis_size("fsdp")
    for bit in bits:
        tokens, features = rows.shape
        split = rows.reshape(tokens, size, 2, features // (2 * size))
        first = split[:, :, 0].reshape(tokens, features // 2)
        second = split[:, :, 1].reshape(tokens, features // 2)
        even = (lax.axis_index("rep") // bit) % 2 == 0
        rows = met(jnp.where(even, first, second), jnp.where(even, second, first), bit)
    return rows


def met_all(rows, bits):
    for bit in bits:
        rows = met(rows, rows, bit)
    return rows


def owner_parts(lefts, rights, bits):
    size = lax.axis_size("fsdp")
    if not ringed():
        return [product_left(left, right).astype(jnp.bfloat16) for left, right in zip(lefts, rights)]
    dealt_lefts, parts = {}, []
    for left, right in zip(lefts, rights):
        if id(left) not in dealt_lefts:
            dealt_lefts[id(left)] = dealt(left, bits)
        part = product_left(dealt_lefts[id(left)], met_all(right, bits)).astype(jnp.bfloat16)
        parts.append(part.reshape(size, part.shape[0] // size, part.shape[1]))
    return parts


def all_sums(ffn_parts, mix_parts, flat, kernel_id):
    parts, reps = mix_parts + ffn_parts, lax.axis_size("rep")
    if not ringed():
        totals = [lax.psum_scatter(part, "fsdp", scatter_dimension=0, tiled=True) for part in parts]
        totals = [lax.psum(rows, "rep").astype(jnp.float32) for rows in totals]
        return totals, lax.psum(flat, ("rep", "fsdp"))
    wide = [False] * len(mix_parts) + [plane_count() == 2] * len(ffn_parts)
    late = [0] * len(mix_parts) + [LATE_STEPS] * len(ffn_parts)
    tile = 8 * LANES
    small = jnp.pad(flat, (0, -flat.size % tile)).reshape(-1, LANES)
    *summed, small = scattered(parts, small, wide, late, kernel_id)
    totals = []
    for own in summed:
        own = own.reshape(-1, own.shape[2])
        bit = 2 * plane_count()
        while bit < reps:
            own = rounded(own.astype(jnp.float32) + swapped(own, reps, bit).astype(jnp.float32))
            bit = 2 * bit
        totals.append(own.astype(jnp.float32))
    return totals, small.reshape(-1)[: flat.size]


def column_parts(array, widths):
    parts, start = [], 0
    for width in widths:
        parts.append(array[:, start : start + width])
        start = start + width
    return parts


def local(
    block_input,
    cotangent,
    doc_lengths,
    gain_mix,
    w_query,
    w_key,
    w_value,
    w_gate,
    w_decay,
    w_write,
    conv_query,
    conv_key,
    conv_value,
    decay_log,
    decay_bias,
    out_gain,
    w_out,
    gain_ffn,
    w_hidden,
    w_up,
    w_down,
):
    tokens = block_input.shape[0]
    segment = doc_segments(doc_lengths[0], tokens)
    head_count = decay_log.shape[0]
    narrow_widths = [w_query.shape[1], head_count, head_count]
    spare = -sum(narrow_widths) % LANES
    narrow = jnp.concatenate([w_query, w_decay, w_write], axis=1)
    narrow = jnp.pad(narrow, ((0, 0), (0, spare)))
    mixing = gathered([narrow, w_key, w_value, w_gate], 0)
    outward, hidden, up, downward = gathered([w_out, w_hidden, w_up, w_down], 1)
    upstream = cotangent.astype(jnp.bfloat16)

    normed, norm_back = jax.vjp(rms_norm, block_input, gain_mix)
    first_input = normed.astype(jnp.bfloat16)
    narrow_proj, key_proj, value_proj, gate_proj = [
        product(first_input, weight) for weight in mixing
    ]
    query_proj, decay_proj, write_proj = column_parts(narrow_proj, narrow_widths)

    def rows_of(maker):
        return lambda proj, kernel: maker(proj, kernel, segment, head_count)

    queries, query_back = jax.vjp(rows_of(query_rows_of), query_proj, conv_query)
    key_rows, key_back = jax.vjp(rows_of(unit_rows), key_proj, conv_key)
    value_rows, value_back = jax.vjp(rows_of(conv_rows), value_proj, conv_value)
    (decays, strength), gates_back = jax.vjp(
        head_gates, decay_proj, write_proj, decay_log, decay_bias
    )
    readout, readout_back = jax.vjp(
        lambda *operands: delta_rule(*operands, segment),
        queries,
        key_rows,
        value_rows,
        decays,
        strength,
    )
    mixed_out, mixed_back = jax.vjp(gated_norm, readout, gate_proj, out_gain)
    gated_out = mixed_out.astype(jnp.bfloat16)
    residual = block_input + product(gated_out, outward)
    normed_ffn, norm_ffn_back = jax.vjp(rms_norm, residual, gain_ffn)
    second = normed_ffn.astype(jnp.bfloat16)
    swiglu_out, swiglu_back = jax.vjp(swiglu, product(second, hidden), product(second, up))
    activation = swiglu_out.astype(jnp.bfloat16)
    block_out = residual + product(activation, downward)
    d_hidden, d_up = [
        grad.astype(jnp.bfloat16) for grad in swiglu_back(product_right(upstream, downward))
    ]
    d_second = product_right(d_hidden, hidden) + product_right(d_up, up)
    ffn_parts = owner_parts(
        [activation, second, second],
        [upstream, d_hidden, d_up],
        (2, 1) if plane_count() == 2 else (1,),
    )
    d_norm_ffn, grad_gain_ffn = norm_ffn_back(d_second)
    d_residual = cotangent + d_norm_ffn
    upstream_mix = d_residual.astype(jnp.bfloat16)
    d_mixed = product_right(upstream_mix, outward)
    d_readout, d_gate, grad_out_gain = mixed_back(d_mixed)
    d_queries, d_keys, d_values, d_decays, d_strength = readout_back(d_readout)
    d_value, grad_conv_value = value_back(d_values)
    d_query, grad_conv_query = query_back(d_queries)
    d_key, grad_conv_key = key_back(d_keys)
    d_decay, d_write, grad_decay_log, grad_decay_bias = gates_back((d_decays, d_strength))
    d_narrow = jnp.concatenate([d_query, d_decay, d_write], axis=1).astype(jnp.bfloat16)
    d_narrow = jnp.pad(d_narrow, ((0, 0), (0, spare)))
    d_mix = [d_narrow, *(rows.astype(jnp.bfloat16) for rows in (d_key, d_value, d_gate))]
    mix_parts = owner_parts([gated_out] + [first_input] * 4, [upstream_mix] + d_mix, (1,))
    d_first = sum(product_right(rows, weight) for rows, weight in zip(d_mix, mixing))
    d_norm, grad_gain_mix = norm_back(d_first)
    input_grad = d_residual + d_norm
    small = (
        grad_gain_mix,
        grad_conv_query,
        grad_conv_key,
        grad_conv_value,
        grad_decay_log,
        grad_decay_bias,
        grad_out_gain,
        grad_gain_ffn,
    )
    flat = jnp.concatenate([grad.reshape(-1) for grad in small])
    sums, flat = all_sums(ffn_parts, mix_parts, flat, 2)
    grad_out, grad_narrow, grad_key, grad_value, grad_gate = sums[:5]
    grad_down, grad_hidden, grad_up = sums[5:]
    grad_query, grad_decay, grad_write = column_parts(grad_narrow, narrow_widths)
    small_totals, start = [], 0
    for grad in small:
        small_totals.append(flat[start : start + grad.size].reshape(grad.shape))
        start = start + grad.size
    return (
        block_out,
        input_grad,
        small_totals[0],
        grad_query,
        grad_key,
        grad_value,
        grad_gate,
        grad_decay,
        grad_write,
        *small_totals[1:7],
        grad_out,
        small_totals[7],
        grad_hidden,
        grad_up,
        grad_down,
    )


def solution(mesh):
    placed = (
        P(("rep", "fsdp"), None),
        P(("rep", "fsdp"), None),
        P(("rep", "fsdp"), None),
        P(),
        P("fsdp", None),
        P("fsdp", None),
        P("fsdp", None),
        P("fsdp", None),
        P("fsdp", None),
        P("fsdp", None),
        P(),
        P(),
        P(),
        P(),
        P(),
        P(),
        P("fsdp", None),
        P(),
        P("fsdp", None),
        P("fsdp", None),
        P("fsdp", None),
    )
    return jax.shard_map(
        local,
        mesh=mesh,
        in_specs=placed,
        out_specs=(
            P(("rep", "fsdp"), None),
            P(("rep", "fsdp"), None),
            P(),
            P("fsdp", None),
            P("fsdp", None),
            P("fsdp", None),
            P("fsdp", None),
            P("fsdp", None),
            P("fsdp", None),
            P(),
            P(),
            P(),
            P(),
            P(),
            P(),
            P("fsdp", None),
            P(),
            P("fsdp", None),
            P("fsdp", None),
            P("fsdp", None),
        ),
        check_vma=False,
    )
```

```python
import functools

import jax
import jax.numpy as jnp
from jax import lax
from jax.experimental import pallas as pl
from jax.experimental.pallas import tpu as pltpu
from jax.sharding import PartitionSpec as P

EPSILON = 1e-06
TOP_PRECISION = lax.Precision.HIGHEST
MIX_PRECISION = lax.Precision.HIGH
LANES = 128
SUBLANES = 16
LATE_STEPS = 3
VMEM_BYTES = 48 * 1024 * 1024
MESH = pl.DeviceIdType.MESH


def product(left, right):
    return jnp.dot(left, right, preferred_element_type=jnp.float32)


def product_left(left, right):
    return lax.dot_general(
        left, right, (((0,), (0,)), ((), ())), preferred_element_type=jnp.float32
    )


def product_right(left, right):
    return lax.dot_general(
        left, right, (((1,), (1,)), ((), ())), preferred_element_type=jnp.float32
    )


def rms_norm(values, gain):
    return values * lax.rsqrt(jnp.mean(values * values, axis=-1, keepdims=True) + EPSILON) * gain


def swiglu(hidden_pre, up_pre):
    return jax.nn.silu(hidden_pre) * up_pre


def doc_segments(lengths, tokens):
    order = jnp.arange(lengths.shape[0], dtype=jnp.int32)
    upto = order[None, :] <= order[:, None]
    doc_ends = jnp.sum(jnp.where(upto, lengths[None, :], 0), axis=1)
    positions = jnp.arange(tokens, dtype=jnp.int32)
    return jnp.sum((positions[:, None] >= doc_ends[None, :]).astype(jnp.int32), axis=1)


def shifted(values, offset, fill):
    filler = jnp.full((offset,) + values.shape[1:], fill, values.dtype)
    return jnp.concatenate([filler, values[:-offset]], axis=0)


def short_conv(values, kernel, segment):
    summed = values * kernel[0]
    for offset in range(1, kernel.shape[0]):
        same_doc = (shifted(segment, offset, -1) == segment).astype(values.dtype)
        summed = summed + shifted(values, offset, 0.0) * kernel[offset] * same_doc[:, None]
    return summed


def unit_inverse(lower_part):
    width = lower_part.shape[-1]
    index = jnp.arange(width, dtype=jnp.int32)
    inverse = None
    size = 1
    while size < width:
        rows, columns = index[:, None] // size, index[None, :] // size
        pairs = (rows % 2 == 1) & (columns == rows - 1)
        level = jnp.where(pairs[None], lower_part, 0.0)
        if inverse is None:
            inverse = jnp.eye(width, dtype=lower_part.dtype)[None] - level
        else:
            step = jnp.einsum("hij,hjk->hik", level, inverse, precision=MIX_PRECISION)
            inverse = inverse - jnp.einsum("hij,hjk->hik", inverse, step, precision=MIX_PRECISION)
        size = 2 * size
    return inverse


@jax.custom_vjp
def unit_solve(lower_part, sources):
    return jnp.einsum("hij,hjv->hiv", unit_inverse(lower_part), sources, precision=MIX_PRECISION)


def unit_solve_fwd(lower_part, sources):
    inverse = unit_inverse(lower_part)
    solved = jnp.einsum("hij,hjv->hiv", inverse, sources, precision=MIX_PRECISION)
    return solved, (inverse, solved)


def unit_solve_bwd(saved, d_solved):
    inverse, solved = saved
    d_sources = jnp.einsum("hji,hjv->hiv", inverse, d_solved, precision=MIX_PRECISION)
    d_lower = -jnp.einsum("hiv,hjv->hij", d_sources, solved, precision=MIX_PRECISION)
    return d_lower, d_sources


unit_solve.defvjp(unit_solve_fwd, unit_solve_bwd)


def delta_rule(query_rows, key_matrix, value_rows, decays, strength, segment):
    width = segment.shape[0]
    positions = jnp.arange(width, dtype=jnp.int32)
    same_doc = segment[:, None] == segment[None, :]
    lower_mask = same_doc & (positions[:, None] >= positions[None, :])
    strict_mask = same_doc & (positions[:, None] > positions[None, :])
    cumulative = jnp.einsum(
        "ij,hj->hi", lower_mask.astype(decays.dtype), decays, precision=TOP_PRECISION
    )
    spread = jnp.minimum(cumulative[:, :, None] - cumulative[:, None, :], 0.0)
    ratios = jnp.where(lower_mask[None], jnp.exp(spread), 0.0)
    key_inner = jnp.einsum("hid,hjd->hij", key_matrix, key_matrix, precision=MIX_PRECISION)
    lower_part = jnp.where(strict_mask[None], strength[:, :, None] * ratios * key_inner, 0.0)
    delta_rows = unit_solve(lower_part, strength[:, :, None] * value_rows)
    scores = jnp.einsum("hid,hjd->hij", query_rows, key_matrix, precision=MIX_PRECISION) * ratios
    return jnp.einsum("hij,hjv->hiv", scores, delta_rows, precision=MIX_PRECISION)


def conv_rows(proj, kernel, segment, head_count):
    rows = jax.nn.silu(short_conv(proj, kernel, segment))
    return jnp.swapaxes(rows.reshape(proj.shape[0], head_count, -1), 0, 1)


def unit_rows(proj, kernel, segment, head_count):
    rows = conv_rows(proj, kernel, segment, head_count)
    return rows * lax.rsqrt(jnp.sum(rows * rows, axis=2, keepdims=True) + EPSILON)


def query_rows_of(proj, kernel, segment, head_count):
    rows = unit_rows(proj, kernel, segment, head_count)
    return rows * rows.shape[2] ** (-0.5)


def head_gates(decay_proj, write_proj, decay_log, decay_bias):
    decays = -jnp.exp(decay_log) * jax.nn.softplus(decay_proj + decay_bias)
    return decays.T, jax.nn.sigmoid(write_proj).T


def gated_norm(readout_rows, gate_proj, out_gain):
    tokens = gate_proj.shape[0]
    rows = jnp.swapaxes(readout_rows, 0, 1)
    rows = rows * lax.rsqrt(jnp.mean(rows * rows, axis=2, keepdims=True) + EPSILON) * out_gain
    return (rows * jax.nn.silu(gate_proj.reshape(rows.shape))).reshape(tokens, -1)


def ring_index(place, size):
    half = (size + 1) // 2
    back = place // half
    return (1 - back) * (2 * place) + back * (2 * (size - 1 - place) + 1)


def ring_place(index, size):
    odd = index % 2
    return (1 - odd) * (index // 2) + odd * (size - 1 - index // 2)


def ring_neighbours(size):
    place = ring_place(lax.axis_index("fsdp"), size)
    return (
        place,
        ring_index((place + 1) % size, size),
        ring_index((place + size - 1) % size, size),
    )


def greet(partners):
    barrier = pltpu.get_barrier_semaphore()
    for partner in partners:
        pl.semaphore_signal(barrier, inc=1, device_id=partner, device_id_type=MESH)
    pl.semaphore_wait(barrier, len(partners))


def column_cuts(columns):
    cut = (columns // (2 * LANES)) * LANES
    return ((0, cut), (cut, columns - cut))


def plane_count():
    return 2 if lax.axis_size("rep") % 4 == 0 else 1


def rep_partners():
    rep = lax.axis_index("rep")
    core, plane = rep % 2, (rep // 2) % 2
    return rep, core, plane, rep + 1 - 2 * core, rep + 2 - 4 * plane


def plane_columns(columns, planes, plane):
    if planes == 1:
        cuts = column_cuts(columns)
        return (*cuts, cuts[0])
    third = (columns // LANES // 3) * LANES
    own = pl.multiple_of(plane * third, LANES)
    other = pl.multiple_of((1 - plane) * third, LANES)
    return (own, third), (2 * third, columns - 2 * third), (other, third)


OWN, BOTH, OTHER = range(3)


def gather_kernel(size, planes, count, *refs):
    shards, wholes = refs[:count], refs[count : 2 * count]
    ring_out, ring_in, core_out, core_in, plane_out, plane_in, local_sem = refs[2 * count :]
    place, right, left = ring_neighbours(size)
    me = lax.axis_index("fsdp")
    rep, core, plane, sibling, across = rep_partners()
    partners = [(rep, right), (rep, left), (sibling, me)]
    greet(partners + ([(across, me)] if planes == 2 else []))

    def piece(ref, array, kind, base):
        rows, columns = shards[array].shape
        by_rows = (rows // 2) % SUBLANES == 0
        width = columns if by_rows else columns // 2
        first, part = plane_columns(width, planes, plane)[kind]
        if by_rows:
            base, height = base + core * (rows // 2), rows // 2
        else:
            first, height = pl.multiple_of(core * width + first, LANES), rows
        return ref.at[pl.ds(pl.multiple_of(base, SUBLANES), height), pl.ds(first, part)]

    def rightward(array, kind):
        return (kind == BOTH) == (array % 2 == 1)

    def placed(array, kind, step):
        shift = (size - step) if rightward(array, kind) else step
        owner = ring_index((place + shift) % size, size)
        return piece(wholes[array], array, kind, owner * shards[array].shape[0])

    def ring_copy(array, way, step):
        block = placed(array, way, step)
        return pltpu.make_async_remote_copy(
            src_ref=block if step else piece(shards[array], array, way, 0),
            dst_ref=block,
            send_sem=ring_out.at[array, way, step],
            recv_sem=ring_in.at[array, way, step],
            device_id=(rep, right if rightward(array, way) else left),
            device_id_type=MESH,
        )

    def core_copy(array, kind, step):
        block = placed(array, kind, step + 1)
        return pltpu.make_async_remote_copy(
            src_ref=block,
            dst_ref=block,
            send_sem=core_out.at[array, kind, step],
            recv_sem=core_in.at[array, kind, step],
            device_id=(sibling, me),
            device_id_type=MESH,
        )

    def plane_copy(array, step):
        block = placed(array, OWN, step + 1)
        return pltpu.make_async_remote_copy(
            src_ref=block,
            dst_ref=block,
            send_sem=plane_out.at[array, step],
            recv_sem=plane_in.at[array, step],
            device_id=(across, me),
            device_id_type=MESH,
        )

    def own_copy(array):
        rows = shards[array].shape[0]
        start = pl.multiple_of(me * rows, SUBLANES)
        return pltpu.make_async_copy(
            shards[array], wholes[array].at[pl.ds(start, rows)], local_sem.at[array]
        )

    def hand_over(step):
        for array in range(count):
            plane_copy(array, step).wait_recv()
            core_copy(array, OTHER, step).start()

    pairs = [(array, way) for array in range(count) for way in (OWN, BOTH)]
    for array, way in pairs:
        ring_copy(array, way, 0).start()
    for array in range(count):
        own_copy(array).start()
    for step in range(size - 1):
        for array, way in pairs:
            ring_copy(array, way, step).wait_recv()
            if step < size - 2:
                ring_copy(array, way, step + 1).start()
            if way == OWN and planes == 2:
                plane_copy(array, step).start()
            core_copy(array, way, step).start()
        if planes == 2 and step:
            hand_over(step - 1)
    if planes == 2:
        hand_over(size - 2)
    for array in range(count):
        own_copy(array).wait()
    for step in range(size - 1):
        for array, way in pairs:
            ring_copy(array, way, step).wait_send()
            core_copy(array, way, step).wait()
        if planes == 2:
            for array in range(count):
                plane_copy(array, step).wait_send()
                core_copy(array, OTHER, step).wait()


def gathered(weights, kernel_id):
    size, reps = lax.axis_size("fsdp"), lax.axis_size("rep")
    if size < 3 or reps % 2:
        return [lax.all_gather(weight, "fsdp", axis=0, tiled=True) for weight in weights]
    count, planes = len(weights), plane_count()
    anywhere = pl.BlockSpec(memory_space=pl.ANY)
    copies = [(count, 2), (count, 2), (count, 3), (count, 3), (count,), (count,)]
    semaphores = [pltpu.SemaphoreType.DMA((*shape, size - 1)) for shape in copies]
    return pl.pallas_call(
        functools.partial(gather_kernel, size, planes, count),
        out_shape=[
            jax.ShapeDtypeStruct((size * weight.shape[0], weight.shape[1]), weight.dtype)
            for weight in weights
        ],
        in_specs=[anywhere] * count,
        out_specs=[anywhere] * count,
        scratch_shapes=semaphores + [pltpu.SemaphoreType.DMA((count,))],
        compiler_params=pltpu.CompilerParams(collective_id=kernel_id, has_side_effects=True),
        name="gather_rows",
    )(*weights)


def swapped(array, axis_size, bit):
    return lax.ppermute(array, "rep", [(rank, rank ^ bit) for rank in range(axis_size)])


def paired(axis_size):
    return axis_size > 1 and axis_size & (axis_size - 1) == 0


def rounded(values):
    return lax.reduce_precision(values, 8, 7).astype(jnp.bfloat16)


def flipped(index, bit):
    return index + bit - 2 * bit * ((index // bit) % 2)


def bits_below(size):
    return [1 << power for power in range(size.bit_length() - 1)]


def scatter_kernel(size, reps, planes, wide, late, *refs):
    count = len(wide)
    parts, small, refs = refs[:count], refs[count], refs[count + 1 :]
    sums, small_total, refs = refs[:count], refs[count], refs[count + 1 :]
    slots, ends, refs = refs[: 2 * count], refs[2 * count : 3 * count], refs[3 * count :]
    subtotals, inbox, small_out, small_in = refs[:4]
    ring_out, ring_in, plane_out, plane_in, core_out, core_in = refs[4:]
    place, right, left = ring_neighbours(size)
    me = lax.axis_index("fsdp")
    rep, core, plane, sibling, across = rep_partners()
    exchanges = [(flipped(rep, bit), me) for bit in bits_below(reps)]
    exchanges += [(rep, flipped(me, bit)) for bit in bits_below(size)]
    greet([(rep, right), (rep, left), *exchanges])

    def small_copy(turn):
        return pltpu.make_async_remote_copy(
            src_ref=subtotals.at[turn - 1] if turn else small,
            dst_ref=inbox.at[turn],
            send_sem=small_out.at[turn],
            recv_sem=small_in.at[turn],
            device_id=exchanges[turn],
            device_id_type=MESH,
        )

    def small_take(turn):
        small_copy(turn).wait_recv()
        own = subtotals[turn - 1] if turn else small[...]
        if turn < len(exchanges) - 1:
            subtotals[turn] = own + inbox[turn]
            small_copy(turn + 1).start()
        else:
            small_total[...] = own + inbox[turn]

    def columns(array, way):
        first, width = column_cuts(parts[array].shape[2])[way]
        return pl.ds(first, width)

    def part(array, way, step):
        shift = (size - 1 - step) if way == 0 else (1 + step)
        owner = ring_index((place + shift) % size, size)
        return parts[array].at[owner, :, columns(array, way)]

    def slot(array, way, step):
        return slots[2 * array + way].at[step]

    def ring_copy(array, way, step):
        return pltpu.make_async_remote_copy(
            src_ref=slot(array, way, step - 1) if step else part(array, way, 0),
            dst_ref=slot(array, way, step),
            send_sem=ring_out.at[array, way, step],
            recv_sem=ring_in.at[array, way, step],
            device_id=(rep, right if way == 0 else left),
            device_id_type=MESH,
        )

    def result(array, second=False):
        if not wide[array]:
            return sums[array].at[core]
        return sums[array].at[2 * ((1 - plane) if second else plane) + core]

    def added_over_planes(array):
        return planes == 2 and not wide[array]

    def plane_copy(array):
        added = added_over_planes(array)
        return pltpu.make_async_remote_copy(
            src_ref=ends[array].at[0] if added else result(array),
            dst_ref=ends[array].at[1] if added else result(array),
            send_sem=plane_out.at[array],
            recv_sem=plane_in.at[array],
            device_id=(across, me),
            device_id_type=MESH,
        )

    def core_copy(array, second=False):
        block = result(array, second)
        return pltpu.make_async_remote_copy(
            src_ref=block,
            dst_ref=block,
            send_sem=core_out.at[array, int(second)],
            recv_sem=core_in.at[array, int(second)],
            device_id=(sibling, me),
            device_id_type=MESH,
        )

    def take(array, way, step):
        ring_copy(array, way, step).wait_recv()
        arrived, here = slot(array, way, step), part(array, way, step + 1)
        total = arrived[...].astype(jnp.float32) + here[...].astype(jnp.float32)
        total = total.astype(arrived.dtype)
        if step < size - 2:
            arrived[...] = total
            ring_copy(array, way, step + 1).start()
        elif added_over_planes(array):
            ends[array][0, :, columns(array, way)] = total
        else:
            index = 2 * plane + core if wide[array] else core
            sums[array][index, :, columns(array, way)] = total

    def hand_out(array):
        if planes == 2:
            plane_copy(array).start()
        if not added_over_planes(array):
            core_copy(array).start()

    def finish(array):
        if planes == 1:
            return
        plane_copy(array).wait_recv()
        if wide[array]:
            core_copy(array, True).start()
            return
        both = ends[array][0].astype(jnp.float32) + ends[array][1].astype(jnp.float32)
        sums[array][core] = both.astype(sums[array].dtype)
        core_copy(array).start()

    pairs = [(array, way) for array in range(count) for way in range(2)]
    for array, way in pairs:
        if late[array] == 0:
            ring_copy(array, way, 0).start()
    small_copy(0).start()
    for turn in range(max(size + max(late) + 1, len(exchanges))):
        for array in range(count):
            step = turn - late[array]
            for way in range(2):
                if step == -1:
                    ring_copy(array, way, 0).start()
                if 0 <= step < size - 1:
                    take(array, way, step)
            if step == size - 2:
                hand_out(array)
            if turn == size - 1 + max(late) + (late[array] > 0):
                finish(array)
        if turn < len(exchanges):
            small_take(turn)
    for turn in range(len(exchanges)):
        small_copy(turn).wait_send()
    for array in range(count):
        for way in range(2):
            for step in range(size - 1):
                ring_copy(array, way, step).wait_send()
        core_copy(array).wait()
        if planes == 2:
            plane_copy(array).wait_send()
            if wide[array]:
                core_copy(array, True).wait()


def scattered(parts, small, wide, late, kernel_id):
    size, reps, planes = lax.axis_size("fsdp"), lax.axis_size("rep"), plane_count()
    rounds = len(bits_below(size)) + len(bits_below(reps))
    count = len(parts)
    on_chip = pl.BlockSpec(memory_space=pltpu.VMEM)
    slots = [
        pltpu.VMEM((size - 1, part.shape[1], width), part.dtype)
        for part in parts
        for _, width in column_cuts(part.shape[2])
    ]
    ends = [
        pltpu.VMEM((2, SUBLANES, LANES) if spread else (2, *part.shape[1:]), part.dtype)
        for part, spread in zip(parts, wide)
    ]
    copies = [(count, 2, size - 1)] * 2 + [(count,)] * 2 + [(count, 2)] * 2
    return pl.pallas_call(
        functools.partial(scatter_kernel, size, reps, planes, wide, late),
        out_shape=[
            jax.ShapeDtypeStruct((4 if spread else 2, *part.shape[1:]), part.dtype)
            for part, spread in zip(parts, wide)
        ]
        + [jax.ShapeDtypeStruct(small.shape, small.dtype)],
        in_specs=[on_chip] * (count + 1),
        out_specs=[on_chip] * (count + 1),
        scratch_shapes=slots
        + ends
        + [pltpu.VMEM((rounds, *small.shape), small.dtype)] * 2
        + [pltpu.SemaphoreType.DMA((rounds,))] * 2
        + [pltpu.SemaphoreType.DMA(shape) for shape in copies],
        compiler_params=pltpu.CompilerParams(
            collective_id=kernel_id, has_side_effects=True, vmem_limit_bytes=VMEM_BYTES
        ),
        name="scatter_sums",
    )(*parts, small)


def ringed():
    size = lax.axis_size("fsdp")
    return size > 2 and paired(size) and paired(lax.axis_size("rep"))


def met(mine, theirs, bit):
    return jnp.concatenate([mine, swapped(theirs, lax.axis_size("rep"), bit)], axis=0)


def dealt(rows, bits):
    size = lax.axis_size("fsdp")
    for bit in bits:
        tokens, features = rows.shape
        split = rows.reshape(tokens, size, 2, features // (2 * size))
        first = split[:, :, 0].reshape(tokens, features // 2)
        second = split[:, :, 1].reshape(tokens, features // 2)
        even = (lax.axis_index("rep") // bit) % 2 == 0
        rows = met(jnp.where(even, first, second), jnp.where(even, second, first), bit)
    return rows


def met_all(rows, bits):
    for bit in bits:
        rows = met(rows, rows, bit)
    return rows


def owner_parts(lefts, rights, bits):
    size = lax.axis_size("fsdp")
    if not ringed():
        return [product_left(left, right).astype(jnp.bfloat16) for left, right in zip(lefts, rights)]
    dealt_lefts, parts = {}, []
    for left, right in zip(lefts, rights):
        if id(left) not in dealt_lefts:
            dealt_lefts[id(left)] = dealt(left, bits)
        part = product_left(dealt_lefts[id(left)], met_all(right, bits)).astype(jnp.bfloat16)
        parts.append(part.reshape(size, part.shape[0] // size, part.shape[1]))
    return parts


def all_sums(ffn_parts, mix_parts, flat, kernel_id):
    parts, reps = mix_parts + ffn_parts, lax.axis_size("rep")
    if not ringed():
        totals = [lax.psum_scatter(part, "fsdp", scatter_dimension=0, tiled=True) for part in parts]
        totals = [lax.psum(rows, "rep").astype(jnp.float32) for rows in totals]
        return totals, lax.psum(flat, ("rep", "fsdp"))
    wide = [False] * len(mix_parts) + [plane_count() == 2] * len(ffn_parts)
    late = [0] * len(mix_parts) + [LATE_STEPS] * len(ffn_parts)
    tile = 8 * LANES
    small = jnp.pad(flat, (0, -flat.size % tile)).reshape(-1, LANES)
    *summed, small = scattered(parts, small, wide, late, kernel_id)
    totals = []
    for own in summed:
        own = own.reshape(-1, own.shape[2])
        bit = 2 * plane_count()
        while bit < reps:
            own = rounded(own.astype(jnp.float32) + swapped(own, reps, bit).astype(jnp.float32))
            bit = 2 * bit
        totals.append(own.astype(jnp.float32))
    return totals, small.reshape(-1)[: flat.size]


def column_parts(array, widths):
    parts, start = [], 0
    for width in widths:
        parts.append(array[:, start : start + width])
        start = start + width
    return parts


def local(
    block_input,
    cotangent,
    doc_lengths,
    gain_mix,
    w_query,
    w_key,
    w_value,
    w_gate,
    w_decay,
    w_write,
    conv_query,
    conv_key,
    conv_value,
    decay_log,
    decay_bias,
    out_gain,
    w_out,
    gain_ffn,
    w_hidden,
    w_up,
    w_down,
):
    tokens = block_input.shape[0]
    segment = doc_segments(doc_lengths[0], tokens)
    head_count = decay_log.shape[0]
    narrow_widths = [w_query.shape[1], head_count, head_count]
    spare = -sum(narrow_widths) % LANES
    narrow = jnp.concatenate([w_query, w_decay, w_write], axis=1)
    narrow = jnp.pad(narrow, ((0, 0), (0, spare)))
    mixing = gathered([narrow, w_key, w_value, w_gate], 0)
    outward, hidden, up, downward = gathered([w_out, w_hidden, w_up, w_down], 1)
    upstream = cotangent.astype(jnp.bfloat16)

    normed, norm_back = jax.vjp(rms_norm, block_input, gain_mix)
    first_input = normed.astype(jnp.bfloat16)
    narrow_proj, key_proj, value_proj, gate_proj = [
        product(first_input, weight) for weight in mixing
    ]
    query_proj, decay_proj, write_proj = column_parts(narrow_proj, narrow_widths)

    def rows_of(maker):
        return lambda proj, kernel: maker(proj, kernel, segment, head_count)

    queries, query_back = jax.vjp(rows_of(query_rows_of), query_proj, conv_query)
    key_rows, key_back = jax.vjp(rows_of(unit_rows), key_proj, conv_key)
    value_rows, value_back = jax.vjp(rows_of(conv_rows), value_proj, conv_value)
    (decays, strength), gates_back = jax.vjp(
        head_gates, decay_proj, write_proj, decay_log, decay_bias
    )
    readout, readout_back = jax.vjp(
        lambda *operands: delta_rule(*operands, segment),
        queries,
        key_rows,
        value_rows,
        decays,
        strength,
    )
    mixed_out, mixed_back = jax.vjp(gated_norm, readout, gate_proj, out_gain)
    gated_out = mixed_out.astype(jnp.bfloat16)
    residual = block_input + product(gated_out, outward)
    normed_ffn, norm_ffn_back = jax.vjp(rms_norm, residual, gain_ffn)
    second = normed_ffn.astype(jnp.bfloat16)
    swiglu_out, swiglu_back = jax.vjp(swiglu, product(second, hidden), product(second, up))
    activation = swiglu_out.astype(jnp.bfloat16)
    block_out = residual + product(activation, downward)
    d_hidden, d_up = [
        grad.astype(jnp.bfloat16) for grad in swiglu_back(product_right(upstream, downward))
    ]
    d_second = product_right(d_hidden, hidden) + product_right(d_up, up)
    ffn_parts = owner_parts(
        [activation, second, second],
        [upstream, d_hidden, d_up],
        (2, 1) if plane_count() == 2 else (1,),
    )
    d_norm_ffn, grad_gain_ffn = norm_ffn_back(d_second)
    d_residual = cotangent + d_norm_ffn
    upstream_mix = d_residual.astype(jnp.bfloat16)
    d_mixed = product_right(upstream_mix, outward)
    d_readout, d_gate, grad_out_gain = mixed_back(d_mixed)
    d_queries, d_keys, d_values, d_decays, d_strength = readout_back(d_readout)
    d_value, grad_conv_value = value_back(d_values)
    d_query, grad_conv_query = query_back(d_queries)
    d_key, grad_conv_key = key_back(d_keys)
    d_decay, d_write, grad_decay_log, grad_decay_bias = gates_back((d_decays, d_strength))
    d_narrow = jnp.concatenate([d_query, d_decay, d_write], axis=1).astype(jnp.bfloat16)
    d_narrow = jnp.pad(d_narrow, ((0, 0), (0, spare)))
    d_mix = [d_narrow, *(rows.astype(jnp.bfloat16) for rows in (d_key, d_value, d_gate))]
    mix_parts = owner_parts([gated_out] + [first_input] * 4, [upstream_mix] + d_mix, (1,))
    d_first = sum(product_right(rows, weight) for rows, weight in zip(d_mix, mixing))
    d_norm, grad_gain_mix = norm_back(d_first)
    input_grad = d_residual + d_norm
    small = (
        grad_gain_mix,
        grad_conv_query,
        grad_conv_key,
        grad_conv_value,
        grad_decay_log,
        grad_decay_bias,
        grad_out_gain,
        grad_gain_ffn,
    )
    flat = jnp.concatenate([grad.reshape(-1) for grad in small])
    sums, flat = all_sums(ffn_parts, mix_parts, flat, 2)
    grad_out, grad_narrow, grad_key, grad_value, grad_gate = sums[:5]
    grad_down, grad_hidden, grad_up = sums[5:]
    grad_query, grad_decay, grad_write = column_parts(grad_narrow, narrow_widths)
    small_totals, start = [], 0
    for grad in small:
        small_totals.append(flat[start : start + grad.size].reshape(grad.shape))
        start = start + grad.size
    return (
        block_out,
        input_grad,
        small_totals[0],
        grad_query,
        grad_key,
        grad_value,
        grad_gate,
        grad_decay,
        grad_write,
        *small_totals[1:7],
        grad_out,
        small_totals[7],
        grad_hidden,
        grad_up,
        grad_down,
    )


def solution(mesh):
    placed = (
        P(("rep", "fsdp"), None),
        P(("rep", "fsdp"), None),
        P(("rep", "fsdp"), None),
        P(),
        P("fsdp", None),
        P("fsdp", None),
        P("fsdp", None),
        P("fsdp", None),
        P("fsdp", None),
        P("fsdp", None),
        P(),
        P(),
        P(),
        P(),
        P(),
        P(),
        P("fsdp", None),
        P(),
        P("fsdp", None),
        P("fsdp", None),
        P("fsdp", None),
    )
    return jax.shard_map(
        local,
        mesh=mesh,
        in_specs=placed,
        out_specs=(
            P(("rep", "fsdp"), None),
            P(("rep", "fsdp"), None),
            P(),
            P("fsdp", None),
            P("fsdp", None),
            P("fsdp", None),
            P("fsdp", None),
            P("fsdp", None),
            P("fsdp", None),
            P(),
            P(),
            P(),
            P(),
            P(),
            P(),
            P("fsdp", None),
            P(),
            P("fsdp", None),
            P("fsdp", None),
            P("fsdp", None),
        ),
        check_vma=False,
    )
```
